256 devices in a mesh: case: 4 (over y_hi, core), mod: 64 (over x, y_lo, z).
Axes of the slice: x: 4, y: 4 (y_hi: 2, y_lo: 2; y = y_hi * 2 + y_lo), z: 8, core: 2. Of those that a mesh axis runs over, the one named last changes fastest.
Arguments:
- turbulence: float32 [4, 256, 256], P('case'), may hold values from -6 to 6
- pupil_amp: float32 [256, 256], replicated, may hold values from 0.3 to 1
- mod_points: int32 [64], P('mod'), may hold values from 0 to 255
- valid_pix: int32 [65536], P('mod'), may hold values from 0 to 262143, as said below
- recon: bfloat16 [5120, 65536], P('case', 'mod'), may hold values from -0.0234375 to 0.0234375
- gx: float32 [256, 64], replicated, may hold values from -1.2 to 1.2
- gy: float32 [256, 80], replicated, may hold values from -1.2 to 1.2
- act_map: int32 [5120], replicated, may hold values from 0 to 5119, each once
Outputs:
- command_total: float32 [4, 5120], P('case')
- frame: float32 [4, 512, 512], P('case', 'mod')
The draws below stay inside these ranges and needn't reach their ends.
Inputs may be any that keep to these rules, and one draw needn't show every extreme that they name: `valid_pix`: entries k * 1024 to (k + 1) * 1024 - 1 are flat indices (row times 512 plus column) of pixels in detector rows k * 8 to (k + 1) * 8 - 1.
All inputs are finite; a program needn't handle non-finite values.
Results may differ from the reference program's by a relative error of at most 0.0058.
Values may be sent and summed in bfloat16 or wider, within the bound.
A program may use at most 64 MiB of HBM per device.

```python
import math
import jax
import jax.numpy as jnp
from jax import lax

PUPIL = 256
NF = 512
AY = 64
AX = 80
SIG_DEV = 1024
STEPS = 2
CASES = 4
MODS = 64
NACT = 5120
NSIG = 65536
ROWBLK = 8


def draw_valid_pix(key, part):
    block_pixels = ROWBLK * NF
    keys = jax.random.split(jax.random.fold_in(key, 7), MODS)

    def one_block(block_key):
        return jax.random.permutation(block_key, block_pixels)[:SIG_DEV].astype(jnp.int32)
    picks = jax.vmap(one_block)(keys)
    base = jnp.arange(MODS, dtype=jnp.int32)[:, None] * block_pixels
    flat = (picks + base).reshape(-1).astype(jnp.int32)
    flat = flat.at[0].set(0)
    flat = flat.at[-1].set(NF * NF - 1)
    return flat


def plant(entries, rng, smallest, largest):
    spot = [jax.random.randint(jax.random.fold_in(rng, axis), (), 0, length) for axis, length in enumerate(entries.shape)]
    longest = entries.shape.index(max(entries.shape))
    next_to = spot[:longest] + [(spot[longest] + 1) % entries.shape[longest]] + spot[longest + 1:]
    return entries.at[tuple(spot)].set(smallest).at[tuple(next_to)].set(largest)


def levels(rng, dims, pieces, low, largest):
    def one(dim, parts):
        draws = jax.random.uniform(jax.random.fold_in(jax.random.fold_in(rng, 6), dim), (parts,), jnp.float32, low / len(pieces), largest / len(pieces))
        return jnp.repeat(jnp.exp(draws), dims[dim] // parts).reshape((-1,) + (1,) * (len(dims) - dim - 1))

    loudness = one(*pieces[0])
    for cut in pieces[1:]:
        loudness = loudness * one(*cut)
    return loudness


def bell_draw(key, dims, deviation, reach, pieces=(), kind=jnp.bfloat16):
    values = jax.random.normal(key, dims, jnp.float32) * deviation
    if len(pieces) > 0:
        values = levels(key, dims, pieces, -0.22, 0.18) * values
    return jnp.clip(values, min=-reach, max=reach).astype(kind)


def setup_inputs(seed: int = 0) -> dict:
    streams_of = jax.random.split(jax.random.key(seed), 9)
    return {
        "turbulence": bell_draw(streams_of[0], (CASES, PUPIL, PUPIL), 1.0, 6.0, ((0, 4),), jnp.float32),
        "pupil_amp": jnp.clip(jax.random.uniform(streams_of[1], (PUPIL, PUPIL), jnp.float32, 0.3, 1.0), 0.3, 1.0),
        "mod_points": plant(jax.random.randint(streams_of[2], (MODS,), 0, 256), jax.random.fold_in(streams_of[2], 1), 0, 255).astype(jnp.int32),
        "valid_pix": draw_valid_pix(jax.random.fold_in(streams_of[8], 71), 0),
        "recon": bell_draw(streams_of[4], (NACT, NSIG), NSIG ** -0.5, 0.0234375, ((0, 4), (1, 64))),
        "gx": bell_draw(streams_of[5], (PUPIL, AY), 0.2, 1.2, (), jnp.float32),
        "gy": bell_draw(streams_of[6], (PUPIL, AX), 0.2, 1.2, (), jnp.float32),
        "act_map": jax.random.permutation(streams_of[7], NACT).astype(jnp.int32),
    }


loop_gain = 0.5
radius_pixels = 6.0
point_count = 256

def product(left, right):
    return jnp.dot(left.astype(jnp.float32), right.astype(jnp.float32), preferred_element_type=jnp.float32)

def phase_table(length, pupil_width, sign_factor):
    centred = jnp.arange(length, dtype=jnp.int32) - length // 2
    position = jnp.arange(pupil_width, dtype=jnp.int32)
    wrapped = jnp.mod(centred[:, None] * position[None, :], length).astype(jnp.float32)
    angles = 2.0 * math.pi / length * wrapped
    factor = 1.0 / math.sqrt(length)
    return (jnp.cos(angles) * factor, sign_factor * jnp.sin(angles) * factor)

def optics_tables(pupil_size, length):
    fwd_cos, fwd_sin = phase_table(length, pupil_size, -1.0)
    inv_cos, inv_sin = phase_table(length, length, 1.0)
    inv_cos = inv_cos.T
    inv_sin = inv_sin.T
    table_one = jnp.concatenate([fwd_cos, fwd_sin], 0).astype(jnp.bfloat16)
    table_two = jnp.concatenate([jnp.concatenate([fwd_cos.T, fwd_sin.T], 1), jnp.concatenate([-fwd_sin.T, fwd_cos.T], 1)], 0).astype(jnp.bfloat16)
    table_three = jnp.concatenate([inv_cos, inv_sin], 0).astype(jnp.bfloat16)
    table_four = jnp.concatenate([jnp.concatenate([inv_cos.T, inv_sin.T], 1), jnp.concatenate([-inv_sin.T, inv_cos.T], 1)], 0).astype(jnp.bfloat16)
    offset = jnp.abs(jnp.arange(length, dtype=jnp.float32) - length // 2)
    mask_angle = 0.5 * math.pi * (offset[:, None] + offset[None, :])
    return (table_one, table_two, table_three, table_four, jnp.cos(mask_angle), jnp.sin(mask_angle))

def detector_frame(pupil_phase, amplitude, mod_point, tables):
    table_one, table_two, table_three, table_four, mask_cos, mask_sin = tables
    pupil_size = pupil_phase.shape[0]
    length = mask_cos.shape[0]
    centred = jnp.arange(pupil_size, dtype=jnp.float32) - pupil_size // 2
    tilt_angle = 2.0 * math.pi / point_count * mod_point.astype(jnp.float32)
    tilt_phase = 2.0 * math.pi * radius_pixels / length * (centred[:, None] * jnp.cos(tilt_angle) + centred[None, :] * jnp.sin(tilt_angle))
    total_phase = pupil_phase + tilt_phase
    pupil_field = jnp.concatenate([amplitude * jnp.cos(total_phase), amplitude * jnp.sin(total_phase)], 1).astype(jnp.bfloat16)
    section_one = product(table_one, pupil_field)
    real_part = section_one[:length, :pupil_size] - section_one[length:, pupil_size:]
    imag_part = section_one[:length, pupil_size:] + section_one[length:, :pupil_size]
    focal_half = jnp.concatenate([real_part, imag_part], 1).astype(jnp.bfloat16)
    focal_field = product(focal_half, table_two)
    focal_real = focal_field[:, :length]
    focal_imag = focal_field[:, length:]
    masked = jnp.concatenate([focal_real * mask_cos - focal_imag * mask_sin, focal_real * mask_sin + focal_imag * mask_cos], 1).astype(jnp.bfloat16)
    section_three = product(table_three, masked)
    inverse_half = jnp.concatenate([section_three[:length, :length] - section_three[length:, length:], section_three[:length, length:] + section_three[length:, :length]], 1).astype(jnp.bfloat16)
    detector_field = product(inverse_half, table_four)
    return detector_field[:, :length] ** 2 + detector_field[:, length:] ** 2

def mirror_surface(commands, act_map, gx, gy):
    actuator_grid = commands[act_map].reshape(gx.shape[1], gy.shape[1])
    rows_mapped = jnp.dot(gx, actuator_grid, precision=lax.Precision.HIGHEST, preferred_element_type=jnp.float32)
    return jnp.dot(rows_mapped, gy.T, precision=lax.Precision.HIGHEST, preferred_element_type=jnp.float32)

def reference(turbulence, pupil_amp, mod_points, valid_pix, recon, gx, gy, act_map):
    tables = optics_tables(PUPIL, NF)

    def case_frame(pupil_phase):

        def add_point(running, mod_point):
            return (running + detector_frame(pupil_phase, pupil_amp, mod_point, tables) / MODS, None)
        summed, unused = lax.scan(add_point, jnp.zeros((NF, NF), jnp.float32), mod_points)
        return summed
    command_total = jnp.zeros((CASES, NACT), jnp.float32)
    pupil_phase = turbulence
    frames = jnp.zeros((CASES, NF, NF), jnp.float32)
    for iteration in range(STEPS):
        frames = lax.map(case_frame, pupil_phase)
        signals = frames.reshape(CASES, NF * NF)[:, valid_pix].astype(jnp.bfloat16)
        commands = product(signals, recon.T)
        command_total = command_total + loop_gain * commands
        if iteration + 1 < STEPS:
            surfaces = jax.vmap(lambda single: mirror_surface(single, act_map, gx, gy))(command_total)
            pupil_phase = turbulence - surfaces
    return (command_total, frames)
```

```python
import functools
import math

import jax
import jax.numpy as jnp
import numpy as np
from jax import lax
from jax.experimental import pallas as pl
from jax.experimental.pallas import tpu as pltpu
from jax.sharding import PartitionSpec as P

STEPS = 2
PUPIL = 256
NF = 512
AY = 64
AX = 80
LOOP_GAIN = 0.5
RADIUS = 6.0
POINTS = 256
NX, NYL, NZ = 4, 2, 8
NCASE = 4
MESH = pl.DeviceIdType.MESH
F32 = jnp.float32
BF16 = jnp.bfloat16


def sensor_tables():
    k = np.arange(NF) - NF // 2
    n = np.arange(PUPIL)
    p = np.arange(NF)
    w = np.exp(-2j * np.pi * np.outer(k, n) / NF) / np.sqrt(NF)
    v = np.exp(2j * np.pi * np.outer(p, k) / NF) / np.sqrt(NF)
    turn = np.array([1, 1j, -1, -1j])[np.abs(k) % 4]
    m = (v * turn) @ w
    rows = np.stack([m.real, m.imag]).astype(np.float32)
    return rows, m.imag.T.astype(np.float32)


def sincos(x):
    k = jnp.floor(x * (2.0 / math.pi) + 0.5)
    r = ((x - k * 1.5703125) - k * 4.837512969970703e-4) - k * 7.549789948768648e-8
    r2 = r * r
    s = r + r * r2 * (-1.6666654611e-1 + r2 * (8.3321608736e-3 + r2 * -1.9515295891e-4))
    c = 1.0 + r2 * (-0.5 + r2 * (4.166664568298827e-2 + r2 * (-1.388731625493765e-3 + r2 * 2.443315711809948e-5)))
    q = k - 4.0 * jnp.floor(k * 0.25)
    odd = (q == 1.0) | (q == 3.0)
    sn = jnp.where(odd, c, s)
    cs = jnp.where(odd, s, c)
    sn = jnp.where(q >= 2.0, -sn, sn)
    cs = jnp.where((q == 1.0) | (q == 2.0), -cs, cs)
    return cs, sn


def kernel(
    mod_ref, turb_ref, amp_ref, pix_ref, act_ref, gx_ref, gy_ref, gt_ref, rows_hbm, recon_hbm,
    cmd_out, frame_out,
    recon_ref, rows_ref, mod_a, mod_b, v_ref, l_ref, e_ref, x_ref, t_ref, y_ref,
    oh_sig, oh_act, fr_ref, sig_buf, part_ref, part_bf, plane_buf, tot_ref, z_buf, gat_ref, grid_ref,
    local_sem, send_sem, recv_sem,
):
    c = lax.axis_index("case")
    m = lax.axis_index("mod")
    z = lax.rem(m, NZ)
    xy = lax.div(m, NZ)
    yl = lax.rem(xy, NYL)
    x = lax.div(xy, NYL)

    plane = [(dx, dy, dc) for dx in range(NX) for dy in range(NYL) for dc in range(NCASE) if (dx, dy, dc) != (0, 0, 0)]

    def plane_device(dx, dy, dc):
        px = lax.rem(x + dx, NX)
        py = lax.rem(yl + dy, NYL)
        pc = lax.rem(c + dc, NCASE)
        return pc, (px * NYL + py) * NZ + z

    def z_device(dz):
        return c, xy * NZ + lax.rem(z + dz, NZ)

    barrier = pltpu.get_barrier_semaphore()
    for d in plane:
        pl.semaphore_signal(barrier, inc=1, device_id=plane_device(*d), device_id_type=MESH)
    for dz in range(1, NZ):
        pl.semaphore_signal(barrier, inc=1, device_id=z_device(dz), device_id_type=MESH)

    rows_copy = pltpu.make_async_copy(rows_hbm.at[:, pl.ds(pl.multiple_of(m * 8, 8), 8), :], rows_ref, local_sem.at[0])
    rows_copy.start()
    recon_copy = pltpu.make_async_copy(recon_hbm, recon_ref, local_sem.at[1])
    recon_copy.start()

    def send(src, dst, phase, device):
        pltpu.make_async_remote_copy(
            src_ref=src, dst_ref=dst, send_sem=send_sem.at[phase], recv_sem=recv_sem.at[phase],
            device_id=device, device_id_type=MESH,
        ).start()

    def await_all(ref, phase):
        pltpu.make_async_remote_copy(
            src_ref=ref, dst_ref=ref, send_sem=send_sem.at[phase], recv_sem=recv_sem.at[phase],
            device_id=z_device(1), device_id_type=MESH,
        ).wait_recv()

    def await_sent(ref, phase):
        pltpu.make_async_remote_copy(
            src_ref=ref, dst_ref=ref, send_sem=send_sem.at[phase], recv_sem=recv_sem.at[phase],
            device_id=z_device(1), device_id_type=MESH,
        ).wait_send()

    mod_a[xy] = jnp.full((1, 128), mod_ref[0], jnp.int32).astype(F32)

    def make_field(r, phase):
        cs, sn = sincos(phase)
        amp = amp_ref[r, :]
        er = (amp * cs).astype(BF16)
        ei = (amp * sn).astype(BF16)
        low = slice(r.start + PUPIL, r.stop + PUPIL)
        e_ref[r, 0:PUPIL] = er
        e_ref[r, PUPIL:] = ei
        e_ref[low, 0:PUPIL] = -ei
        e_ref[low, PUPIL:] = er

    for r0 in range(0, PUPIL, 32):
        r = slice(r0, r0 + 32)
        make_field(r, turb_ref[r, :])

    lane = lax.broadcasted_iota(jnp.int32, (128, 128), 0)
    local = pix_ref[...] - m * (8 * NF)
    pix_r = lax.rem(local, 128)
    pix_q = lax.rem(lax.div(local, 128), 4) * 8 + lax.div(local, NF)
    for s in range(8):
        oh_sig[:, 128 * s:128 * s + 128] = jnp.where(lane == pix_r[s:s + 1, :], 1.0, 0.0).astype(BF16)
    act = act_ref[...]
    act_r = lax.rem(act, 128)
    act_q = lax.div(act, 128)
    for s in range(40):
        oh_act[:, 128 * s:128 * s + 128] = jnp.where(lane == act_r[s:s + 1, :], 1.0, 0.0).astype(BF16)
    part_ref[...] = jnp.zeros_like(part_ref)

    pl.semaphore_wait(barrier, len(plane) + NZ - 1)

    near = [(dx, dy) for dx in range(NX) for dy in range(NYL) if (dx, dy) != (0, 0)]
    for dx, dy in near:
        send(mod_a.at[xy], mod_a.at[xy], 0, plane_device(dx, dy, 0))
    await_all(mod_a.at[pl.ds(0, len(near))], 0)
    for j in range(NX * NYL):
        mod_b[z, j:j + 1, :] = mod_a[j]
    for dz in range(1, NZ):
        send(mod_b.at[z], mod_b.at[z], 1, z_device(dz))
    await_all(mod_b.at[pl.ds(0, NZ - 1)], 1)

    angle = (2.0 * math.pi / POINTS) * mod_b[...].reshape(64, 128)
    ca, sa = sincos(angle)
    centred = lax.broadcasted_iota(jnp.int32, (64, 128), 1).astype(F32)
    scale = 2.0 * math.pi * RADIUS / NF
    rows_copy.wait()
    for h in range(2):
        pos = scale * (centred + (128.0 * h - PUPIL // 2))
        cols = slice(128 * h, 128 * h + 128)
        vr, vi = sincos(pos * sa)
        v_ref[0, :, cols] = vr
        v_ref[1, :, cols] = vi
        ur, ui = sincos(pos * ca)
        for i in range(8):
            mr = rows_ref[0, i:i + 1, cols]
            mi = rows_ref[1, i:i + 1, cols]
            l_ref[64 * i:64 * i + 64, cols] = (mr * ur - mi * ui).astype(BF16)
            l_ref[64 * i:64 * i + 64, 128 * h + PUPIL:128 * h + PUPIL + 128] = (mr * ui + mi * ur).astype(BF16)

    for step in range(STEPS):
        if step > 0:
            total = tot_ref[step - 1]
            high = total.astype(BF16)
            low = (total - high.astype(F32)).astype(BF16)
            picked = jnp.dot(jnp.concatenate([high, low], 0), oh_act[...], preferred_element_type=F32)
            q_iota = lax.broadcasted_iota(jnp.int32, (40, 128), 0)
            for s in range(40):
                cols = slice(128 * s, 128 * s + 128)
                block = picked[0:40, cols] + picked[40:80, cols]
                gat_ref[s:s + 1, :] = jnp.sum(jnp.where(q_iota == act_q[s:s + 1, :], block, 0.0), axis=0, keepdims=True)
            for y8 in range(8):
                s5, t = divmod(AX * y8, 128)
                first = gat_ref[pl.ds(s5, 8, stride=5), :]
                if t + AX <= 128:
                    row = first[:, t:t + AX]
                else:
                    second = gat_ref[pl.ds(s5 + 1, 8, stride=5), :]
                    row = jnp.concatenate([first[:, t:], second[:, :t + AX - 128]], axis=1)
                grid_ref[pl.ds(y8, 8, stride=8), :] = jnp.concatenate([row, jnp.zeros((8, 128 - AX), F32)], axis=1)
            mapped = jnp.dot(gx_ref[...], grid_ref[:, 0:AX], precision=lax.Precision.HIGHEST, preferred_element_type=F32)
            surface = lax.dot_general(
                mapped, gy_ref[...], (((1,), (1,)), ((), ())),
                precision=lax.Precision.HIGHEST, preferred_element_type=F32,
            )
            for r0 in range(0, PUPIL, 32):
                r = slice(r0, r0 + 32)
                make_field(r, turb_ref[r, :] - surface[r, :])

        x_ref[...] = jnp.dot(l_ref[...], e_ref[...], preferred_element_type=F32)
        for i in range(8):
            r = slice(64 * i, 64 * i + 64)
            xr = x_ref[r, 0:PUPIL]
            xi = x_ref[r, PUPIL:]
            vr = v_ref[0]
            vi = v_ref[1]
            tr = xr * vr - xi * vi
            ti = xr * vi + xi * vr
            x_ref[r, 0:PUPIL] = tr
            x_ref[r, PUPIL:] = ti
            t_ref[r, :] = tr.astype(BF16)
            t_ref[64 * i + 512:64 * i + 576, :] = ti.astype(BF16)
        y_ref[...] = jnp.dot(t_ref[...], gt_ref[...], preferred_element_type=F32)
        for i in range(8):
            for q in range(4):
                cols = slice(128 * q, 128 * q + 128)
                src = 128 * (1 - q % 2)
                r = slice(64 * i, 64 * i + 64)
                dr = 0.5 * x_ref[r, src:src + 128] - y_ref[64 * i + 512:64 * i + 576, cols]
                di = 0.5 * x_ref[r, src + PUPIL:src + PUPIL + 128] + y_ref[r, cols]
                fr_ref[i:i + 1, cols] = jnp.sum(dr * dr + di * di, axis=0, keepdims=True) * (1.0 / 64)
        frame = fr_ref[...]
        if step == STEPS - 1:
            frame_out[...] = frame

        stacked = jnp.concatenate([frame[:, 128 * q:128 * q + 128] for q in range(4)], axis=0).astype(BF16)
        picked_sig = jnp.dot(stacked, oh_sig[...], preferred_element_type=F32)
        s_iota = lax.broadcasted_iota(jnp.int32, (32, 128), 0)
        for s in range(8):
            cols = slice(128 * s, 128 * s + 128)
            sig_buf[step, c, :, cols] = jnp.sum(
                jnp.where(s_iota == pix_q[s:s + 1, :], picked_sig[:, cols], 0.0), axis=0, keepdims=True
            )
        base = 2 + 3 * step
        for dc in range(1, NCASE):
            send(sig_buf.at[step, c], sig_buf.at[step, c], base, plane_device(0, 0, dc))
        if step == 0:
            recon_copy.wait()
        await_all(sig_buf.at[step, pl.ds(0, NCASE - 1)], base)

        signals = jnp.concatenate([sig_buf[step, k] for k in range(NCASE)], axis=0).astype(BF16)
        part = lax.dot_general(signals, recon_ref[...], (((1,), (1,)), ((), ())), preferred_element_type=F32)
        for k in range(NCASE):
            for j in range(10):
                part_ref[k, j:j + 1, :] = part[k:k + 1, 128 * j:128 * j + 128]
        part_bf[step] = part_ref[...].astype(BF16)
        plane_buf[step, xy * NCASE + c] = part_bf[step, c]
        for d in plane:
            device = plane_device(*d)
            send(part_bf.at[step, device[0]], plane_buf.at[step, xy * NCASE + c], base + 1, device)
        await_all(plane_buf.at[step, pl.ds(0, len(plane))], base + 1)
        for k in range(NCASE):
            acc = plane_buf[step, k].astype(F32)
            for j in range(1, NX * NYL):
                acc = acc + plane_buf[step, j * NCASE + k].astype(F32)
            tot_ref[step, 10 * k:10 * k + 10, :] = acc[0:10, :]
        z_buf[step, z] = tot_ref[step].astype(BF16)
        for dz in range(1, NZ):
            send(z_buf.at[step, z], z_buf.at[step, z], base + 2, z_device(dz))
        await_all(z_buf.at[step, pl.ds(0, NZ - 1)], base + 2)
        acc = z_buf[step, 0].astype(F32)
        for j in range(1, NZ):
            acc = acc + z_buf[step, j].astype(F32)
        acc = LOOP_GAIN * acc
        if step > 0:
            acc = acc + tot_ref[step - 1]
        tot_ref[step] = acc
        if step == STEPS - 1:
            cmd_out[...] = acc

    await_sent(mod_a.at[pl.ds(0, len(near))], 0)
    await_sent(mod_b.at[pl.ds(0, NZ - 1)], 1)
    for step in range(STEPS):
        base = 2 + 3 * step
        await_sent(sig_buf.at[step, pl.ds(0, NCASE - 1)], base)
        await_sent(plane_buf.at[step, pl.ds(0, len(plane))], base + 1)
        await_sent(z_buf.at[step, pl.ds(0, NZ - 1)], base + 2)


def body(turbulence, pupil_amp, mod_points, valid_pix, recon, gx, gy, act_map):
    rows, gt = sensor_tables()
    vmem = pl.BlockSpec(memory_space=pltpu.VMEM)
    anywhere = pl.BlockSpec(memory_space=pl.ANY)
    command, frame = pl.pallas_call(
        kernel,
        out_shape=(jax.ShapeDtypeStruct((40, 128), F32), jax.ShapeDtypeStruct((8, NF), F32)),
        in_specs=[pl.BlockSpec(memory_space=pltpu.SMEM)] + [vmem] * 7 + [anywhere] * 2,
        out_specs=(vmem, vmem),
        scratch_shapes=[
            pltpu.VMEM((1280, 1024), BF16),
            pltpu.VMEM((2, 8, PUPIL), F32),
            pltpu.VMEM((8, 1, 128), F32),
            pltpu.VMEM((8, 8, 128), F32),
            pltpu.VMEM((2, 64, PUPIL), F32),
            pltpu.VMEM((512, 512), BF16),
            pltpu.VMEM((512, 512), BF16),
            pltpu.VMEM((512, 512), F32),
            pltpu.VMEM((1024, PUPIL), BF16),
            pltpu.VMEM((1024, NF), F32),
            pltpu.VMEM((128, 1024), BF16),
            pltpu.VMEM((128, 5120), BF16),
            pltpu.VMEM((8, NF), F32),
            pltpu.VMEM((STEPS, NCASE, 1, 1024), F32),
            pltpu.VMEM((NCASE, 16, 128), F32),
            pltpu.VMEM((STEPS, NCASE, 16, 128), BF16),
            pltpu.VMEM((STEPS, 32, 16, 128), BF16),
            pltpu.VMEM((STEPS, 40, 128), F32),
            pltpu.VMEM((STEPS, NZ, 40, 128), BF16),
            pltpu.VMEM((40, 128), F32),
            pltpu.VMEM((64, 128), F32),
            pltpu.SemaphoreType.DMA((2,)),
            pltpu.SemaphoreType.DMA((2 + 3 * STEPS,)),
            pltpu.SemaphoreType.DMA((2 + 3 * STEPS,)),
        ],
        compiler_params=pltpu.CompilerParams(
            collective_id=0, has_side_effects=True, vmem_limit_bytes=40 * 1024 * 1024
        ),
    )(
        mod_points, turbulence[0], pupil_amp, valid_pix.reshape(8, 128), act_map.reshape(40, 128), gx, gy,
        jnp.asarray(gt).astype(BF16), jnp.asarray(rows), recon,
    )
    return command.reshape(1, 5120), frame[None]


def solution(mesh):
    return jax.shard_map(
        body,
        mesh=mesh,
        in_specs=(P("case", None, None), P(), P("mod"), P("mod"), P("case", "mod"), P(), P(), P()),
        out_specs=(P("case", None), P("case", "mod", None)),
        check_vma=False,
    )
```

```python
import functools
import math

import jax
import jax.numpy as jnp
import numpy as np
from jax import lax
from jax.experimental import pallas as pl
from jax.experimental.pallas import tpu as pltpu
from jax.sharding import PartitionSpec as P

STEPS = 2
PUPIL = 256
NF = 512
AY = 64
AX = 80
LOOP_GAIN = 0.5
RADIUS = 6.0
POINTS = 256
NX, NYL, NZ = 4, 2, 8
NCASE = 4
MESH = pl.DeviceIdType.MESH
F32 = jnp.float32
BF16 = jnp.bfloat16


def sensor_tables():
    k = np.arange(NF) - NF // 2
    n = np.arange(PUPIL)
    p = np.arange(NF)
    w = np.exp(-2j * np.pi * np.outer(k, n) / NF) / np.sqrt(NF)
    v = np.exp(2j * np.pi * np.outer(p, k) / NF) / np.sqrt(NF)
    turn = np.array([1, 1j, -1, -1j])[np.abs(k) % 4]
    m = (v * turn) @ w
    rows = np.stack([m.real, m.imag]).astype(np.float32)
    return rows, m.imag.T.astype(np.float32)


def sincos(x):
    k = jnp.floor(x * (2.0 / math.pi) + 0.5)
    r = ((x - k * 1.5703125) - k * 4.837512969970703e-4) - k * 7.549789948768648e-8
    r2 = r * r
    s = r + r * r2 * (-1.6666654611e-1 + r2 * (8.3321608736e-3 + r2 * -1.9515295891e-4))
    c = 1.0 + r2 * (-0.5 + r2 * (4.166664568298827e-2 + r2 * (-1.388731625493765e-3 + r2 * 2.443315711809948e-5)))
    q = k - 4.0 * jnp.floor(k * 0.25)
    odd = (q == 1.0) | (q == 3.0)
    sn = jnp.where(odd, c, s)
    cs = jnp.where(odd, s, c)
    sn = jnp.where(q >= 2.0, -sn, sn)
    cs = jnp.where((q == 1.0) | (q == 2.0), -cs, cs)
    return cs, sn


def halves(x):
    high = x.astype(BF16)
    return high, (x - high.astype(F32)).astype(BF16)


def kernel(
    mod_ref, turb_hbm, amp_hbm, pix_hbm, act_hbm, gx_hbm, gy_hbm, gt_hbm, rows_hbm, recon_hbm,
    cmd_out, frame_out,
    turb_ref, amp_ref, pix_ref, act_ref, gx_ref, gy_ref, gt_ref, gx_wide, gy_tall,
    recon_ref, rows_ref, mod_a, mod_b, v_ref, l_ref, e_ref, x_ref, t_ref, y_ref,
    oh_sig, oh_act, fr_ref, sig_buf, part_ref, part_bf, plane_buf, tot_ref, z_buf, gat_ref, grid_ref,
    local_sem, send_sem, recv_sem,
):
    c = lax.axis_index("case")
    m = lax.axis_index("mod")
    z = lax.rem(m, NZ)
    xy = lax.div(m, NZ)
    yl = lax.rem(xy, NYL)
    x = lax.div(xy, NYL)

    plane = [(dx, dy, dc) for dx in range(NX) for dy in range(NYL) for dc in range(NCASE) if (dx, dy, dc) != (0, 0, 0)]

    def plane_device(dx, dy, dc):
        px = lax.rem(x + dx, NX)
        py = lax.rem(yl + dy, NYL)
        pc = lax.rem(c + dc, NCASE)
        return pc, (px * NYL + py) * NZ + z

    def z_device(dz):
        return c, xy * NZ + lax.rem(z + dz, NZ)

    barrier = pltpu.get_barrier_semaphore()
    for d in plane:
        pl.semaphore_signal(barrier, inc=1, device_id=plane_device(*d), device_id_type=MESH)
    for dz in range(1, NZ):
        pl.semaphore_signal(barrier, inc=1, device_id=z_device(dz), device_id_type=MESH)

    loads = [
        pltpu.make_async_copy(src, dst, local_sem.at[i])
        for i, (src, dst) in enumerate((
            (turb_hbm, turb_ref), (amp_hbm, amp_ref), (pix_hbm, pix_ref), (act_hbm, act_ref),
            (rows_hbm.at[:, pl.ds(pl.multiple_of(m * 8, 8), 8), :], rows_ref), (gt_hbm, gt_ref),
            (gx_hbm, gx_ref), (gy_hbm, gy_ref), (recon_hbm, recon_ref),
        ))
    ]
    for load in loads:
        load.start()
    turb_load, amp_load, pix_load, act_load, rows_load, gt_load, gx_load, gy_load, recon_load = loads

    def send(src, dst, phase, device):
        pltpu.make_async_remote_copy(
            src_ref=src, dst_ref=dst, send_sem=send_sem.at[phase], recv_sem=recv_sem.at[phase],
            device_id=device, device_id_type=MESH,
        ).start()

    def await_all(ref, phase):
        pltpu.make_async_remote_copy(
            src_ref=ref, dst_ref=ref, send_sem=send_sem.at[phase], recv_sem=recv_sem.at[phase],
            device_id=z_device(1), device_id_type=MESH,
        ).wait_recv()

    def await_sent(ref, phase):
        pltpu.make_async_remote_copy(
            src_ref=ref, dst_ref=ref, send_sem=send_sem.at[phase], recv_sem=recv_sem.at[phase],
            device_id=z_device(1), device_id_type=MESH,
        ).wait_send()

    mod_a[xy] = jnp.full((1, 128), mod_ref[0], jnp.int32).astype(F32)

    def make_field(r, phase):
        cs, sn = sincos(phase)
        amp = amp_ref[r, :]
        er = (amp * cs).astype(BF16)
        ei = (amp * sn).astype(BF16)
        low = slice(r.start + PUPIL, r.stop + PUPIL)
        e_ref[r, 0:PUPIL] = er
        e_ref[r, PUPIL:] = ei
        e_ref[low, 0:PUPIL] = -ei
        e_ref[low, PUPIL:] = er

    turb_load.wait()
    amp_load.wait()
    for r0 in range(0, PUPIL, 32):
        r = slice(r0, r0 + 32)
        make_field(r, turb_ref[r, :])

    lane = lax.broadcasted_iota(jnp.int32, (128, 128), 0)
    pix_load.wait()
    local = pix_ref[...] - m * (8 * NF)
    pix_r = lax.rem(local, 128)
    pix_q = lax.rem(lax.div(local, 128), 4) * 8 + lax.div(local, NF)
    for s in range(8):
        oh_sig[:, 128 * s:128 * s + 128] = jnp.where(lane == pix_r[s:s + 1, :], 1.0, 0.0).astype(BF16)
    act_load.wait()
    act = act_ref[...]
    act_r = lax.rem(act, 128)
    act_q = lax.div(act, 128)
    for s in range(40):
        oh_act[:, 128 * s:128 * s + 128] = jnp.where(lane == act_r[s:s + 1, :], 1.0, 0.0).astype(BF16)
    part_ref[...] = jnp.zeros_like(part_ref)
    grid_ref[...] = jnp.zeros_like(grid_ref)

    gx_load.wait()
    gx_high, gx_low = halves(gx_ref[...].T)
    gx_wide[:, 0:AY] = gx_high
    gx_wide[:, AY:2 * AY] = gx_low
    gx_wide[:, 2 * AY:] = gx_high
    gy_load.wait()
    gy_high, gy_low = halves(gy_ref[...])
    gy_tall[...] = jnp.zeros_like(gy_tall)
    gy_tall[0:AX, :] = gy_high
    gy_tall[128:128 + AX, :] = gy_high
    gy_tall[256:256 + AX, :] = gy_low
    gt_load.wait()

    pl.semaphore_wait(barrier, len(plane) + NZ - 1)

    near = [(dx, dy) for dx in range(NX) for dy in range(NYL) if (dx, dy) != (0, 0)]
    for dx, dy in near:
        send(mod_a.at[xy], mod_a.at[xy], 0, plane_device(dx, dy, 0))
    await_all(mod_a.at[pl.ds(0, len(near))], 0)
    for j in range(NX * NYL):
        mod_b[z, j:j + 1, :] = mod_a[j]
    for dz in range(1, NZ):
        send(mod_b.at[z], mod_b.at[z], 1, z_device(dz))
    await_all(mod_b.at[pl.ds(0, NZ - 1)], 1)

    angle = (2.0 * math.pi / POINTS) * mod_b[...].reshape(64, 128)
    ca, sa = sincos(angle)
    centred = lax.broadcasted_iota(jnp.int32, (64, 128), 1).astype(F32)
    scale = 2.0 * math.pi * RADIUS / NF
    rows_load.wait()
    for h in range(2):
        pos = scale * (centred + (128.0 * h - PUPIL // 2))
        cols = slice(128 * h, 128 * h + 128)
        vr, vi = sincos(pos * sa)
        v_ref[0, :, cols] = vr
        v_ref[1, :, cols] = vi
        ur, ui = sincos(pos * ca)
        for i in range(8):
            mr = rows_ref[0, i:i + 1, cols]
            mi = rows_ref[1, i:i + 1, cols]
            l_ref[64 * i:64 * i + 64, cols] = (mr * ur - mi * ui).astype(BF16)
            l_ref[64 * i:64 * i + 64, 128 * h + PUPIL:128 * h + PUPIL + 128] = (mr * ui + mi * ur).astype(BF16)

    for step in range(STEPS):
        if step > 0:
            total = tot_ref[step - 1]
            high, low = halves(total)
            picked = jnp.dot(jnp.concatenate([high, low], 0), oh_act[...], preferred_element_type=F32)
            q_iota = lax.broadcasted_iota(jnp.int32, (40, 128), 0)
            for s in range(40):
                cols = slice(128 * s, 128 * s + 128)
                block = picked[0:40, cols] + picked[40:80, cols]
                gat_ref[s:s + 1, :] = jnp.sum(jnp.where(q_iota == act_q[s:s + 1, :], block, 0.0), axis=0, keepdims=True)
            for y8 in range(8):
                s5, t = divmod(AX * y8, 128)
                first = gat_ref[pl.ds(s5, 8, stride=5), :]
                if t + AX <= 128:
                    row = first[:, t:t + AX]
                else:
                    second = gat_ref[pl.ds(s5 + 1, 8, stride=5), :]
                    row = jnp.concatenate([first[:, t:], second[:, :t + AX - 128]], axis=1)
                grid_ref[pl.ds(y8, 8, stride=8), :] = jnp.concatenate([row, jnp.zeros((8, 128 - AX), F32)], axis=1)
            grid_high, grid_low = halves(grid_ref[...])
            mapped = jnp.dot(
                jnp.concatenate([grid_high, grid_low, grid_high], axis=1), gy_tall[...], preferred_element_type=F32
            )
            mapped_high, mapped_low = halves(mapped)
            surface = jnp.dot(
                gx_wide[...], jnp.concatenate([mapped_high, mapped_high, mapped_low], axis=0),
                preferred_element_type=F32,
            )
            for r0 in range(0, PUPIL, 32):
                r = slice(r0, r0 + 32)
                make_field(r, turb_ref[r, :] - surface[r, :])

        x_ref[...] = jnp.dot(l_ref[...], e_ref[...], preferred_element_type=F32)
        for i in range(8):
            r = slice(64 * i, 64 * i + 64)
            xr = x_ref[r, 0:PUPIL]
            xi = x_ref[r, PUPIL:]
            vr = v_ref[0]
            vi = v_ref[1]
            tr = xr * vr - xi * vi
            ti = xr * vi + xi * vr
            x_ref[r, 0:PUPIL] = tr
            x_ref[r, PUPIL:] = ti
            t_ref[r, :] = tr.astype(BF16)
            t_ref[64 * i + 512:64 * i + 576, :] = ti.astype(BF16)
        y_ref[...] = jnp.dot(t_ref[...], gt_ref[...], preferred_element_type=F32)
        for i in range(8):
            for q in range(4):
                cols = slice(128 * q, 128 * q + 128)
                src = 128 * (1 - q % 2)
                r = slice(64 * i, 64 * i + 64)
                dr = 0.5 * x_ref[r, src:src + 128] - y_ref[64 * i + 512:64 * i + 576, cols]
                di = 0.5 * x_ref[r, src + PUPIL:src + PUPIL + 128] + y_ref[r, cols]
                fr_ref[i:i + 1, cols] = jnp.sum(dr * dr + di * di, axis=0, keepdims=True) * (1.0 / 64)
        frame = fr_ref[...]
        if step == STEPS - 1:
            frame_out[...] = frame

        stacked = jnp.concatenate([frame[:, 128 * q:128 * q + 128] for q in range(4)], axis=0).astype(BF16)
        picked_sig = jnp.dot(stacked, oh_sig[...], preferred_element_type=F32)
        s_iota = lax.broadcasted_iota(jnp.int32, (32, 128), 0)
        for s in range(8):
            cols = slice(128 * s, 128 * s + 128)
            sig_buf[step, c, :, cols] = jnp.sum(
                jnp.where(s_iota == pix_q[s:s + 1, :], picked_sig[:, cols], 0.0), axis=0, keepdims=True
            )
        base = 2 + 3 * step
        for dc in range(1, NCASE):
            send(sig_buf.at[step, c], sig_buf.at[step, c], base, plane_device(0, 0, dc))
        if step == 0:
            recon_load.wait()
        await_all(sig_buf.at[step, pl.ds(0, NCASE - 1)], base)

        signals = jnp.concatenate([sig_buf[step, k] for k in range(NCASE)], axis=0).astype(BF16)
        part = lax.dot_general(signals, recon_ref[...], (((1,), (1,)), ((), ())), preferred_element_type=F32)
        for k in range(NCASE):
            for j in range(10):
                part_ref[k, j:j + 1, :] = part[k:k + 1, 128 * j:128 * j + 128]
        part_bf[step] = part_ref[...].astype(BF16)
        plane_buf[step, xy * NCASE + c] = part_bf[step, c]
        for d in plane:
            device = plane_device(*d)
            send(part_bf.at[step, device[0]], plane_buf.at[step, xy * NCASE + c], base + 1, device)
        await_all(plane_buf.at[step, pl.ds(0, len(plane))], base + 1)
        for k in range(NCASE):
            acc = plane_buf[step, k].astype(F32)
            for j in range(1, NX * NYL):
                acc = acc + plane_buf[step, j * NCASE + k].astype(F32)
            tot_ref[step, 10 * k:10 * k + 10, :] = acc[0:10, :]
        z_buf[step, z] = tot_ref[step].astype(BF16)
        for dz in range(1, NZ):
            send(z_buf.at[step, z], z_buf.at[step, z], base + 2, z_device(dz))
        await_all(z_buf.at[step, pl.ds(0, NZ - 1)], base + 2)
        acc = z_buf[step, 0].astype(F32)
        for j in range(1, NZ):
            acc = acc + z_buf[step, j].astype(F32)
        acc = LOOP_GAIN * acc
        if step > 0:
            acc = acc + tot_ref[step - 1]
        tot_ref[step] = acc
        if step == STEPS - 1:
            cmd_out[...] = acc

    await_sent(mod_a.at[pl.ds(0, len(near))], 0)
    await_sent(mod_b.at[pl.ds(0, NZ - 1)], 1)
    for step in range(STEPS):
        base = 2 + 3 * step
        await_sent(sig_buf.at[step, pl.ds(0, NCASE - 1)], base)
        await_sent(plane_buf.at[step, pl.ds(0, len(plane))], base + 1)
        await_sent(z_buf.at[step, pl.ds(0, NZ - 1)], base + 2)


def body(turbulence, pupil_amp, mod_points, valid_pix, recon, gx, gy, act_map):
    rows, gt = sensor_tables()
    vmem = pl.BlockSpec(memory_space=pltpu.VMEM)
    hbm = pl.BlockSpec(memory_space=pltpu.HBM)
    command, frame = pl.pallas_call(
        kernel,
        out_shape=(jax.ShapeDtypeStruct((40, 128), F32), jax.ShapeDtypeStruct((8, NF), F32)),
        in_specs=[pl.BlockSpec(memory_space=pltpu.SMEM)] + [hbm] * 9,
        out_specs=(vmem, vmem),
        scratch_shapes=[
            pltpu.VMEM((PUPIL, PUPIL), F32),
            pltpu.VMEM((PUPIL, PUPIL), F32),
            pltpu.VMEM((8, 128), jnp.int32),
            pltpu.VMEM((40, 128), jnp.int32),
            pltpu.VMEM((AY, PUPIL), F32),
            pltpu.VMEM((AX, PUPIL), F32),
            pltpu.VMEM((PUPIL, NF), BF16),
            pltpu.VMEM((PUPIL, 3 * AY), BF16),
            pltpu.VMEM((384, PUPIL), BF16),
            pltpu.VMEM((1280, 1024), BF16),
            pltpu.VMEM((2, 8, PUPIL), F32),
            pltpu.VMEM((8, 1, 128), F32),
            pltpu.VMEM((8, 8, 128), F32),
            pltpu.VMEM((2, 64, PUPIL), F32),
            pltpu.VMEM((512, 512), BF16),
            pltpu.VMEM((512, 512), BF16),
            pltpu.VMEM((512, 512), F32),
            pltpu.VMEM((1024, PUPIL), BF16),
            pltpu.VMEM((1024, NF), F32),
            pltpu.VMEM((128, 1024), BF16),
            pltpu.VMEM((128, 5120), BF16),
            pltpu.VMEM((8, NF), F32),
            pltpu.VMEM((STEPS, NCASE, 1, 1024), F32),
            pltpu.VMEM((NCASE, 16, 128), F32),
            pltpu.VMEM((STEPS, NCASE, 16, 128), BF16),
            pltpu.VMEM((STEPS, 32, 16, 128), BF16),
            pltpu.VMEM((STEPS, 40, 128), F32),
            pltpu.VMEM((STEPS, NZ, 40, 128), BF16),
            pltpu.VMEM((40, 128), F32),
            pltpu.VMEM((64, 128), F32),
            pltpu.SemaphoreType.DMA((9,)),
            pltpu.SemaphoreType.DMA((2 + 3 * STEPS,)),
            pltpu.SemaphoreType.DMA((2 + 3 * STEPS,)),
        ],
        compiler_params=pltpu.CompilerParams(
            collective_id=0, has_side_effects=True, vmem_limit_bytes=60 * 1024 * 1024
        ),
    )(
        mod_points, turbulence[0], pupil_amp, valid_pix.reshape(8, 128), act_map.reshape(40, 128), gx.T, gy.T,
        jnp.asarray(gt).astype(BF16), jnp.asarray(rows), recon,
    )
    return command.reshape(1, 5120), frame[None]


def solution(mesh):
    return jax.shard_map(
        body,
        mesh=mesh,
        in_specs=(P("case", None, None), P(), P("mod"), P("mod"), P("case", "mod"), P(), P(), P()),
        out_specs=(P("case", None), P("case", "mod", None)),
        check_vma=False,
    )
```

```python
import functools
import math

import jax
import jax.numpy as jnp
import numpy as np
from jax import lax
from jax.experimental import pallas as pl
from jax.experimental.pallas import tpu as pltpu
from jax.sharding import PartitionSpec as P

STEPS = 2
PUPIL = 256
NF = 512
AY = 64
AX = 80
LOOP_GAIN = 0.5
RADIUS = 6.0
POINTS = 256
NX, NYL, NZ = 4, 2, 8
NCASE = 4
MESH = pl.DeviceIdType.MESH
F32 = jnp.float32
BF16 = jnp.bfloat16


def sensor_tables():
    k = np.arange(NF) - NF // 2
    n = np.arange(PUPIL)
    p = np.arange(NF)
    w = np.exp(-2j * np.pi * np.outer(k, n) / NF) / np.sqrt(NF)
    v = np.exp(2j * np.pi * np.outer(p, k) / NF) / np.sqrt(NF)
    turn = np.array([1, 1j, -1, -1j])[np.abs(k) % 4]
    m = (v * turn) @ w
    rows = np.stack([m.real, m.imag]).astype(np.float32)
    return rows, 2.0 * m.imag.T.astype(np.float32)


def sincos(x):
    t = x * (0.5 / math.pi)
    f = t - jnp.floor(t + 0.5)
    g = f * f
    s = 0.15457872399485673
    for a in (-1.1961721628983193, 5.100079202734692, -10.33541503027875, 6.283185189118328):
        s = s * g + a
    s = s * f
    c = -0.024431927347214694
    for a in (0.23496099890009817, -1.3352176583726172, 4.058709736748474, -4.93480215997534, 1.0):
        c = c * g + a
    return 1.0 - 0.5 * (s * s), s * c


def halves(x):
    high = x.astype(BF16)
    return high, (x - high.astype(F32)).astype(BF16)


def kernel(
    mod_ref, turb_hbm, amp_hbm, pix_hbm, act_hbm, gx_hbm, gy_hbm, gt_hbm, rows_hbm, recon_hbm,
    cmd_out, frame_out,
    turb_ref, amp_ref, pix_ref, act_ref, gx_ref, gy_ref, gt_ref, gx_wide, gy_tall,
    recon_ref, recon_t, rows_ref, mod_a, mod_b, v_ref, l_ref, e_ref, x_ref, t_ref, y_ref,
    oh_sig, oh_act, fr_ref, sig_buf, part_bf, plane_buf, tot_ref, z_buf, gat_ref, grid_ref,
    local_sem, send_sem, recv_sem,
):
    c = lax.axis_index("case")
    m = lax.axis_index("mod")
    z = lax.rem(m, NZ)
    xy = lax.div(m, NZ)
    yl = lax.rem(xy, NYL)
    x = lax.div(xy, NYL)

    high = lax.div(c, 2)
    core = lax.rem(c, 2)

    def hops(d):
        return min(d[0], NX - d[0]) + (2 if d[2] and not d[1] else 1 if d[1] else 0)

    plane = [(dx, fl, fh, fc) for dx in range(NX) for fl in range(2) for fh in range(2) for fc in range(2)]
    plane = sorted(plane[1:], key=hops, reverse=True)
    column = sorted(range(1, NZ), key=lambda d: min(d, NZ - d), reverse=True)

    def plane_device(dx, fl, fh, fc):
        px = lax.rem(x + dx, NX)
        py = lax.rem(yl + fl, NYL)
        return lax.rem(high + fh, 2) * 2 + lax.rem(core + fc, 2), (px * NYL + py) * NZ + z

    def z_device(dz):
        return c, xy * NZ + lax.rem(z + dz, NZ)

    barrier = pltpu.get_barrier_semaphore()
    for d in plane:
        pl.semaphore_signal(barrier, inc=1, device_id=plane_device(*d), device_id_type=MESH)
    for dz in column:
        pl.semaphore_signal(barrier, inc=1, device_id=z_device(dz), device_id_type=MESH)

    loads = [
        pltpu.make_async_copy(src, dst, local_sem.at[i])
        for i, (src, dst) in enumerate((
            (turb_hbm, turb_ref), (amp_hbm, amp_ref), (pix_hbm, pix_ref), (act_hbm, act_ref),
            (rows_hbm.at[:, pl.ds(pl.multiple_of(m * 8, 8), 8), :], rows_ref), (gt_hbm, gt_ref),
            (gx_hbm, gx_ref), (gy_hbm, gy_ref), (recon_hbm, recon_ref),
        ))
    ]
    for load in loads:
        load.start()
    turb_load, amp_load, pix_load, act_load, rows_load, gt_load, gx_load, gy_load, recon_load = loads

    def send(src, dst, phase, device):
        pltpu.make_async_remote_copy(
            src_ref=src, dst_ref=dst, send_sem=send_sem.at[phase], recv_sem=recv_sem.at[phase],
            device_id=device, device_id_type=MESH,
        ).start()

    def await_all(ref, phase):
        pltpu.make_async_remote_copy(
            src_ref=ref, dst_ref=ref, send_sem=send_sem.at[phase], recv_sem=recv_sem.at[phase],
            device_id=z_device(1), device_id_type=MESH,
        ).wait_recv()

    def await_sent(ref, phase):
        pltpu.make_async_remote_copy(
            src_ref=ref, dst_ref=ref, send_sem=send_sem.at[phase], recv_sem=recv_sem.at[phase],
            device_id=z_device(1), device_id_type=MESH,
        ).wait_send()

    mod_a[xy] = jnp.full((1, 128), mod_ref[0], jnp.int32).astype(F32)

    def make_field(r, phase):
        cs, sn = sincos(phase)
        amp = amp_ref[r, :]
        er = (amp * cs).astype(BF16)
        ei = (amp * sn).astype(BF16)
        low = slice(r.start + PUPIL, r.stop + PUPIL)
        e_ref[r, 0:PUPIL] = er
        e_ref[r, PUPIL:] = ei
        e_ref[low, 0:PUPIL] = -ei
        e_ref[low, PUPIL:] = er

    turb_load.wait()
    amp_load.wait()
    for r0 in range(0, PUPIL, 32):
        r = slice(r0, r0 + 32)
        make_field(r, turb_ref[r, :])

    pl.semaphore_wait(barrier, len(plane) + NZ - 1)

    near = [d for d in plane if d[2] == 0 and d[3] == 0]
    for d in near:
        send(mod_a.at[xy], mod_a.at[xy], 0, plane_device(*d))

    lane = lax.broadcasted_iota(jnp.int32, (128, 128), 0)
    pix_load.wait()
    local = pix_ref[...] - m * (8 * NF)
    pix_r = lax.rem(local, 128)
    pix_q = lax.rem(lax.div(local, 128), 4) * 8 + lax.div(local, NF)
    for s in range(8):
        oh_sig[:, 128 * s:128 * s + 128] = jnp.where(lane == pix_r[s:s + 1, :], 1.0, 0.0).astype(BF16)
    act_load.wait()
    act = act_ref[...]
    act_r = lax.rem(act, 128)
    act_q = lax.div(act, 128)
    act_q = lax.rem(act_q, 5) * 8 + lax.div(act_q, 5)
    for s in range(40):
        hot = jnp.where(lane == act_r[s:s + 1, :], 1.0, 0.0).astype(BF16)
        oh_act[0:128, 128 * s:128 * s + 128] = hot
        oh_act[128:256, 128 * s:128 * s + 128] = hot
    grid_ref[...] = jnp.zeros_like(grid_ref)

    gx_load.wait()
    gx_high, gx_low = halves(gx_ref[...].T)
    gx_wide[:, 0:AY] = gx_high
    gx_wide[:, AY:2 * AY] = gx_low
    gx_wide[:, 2 * AY:] = gx_high
    gy_load.wait()
    gy_high, gy_low = halves(gy_ref[...])
    gy_tall[...] = jnp.zeros_like(gy_tall)
    gy_tall[0:AX, :] = gy_high
    gy_tall[128:128 + AX, :] = gy_high
    gy_tall[256:256 + AX, :] = gy_low

    await_all(mod_a.at[pl.ds(0, len(near))], 0)
    for j in range(NX * NYL):
        mod_b[z, j:j + 1, :] = mod_a[j]
    for dz in column:
        send(mod_b.at[z], mod_b.at[z], 1, z_device(dz))
    recon_load.wait()
    for i in range(10):
        recon_t[:, 128 * i:128 * i + 128] = recon_ref[128 * i:128 * i + 128, :].T
    gt_load.wait()
    await_all(mod_b.at[pl.ds(0, NZ - 1)], 1)

    angle = (2.0 * math.pi / POINTS) * mod_b[...].reshape(64, 128)
    ca, sa = sincos(angle)
    centred = lax.broadcasted_iota(jnp.int32, (64, 128), 1).astype(F32)
    scale = 2.0 * math.pi * RADIUS / NF
    rows_load.wait()
    for h in range(2):
        pos = scale * (centred + (128.0 * h - PUPIL // 2))
        cols = slice(128 * h, 128 * h + 128)
        vr, vi = sincos(pos * sa)
        v_ref[0, :, cols] = vr
        v_ref[1, :, cols] = vi
        ur, ui = sincos(pos * ca)
        for i in range(8):
            mr = rows_ref[0, i:i + 1, cols]
            mi = rows_ref[1, i:i + 1, cols]
            l_ref[64 * i:64 * i + 64, cols] = (mr * ur - mi * ui).astype(BF16)
            l_ref[64 * i:64 * i + 64, 128 * h + PUPIL:128 * h + PUPIL + 128] = (mr * ui + mi * ur).astype(BF16)

    for step in range(STEPS):
        if step > 0:
            total = tot_ref[step - 1]
            stacked = jnp.concatenate([total[:, 128 * t:128 * t + 128] for t in range(5)], axis=0)
            picked = jnp.dot(jnp.concatenate(halves(stacked), axis=1), oh_act[...], preferred_element_type=F32)
            q_iota = lax.broadcasted_iota(jnp.int32, (40, 128), 0)
            for s in range(40):
                cols = slice(128 * s, 128 * s + 128)
                block = picked[:, cols]
                gat_ref[s:s + 1, :] = jnp.sum(jnp.where(q_iota == act_q[s:s + 1, :], block, 0.0), axis=0, keepdims=True)
            for y8 in range(8):
                s5, t = divmod(AX * y8, 128)
                first = gat_ref[pl.ds(s5, 8, stride=5), :]
                if t + AX <= 128:
                    row = first[:, t:t + AX]
                else:
                    second = gat_ref[pl.ds(s5 + 1, 8, stride=5), :]
                    row = jnp.concatenate([first[:, t:], second[:, :t + AX - 128]], axis=1)
                grid_ref[pl.ds(y8, 8, stride=8), :] = jnp.concatenate([row, jnp.zeros((8, 128 - AX), F32)], axis=1)
            grid_high, grid_low = halves(grid_ref[...])
            mapped = jnp.dot(
                jnp.concatenate([grid_high, grid_low, grid_high], axis=1), gy_tall[...], preferred_element_type=F32
            )
            mapped_high, mapped_low = halves(mapped)
            surface = jnp.dot(
                gx_wide[...], jnp.concatenate([mapped_high, mapped_high, mapped_low], axis=0),
                preferred_element_type=F32,
            )
            for r0 in range(0, PUPIL, 32):
                r = slice(r0, r0 + 32)
                make_field(r, turb_ref[r, :] - surface[r, :])

        x_ref[...] = jnp.dot(l_ref[...], e_ref[...], preferred_element_type=F32)
        for i in range(8):
            r = slice(64 * i, 64 * i + 64)
            xr = x_ref[r, 0:PUPIL]
            xi = x_ref[r, PUPIL:]
            vr = v_ref[0]
            vi = v_ref[1]
            tr = xr * vr - xi * vi
            ti = xr * vi + xi * vr
            x_ref[r, 0:PUPIL] = tr
            x_ref[r, PUPIL:] = ti
            t_ref[r, :] = tr.astype(BF16)
            t_ref[64 * i + 512:64 * i + 576, :] = ti.astype(BF16)
        y_ref[...] = jnp.dot(t_ref[...], gt_ref[...], preferred_element_type=F32)
        for i in range(8):
            for q in range(4):
                cols = slice(128 * q, 128 * q + 128)
                src = 128 * (1 - q % 2)
                r = slice(64 * i, 64 * i + 64)
                dr = x_ref[r, src:src + 128] - y_ref[64 * i + 512:64 * i + 576, cols]
                di = x_ref[r, src + PUPIL:src + PUPIL + 128] + y_ref[r, cols]
                fr_ref[i:i + 1, cols] = jnp.sum(dr * dr + di * di, axis=0, keepdims=True) * (1.0 / 256)
        frame = fr_ref[...]
        if step == STEPS - 1:
            frame_out[...] = frame

        tiles = jnp.concatenate([frame[:, 128 * q:128 * q + 128] for q in range(4)], axis=0).astype(BF16)
        found = jnp.dot(tiles, oh_sig[...], preferred_element_type=F32)
        s_iota = lax.broadcasted_iota(jnp.int32, (32, 128), 0)
        for s in range(8):
            cols = slice(128 * s, 128 * s + 128)
            sig_buf[step, c, :, cols] = jnp.sum(
                jnp.where(s_iota == pix_q[s:s + 1, :], found[:, cols], 0.0), axis=0, keepdims=True
            )
        base = 2 + 3 * step
        for fh, fc in ((1, 1), (1, 0), (0, 1)):
            send(sig_buf.at[step, c], sig_buf.at[step, c], base, plane_device(0, 0, fh, fc))
        await_all(sig_buf.at[step, pl.ds(0, NCASE - 1)], base)

        signals = jnp.concatenate([sig_buf[step, k] for k in range(NCASE)], axis=0).astype(BF16)
        part = jnp.dot(signals, recon_t[...], preferred_element_type=F32)
        for k in range(NCASE):
            rows = [part[k:k + 1, 640 * h:640 * h + 640] for h in range(2)]
            part_bf[step, k] = jnp.concatenate(rows, axis=0).astype(BF16)
        plane_buf[step, xy * NCASE + c] = part_bf[step, c]
        for d in plane:
            device = plane_device(*d)
            send(part_bf.at[step, device[0]], plane_buf.at[step, xy * NCASE + c], base + 1, device)
        await_all(plane_buf.at[step, pl.ds(0, len(plane))], base + 1)
        for k in range(NCASE):
            acc = plane_buf[step, k].astype(F32)
            for j in range(1, NX * NYL):
                acc = acc + plane_buf[step, j * NCASE + k].astype(F32)
            tot_ref[step, 2 * k:2 * k + 2, :] = acc
        z_buf[step, z] = tot_ref[step].astype(BF16)
        for dz in column:
            send(z_buf.at[step, z], z_buf.at[step, z], base + 2, z_device(dz))
        await_all(z_buf.at[step, pl.ds(0, NZ - 1)], base + 2)
        acc = z_buf[step, 0].astype(F32)
        for j in range(1, NZ):
            acc = acc + z_buf[step, j].astype(F32)
        acc = LOOP_GAIN * acc
        if step > 0:
            acc = acc + tot_ref[step - 1]
        tot_ref[step] = acc
        if step == STEPS - 1:
            for t in range(5):
                cmd_out[pl.ds(t, 8, stride=5), :] = acc[:, 128 * t:128 * t + 128]

    await_sent(mod_a.at[pl.ds(0, len(near))], 0)
    await_sent(mod_b.at[pl.ds(0, NZ - 1)], 1)
    for step in range(STEPS):
        base = 2 + 3 * step
        await_sent(sig_buf.at[step, pl.ds(0, NCASE - 1)], base)
        await_sent(plane_buf.at[step, pl.ds(0, len(plane))], base + 1)
        await_sent(z_buf.at[step, pl.ds(0, NZ - 1)], base + 2)


def body(turbulence, pupil_amp, mod_points, valid_pix, recon, gx, gy, act_map):
    rows, gt = sensor_tables()
    vmem = pl.BlockSpec(memory_space=pltpu.VMEM)
    hbm = pl.BlockSpec(memory_space=pltpu.HBM)
    command, frame = pl.pallas_call(
        kernel,
        out_shape=(pltpu.VMEM((40, 128), F32), pltpu.VMEM((8, NF), F32)),
        in_specs=[pl.BlockSpec(memory_space=pltpu.SMEM)] + [hbm] * 9,
        out_specs=(vmem, vmem),
        scratch_shapes=[
            pltpu.VMEM((PUPIL, PUPIL), F32),
            pltpu.VMEM((PUPIL, PUPIL), F32),
            pltpu.VMEM((8, 128), jnp.int32),
            pltpu.VMEM((40, 128), jnp.int32),
            pltpu.VMEM((AY, PUPIL), F32),
            pltpu.VMEM((AX, PUPIL), F32),
            pltpu.VMEM((PUPIL, NF), BF16),
            pltpu.VMEM((PUPIL, 3 * AY), BF16),
            pltpu.VMEM((384, PUPIL), BF16),
            pltpu.VMEM((1280, 1024), BF16),
            pltpu.VMEM((1024, 1280), BF16),
            pltpu.VMEM((2, 8, PUPIL), F32),
            pltpu.VMEM((8, 1, 128), F32),
            pltpu.VMEM((8, 8, 128), F32),
            pltpu.VMEM((2, 64, PUPIL), F32),
            pltpu.VMEM((512, 512), BF16),
            pltpu.VMEM((512, 512), BF16),
            pltpu.VMEM((512, 512), F32),
            pltpu.VMEM((1024, PUPIL), BF16),
            pltpu.VMEM((1024, NF), F32),
            pltpu.VMEM((128, 1024), BF16),
            pltpu.VMEM((256, 5120), BF16),
            pltpu.VMEM((8, NF), F32),
            pltpu.VMEM((STEPS, NCASE, 1, 1024), F32),
            pltpu.VMEM((STEPS, NCASE, 2, 640), BF16),
            pltpu.VMEM((STEPS, 32, 2, 640), BF16),
            pltpu.VMEM((STEPS, 8, 640), F32),
            pltpu.VMEM((STEPS, NZ, 8, 640), BF16),
            pltpu.VMEM((40, 128), F32),
            pltpu.VMEM((64, 128), F32),
            pltpu.SemaphoreType.DMA((9,)),
            pltpu.SemaphoreType.DMA((2 + 3 * STEPS,)),
            pltpu.SemaphoreType.DMA((2 + 3 * STEPS,)),
        ],
        compiler_params=pltpu.CompilerParams(
            collective_id=0, has_side_effects=True, vmem_limit_bytes=60 * 1024 * 1024
        ),
    )(
        mod_points, turbulence[0], pupil_amp, valid_pix.reshape(8, 128), act_map.reshape(40, 128), gx.T, gy.T,
        jnp.asarray(gt).astype(BF16), jnp.asarray(rows), recon,
    )
    return command.reshape(1, 5120), frame[None]


def solution(mesh):
    return jax.shard_map(
        body,
        mesh=mesh,
        in_specs=(P("case", None, None), P(), P("mod"), P("mod"), P("case", "mod"), P(), P(), P()),
        out_specs=(P("case", None), P("case", "mod", None)),
        check_vma=False,
    )
```

```python
import functools
import math

import jax
import jax.numpy as jnp
import numpy as np
from jax import lax
from jax.experimental import pallas as pl
from jax.experimental.pallas import tpu as pltpu
from jax.sharding import PartitionSpec as P

STEPS = 2
PUPIL = 256
NF = 512
AY = 64
AX = 80
LOOP_GAIN = 0.5
RADIUS = 6.0
POINTS = 256
NX, NYL, NZ = 4, 2, 8
NCASE = 4
MESH = pl.DeviceIdType.MESH
F32 = jnp.float32
BF16 = jnp.bfloat16


def sensor_tables():
    k = np.arange(NF) - NF // 2
    n = np.arange(PUPIL)
    p = np.arange(NF)
    w = np.exp(-2j * np.pi * np.outer(k, n) / NF) / np.sqrt(NF)
    v = np.exp(2j * np.pi * np.outer(p, k) / NF) / np.sqrt(NF)
    turn = np.array([1, 1j, -1, -1j])[np.abs(k) % 4]
    m = (v * turn) @ w
    rows = np.stack([m.real, m.imag]).astype(np.float32)
    return rows, 2.0 * m.imag.T.astype(np.float32)


def sincos(x):
    t = x * (0.5 / math.pi)
    f = t - jnp.floor(t + 0.5)
    g = f * f
    s = 0.10920575
    for a in (-0.8457636, 3.60628896, -7.30824115, 4.44288283):
        s = s * g + a
    s = s * f
    c = 0.31124104
    for a in (-1.88386521, 5.73951693, -6.97885475, 1.4142135623730951):
        c = c * g + a
    return 1.0 - s * s, s * c


def halves(x):
    high = x.astype(BF16)
    return high, (x - high.astype(F32)).astype(BF16)


def kernel(
    mod_ref, turb_hbm, amp_hbm, pix_hbm, act_hbm, gx_hbm, gy_hbm, gt_hbm, rows_hbm, recon_hbm,
    cmd_out, frame_out,
    turb_ref, amp_ref, pix_ref, act_ref, gx_ref, gy_ref, gt_ref, gx_wide, gy_tall,
    recon_ref, recon_t, rows_ref, mod_a, mod_b, v_ref, l_ref, e_ref, x_ref, t_ref, y_ref,
    oh_sig, oh_act, fr_ref, sig_buf, part_bf, plane_buf, tot_ref, z_buf, gat_ref, grid_ref,
    local_sem, send_sem, recv_sem,
):
    c = lax.axis_index("case")
    m = lax.axis_index("mod")
    z = lax.rem(m, NZ)
    xy = lax.div(m, NZ)
    yl = lax.rem(xy, NYL)
    x = lax.div(xy, NYL)

    high = lax.div(c, 2)
    core = lax.rem(c, 2)

    def hops(d):
        return min(d[0], NX - d[0]) + (2 if d[2] and not d[1] else 1 if d[1] else 0)

    plane = [(dx, fl, fh, fc) for dx in range(NX) for fl in range(2) for fh in range(2) for fc in range(2)]
    plane = sorted(plane[1:], key=hops, reverse=True)
    column = sorted(range(1, NZ), key=lambda d: min(d, NZ - d), reverse=True)

    at_x = [x * (NYL * NZ)] + [lax.rem(x + d, NX) * (NYL * NZ) for d in range(1, NX)]
    at_yl = [yl * NZ, (1 - yl) * NZ]
    at_z = [z] + [lax.rem(z + d, NZ) for d in range(1, NZ)]
    at_high = [high * 2, (1 - high) * 2]
    at_core = [core, 1 - core]

    def plane_device(dx, fl, fh, fc):
        return at_high[fh] + at_core[fc], at_x[dx] + at_yl[fl] + z

    def z_device(dz):
        return c, m - z + at_z[dz]

    loads = [
        pltpu.make_async_copy(src, dst, local_sem.at[i])
        for i, (src, dst) in enumerate((
            (turb_hbm, turb_ref), (amp_hbm, amp_ref), (pix_hbm, pix_ref), (act_hbm, act_ref),
            (rows_hbm.at[:, pl.ds(pl.multiple_of(m * 8, 8), 8), :], rows_ref), (gt_hbm, gt_ref),
            (gx_hbm, gx_ref), (gy_hbm, gy_ref), (recon_hbm, recon_ref),
        ))
    ]
    for load in loads:
        load.start()
    barrier = pltpu.get_barrier_semaphore()
    for dz in column:
        pl.semaphore_signal(barrier, inc=1, device_id=z_device(dz), device_id_type=MESH)
    for d in plane:
        pl.semaphore_signal(barrier, inc=1, device_id=plane_device(*d), device_id_type=MESH)

    turb_load, amp_load, pix_load, act_load, rows_load, gt_load, gx_load, gy_load, recon_load = loads

    def send(src, dst, phase, device):
        pltpu.make_async_remote_copy(
            src_ref=src, dst_ref=dst, send_sem=send_sem.at[phase], recv_sem=recv_sem.at[phase],
            device_id=device, device_id_type=MESH,
        ).start()

    def await_all(ref, phase):
        pltpu.make_async_remote_copy(
            src_ref=ref, dst_ref=ref, send_sem=send_sem.at[phase], recv_sem=recv_sem.at[phase],
            device_id=z_device(1), device_id_type=MESH,
        ).wait_recv()

    def await_sent(ref, phase):
        pltpu.make_async_remote_copy(
            src_ref=ref, dst_ref=ref, send_sem=send_sem.at[phase], recv_sem=recv_sem.at[phase],
            device_id=z_device(1), device_id_type=MESH,
        ).wait_send()

    mod_a[xy] = jnp.full((1, 128), mod_ref[0], jnp.int32).astype(F32)

    def make_field(r, phase):
        cs, sn = sincos(phase)
        amp = amp_ref[r, :]
        er = (amp * cs).astype(BF16)
        ei = (amp * sn).astype(BF16)
        low = slice(r.start + PUPIL, r.stop + PUPIL)
        e_ref[r, 0:PUPIL] = er
        e_ref[r, PUPIL:] = ei
        e_ref[low, 0:PUPIL] = -ei
        e_ref[low, PUPIL:] = er

    turb_load.wait()
    amp_load.wait()
    for r0 in range(0, PUPIL, 32):
        r = slice(r0, r0 + 32)
        make_field(r, turb_ref[r, :])

    pl.semaphore_wait(barrier, len(plane) + NZ - 1)

    near = [d for d in plane if d[2] == 0 and d[3] == 0]
    for d in near:
        send(mod_a.at[xy], mod_a.at[xy], 0, plane_device(*d))

    lane = lax.broadcasted_iota(jnp.int32, (128, 128), 0)
    pix_load.wait()
    local = pix_ref[...] - m * (8 * NF)
    pix_r = lax.rem(local, 128)
    pix_q = lax.rem(lax.div(local, 128), 4) * 8 + lax.div(local, NF)
    for s in range(8):
        oh_sig[:, 128 * s:128 * s + 128] = jnp.where(lane == pix_r[s:s + 1, :], 1.0, 0.0).astype(BF16)
    act_load.wait()
    act = act_ref[...]
    act_r = lax.rem(act, 128)
    act_q = lax.div(act, 128)
    act_q = lax.rem(act_q, 5) * 8 + lax.div(act_q, 5)
    for s in range(40):
        oh_act[:, 128 * s:128 * s + 128] = jnp.where(lane == act_r[s:s + 1, :], 1.0, 0.0).astype(BF16)
    grid_ref[...] = jnp.zeros_like(grid_ref)

    gx_load.wait()
    gx_high, gx_low = halves(gx_ref[...].T)
    gx_wide[:, 0:AY] = gx_high
    gx_wide[:, AY:2 * AY] = gx_low
    gx_wide[:, 2 * AY:] = gx_high
    gy_load.wait()
    gy_high, gy_low = halves(gy_ref[...])
    gy_tall[...] = jnp.zeros_like(gy_tall)
    gy_tall[0:AX, :] = gy_high
    gy_tall[128:128 + AX, :] = gy_high
    gy_tall[256:256 + AX, :] = gy_low

    await_all(mod_a.at[pl.ds(0, len(near))], 0)
    for j in range(NX * NYL):
        mod_b[z, j:j + 1, :] = mod_a[j]
    for dz in column:
        send(mod_b.at[z], mod_b.at[z], 1, z_device(dz))
    recon_load.wait()
    for i in range(10):
        recon_t[:, 128 * i:128 * i + 128] = recon_ref[128 * i:128 * i + 128, :].T
    gt_load.wait()
    await_all(mod_b.at[pl.ds(0, NZ - 1)], 1)

    angle = (2.0 * math.pi / POINTS) * mod_b[...].reshape(64, 128)
    ca, sa = sincos(angle)
    centred = lax.broadcasted_iota(jnp.int32, (64, 128), 1).astype(F32)
    scale = 2.0 * math.pi * RADIUS / NF
    rows_load.wait()
    for h in range(2):
        pos = scale * (centred + (128.0 * h - PUPIL // 2))
        cols = slice(128 * h, 128 * h + 128)
        vr, vi = sincos(pos * sa)
        v_ref[0, :, cols] = vr
        v_ref[1, :, cols] = vi
        ur, ui = sincos(pos * ca)
        for i in range(8):
            mr = rows_ref[0, i:i + 1, cols]
            mi = rows_ref[1, i:i + 1, cols]
            l_ref[64 * i:64 * i + 64, cols] = (mr * ur - mi * ui).astype(BF16)
            l_ref[64 * i:64 * i + 64, 128 * h + PUPIL:128 * h + PUPIL + 128] = (mr * ui + mi * ur).astype(BF16)

    for step in range(STEPS):
        if step > 0:
            total = tot_ref[step - 1]
            stacked = jnp.concatenate([total[:, 128 * t:128 * t + 128] for t in range(5)], axis=0)
            picked = jnp.dot(stacked.astype(BF16), oh_act[...], preferred_element_type=F32)
            q_iota = lax.broadcasted_iota(jnp.int32, (40, 128), 0)
            for s in range(40):
                cols = slice(128 * s, 128 * s + 128)
                block = picked[:, cols]
                gat_ref[s:s + 1, :] = jnp.sum(jnp.where(q_iota == act_q[s:s + 1, :], block, 0.0), axis=0, keepdims=True)
            for y8 in range(8):
                s5, t = divmod(AX * y8, 128)
                first = gat_ref[pl.ds(s5, 8, stride=5), :]
                if t + AX <= 128:
                    row = first[:, t:t + AX]
                else:
                    second = gat_ref[pl.ds(s5 + 1, 8, stride=5), :]
                    row = jnp.concatenate([first[:, t:], second[:, :t + AX - 128]], axis=1)
                grid_ref[pl.ds(y8, 8, stride=8), :] = jnp.concatenate([row, jnp.zeros((8, 128 - AX), F32)], axis=1)
            grid_high, grid_low = halves(grid_ref[...])
            mapped = jnp.dot(
                jnp.concatenate([grid_high, grid_low, grid_high], axis=1), gy_tall[...], preferred_element_type=F32
            )
            mapped_high, mapped_low = halves(mapped)
            surface = jnp.dot(
                gx_wide[...], jnp.concatenate([mapped_high, mapped_high, mapped_low], axis=0),
                preferred_element_type=F32,
            )
            for r0 in range(0, PUPIL, 32):
                r = slice(r0, r0 + 32)
                make_field(r, turb_ref[r, :] - surface[r, :])

        x_ref[...] = jnp.dot(l_ref[...], e_ref[...], preferred_element_type=F32)
        for i in range(8):
            r = slice(64 * i, 64 * i + 64)
            xr = x_ref[r, 0:PUPIL]
            xi = x_ref[r, PUPIL:]
            vr = v_ref[0]
            vi = v_ref[1]
            tr = xr * vr - xi * vi
            ti = xr * vi + xi * vr
            x_ref[r, 0:PUPIL] = tr
            x_ref[r, PUPIL:] = ti
            t_ref[r, :] = tr.astype(BF16)
            t_ref[64 * i + 512:64 * i + 576, :] = ti.astype(BF16)
        y_ref[...] = jnp.dot(t_ref[...], gt_ref[...], preferred_element_type=F32)
        for i in range(8):
            for q in range(4):
                cols = slice(128 * q, 128 * q + 128)
                src = 128 * (1 - q % 2)
                r = slice(64 * i, 64 * i + 64)
                dr = x_ref[r, src:src + 128] - y_ref[64 * i + 512:64 * i + 576, cols]
                di = x_ref[r, src + PUPIL:src + PUPIL + 128] + y_ref[r, cols]
                fr_ref[i:i + 1, cols] = jnp.sum(dr * dr + di * di, axis=0, keepdims=True) * (1.0 / 256)
        frame = fr_ref[...]
        if step == STEPS - 1:
            frame_out[...] = frame

        tiles = jnp.concatenate([frame[:, 128 * q:128 * q + 128] for q in range(4)], axis=0).astype(BF16)
        found = jnp.dot(tiles, oh_sig[...], preferred_element_type=F32)
        s_iota = lax.broadcasted_iota(jnp.int32, (32, 128), 0)
        for s in range(8):
            cols = slice(128 * s, 128 * s + 128)
            sig_buf[step, c, :, cols] = jnp.sum(
                jnp.where(s_iota == pix_q[s:s + 1, :], found[:, cols], 0.0), axis=0, keepdims=True
            )
        base = 2 + 4 * step
        for fh, fc in ((1, 1), (1, 0)):
            send(sig_buf.at[step, c], sig_buf.at[step, c], base + 3, plane_device(0, 0, fh, fc))
        send(sig_buf.at[step, c], sig_buf.at[step, c], base, plane_device(0, 0, 0, 1))

        for far in range(2):
            await_all(sig_buf.at[step, pl.ds(0, 1 + far)], base + 3 * far)
            pair = [sig_buf[step, at_high[far] + k] for k in range(2)]
            part = jnp.dot(jnp.concatenate(pair, axis=0).astype(BF16), recon_t[...], preferred_element_type=F32)
            for k in range(2):
                rows = [part[k:k + 1, 640 * h:640 * h + 640] for h in range(2)]
                part_bf[step, at_high[far] + k] = jnp.concatenate(rows, axis=0).astype(BF16)
            if far == 0:
                plane_buf[step, xy * NCASE + c] = part_bf[step, c]
            for d in plane:
                if d[2] == far:
                    device = plane_device(*d)
                    send(part_bf.at[step, device[0]], plane_buf.at[step, xy * NCASE + c], base + 1, device)
        await_all(plane_buf.at[step, pl.ds(0, len(plane))], base + 1)
        for k in range(NCASE):
            acc = plane_buf[step, k].astype(F32)
            for j in range(1, NX * NYL):
                acc = acc + plane_buf[step, j * NCASE + k].astype(F32)
            tot_ref[step, 2 * k:2 * k + 2, :] = acc
        z_buf[step, z] = tot_ref[step].astype(BF16)
        for dz in column:
            send(z_buf.at[step, z], z_buf.at[step, z], base + 2, z_device(dz))
        await_all(z_buf.at[step, pl.ds(0, NZ - 1)], base + 2)
        acc = z_buf[step, 0].astype(F32)
        for j in range(1, NZ):
            acc = acc + z_buf[step, j].astype(F32)
        acc = LOOP_GAIN * acc
        if step > 0:
            acc = acc + tot_ref[step - 1]
        tot_ref[step] = acc
        if step == STEPS - 1:
            for t in range(5):
                cmd_out[pl.ds(t, 8, stride=5), :] = acc[:, 128 * t:128 * t + 128]

    await_sent(mod_a.at[pl.ds(0, len(near))], 0)
    await_sent(mod_b.at[pl.ds(0, NZ - 1)], 1)
    for step in range(STEPS):
        base = 2 + 4 * step
        await_sent(sig_buf.at[step, pl.ds(0, 1)], base)
        await_sent(sig_buf.at[step, pl.ds(0, 2)], base + 3)
        await_sent(plane_buf.at[step, pl.ds(0, len(plane))], base + 1)
        await_sent(z_buf.at[step, pl.ds(0, NZ - 1)], base + 2)


def body(turbulence, pupil_amp, mod_points, valid_pix, recon, gx, gy, act_map):
    rows, gt = sensor_tables()
    vmem = pl.BlockSpec(memory_space=pltpu.VMEM)
    hbm = pl.BlockSpec(memory_space=pltpu.HBM)
    command, frame = pl.pallas_call(
        kernel,
        out_shape=(pltpu.VMEM((40, 128), F32), pltpu.VMEM((8, NF), F32)),
        in_specs=[pl.BlockSpec(memory_space=pltpu.SMEM)] + [hbm] * 9,
        out_specs=(vmem, vmem),
        scratch_shapes=[
            pltpu.VMEM((PUPIL, PUPIL), F32),
            pltpu.VMEM((PUPIL, PUPIL), F32),
            pltpu.VMEM((8, 128), jnp.int32),
            pltpu.VMEM((40, 128), jnp.int32),
            pltpu.VMEM((AY, PUPIL), F32),
            pltpu.VMEM((AX, PUPIL), F32),
            pltpu.VMEM((PUPIL, NF), BF16),
            pltpu.VMEM((PUPIL, 3 * AY), BF16),
            pltpu.VMEM((384, PUPIL), BF16),
            pltpu.VMEM((1280, 1024), BF16),
            pltpu.VMEM((1024, 1280), BF16),
            pltpu.VMEM((2, 8, PUPIL), F32),
            pltpu.VMEM((8, 1, 128), F32),
            pltpu.VMEM((8, 8, 128), F32),
            pltpu.VMEM((2, 64, PUPIL), F32),
            pltpu.VMEM((512, 512), BF16),
            pltpu.VMEM((512, 512), BF16),
            pltpu.VMEM((512, 512), F32),
            pltpu.VMEM((1024, PUPIL), BF16),
            pltpu.VMEM((1024, NF), F32),
            pltpu.VMEM((128, 1024), BF16),
            pltpu.VMEM((128, 5120), BF16),
            pltpu.VMEM((8, NF), F32),
            pltpu.VMEM((STEPS, NCASE, 1, 1024), F32),
            pltpu.VMEM((STEPS, NCASE, 2, 640), BF16),
            pltpu.VMEM((STEPS, 32, 2, 640), BF16),
            pltpu.VMEM((STEPS, 8, 640), F32),
            pltpu.VMEM((STEPS, NZ, 8, 640), BF16),
            pltpu.VMEM((40, 128), F32),
            pltpu.VMEM((64, 128), F32),
            pltpu.SemaphoreType.DMA((9,)),
            pltpu.SemaphoreType.DMA((2 + 4 * STEPS,)),
            pltpu.SemaphoreType.DMA((2 + 4 * STEPS,)),
        ],
        compiler_params=pltpu.CompilerParams(
            collective_id=0, has_side_effects=True, vmem_limit_bytes=60 * 1024 * 1024
        ),
    )(
        mod_points, turbulence[0], pupil_amp, valid_pix.reshape(8, 128), act_map.reshape(40, 128), gx.T, gy.T,
        jnp.asarray(gt).astype(BF16), jnp.asarray(rows), recon,
    )
    return command.reshape(1, 5120), frame[None]


def solution(mesh):
    return jax.shard_map(
        body,
        mesh=mesh,
        in_specs=(P("case", None, None), P(), P("mod"), P("mod"), P("case", "mod"), P(), P(), P()),
        out_specs=(P("case", None), P("case", "mod", None)),
        check_vma=False,
    )
```

```python
import functools
import math

import jax
import jax.numpy as jnp
import numpy as np
from jax import lax
from jax.experimental import pallas as pl
from jax.experimental.pallas import tpu as pltpu
from jax.sharding import PartitionSpec as P

STEPS = 2
PUPIL = 256
NF = 512
AY = 64
AX = 80
LOOP_GAIN = 0.5
RADIUS = 6.0
POINTS = 256
NX, NYL, NZ = 4, 2, 8
NCASE = 4
MESH = pl.DeviceIdType.MESH
FIELD = 2 + 3 * STEPS
F32 = jnp.float32
BF16 = jnp.bfloat16


def sensor_tables():
    k = np.arange(NF) - NF // 2
    n = np.arange(PUPIL)
    p = np.arange(NF)
    w = np.exp(-2j * np.pi * np.outer(k, n) / NF) / np.sqrt(NF)
    v = np.exp(2j * np.pi * np.outer(p, k) / NF) / np.sqrt(NF)
    turn = np.array([1, 1j, -1, -1j])[np.abs(k) % 4]
    m = (v * turn) @ w
    rows = np.stack([m.real, m.imag]).astype(np.float32)
    return rows, 2.0 * m.imag.T.astype(np.float32)


def sincos(x):
    t = x * (0.5 / math.pi)
    f = t - jnp.floor(t + 0.5)
    g = f * f
    s = 0.10920575
    for a in (-0.8457636, 3.60628896, -7.30824115, 4.44288283):
        s = s * g + a
    s = s * f
    c = 0.31124104
    for a in (-1.88386521, 5.73951693, -6.97885475, 1.4142135623730951):
        c = c * g + a
    return 1.0 - s * s, s * c


def halves(x):
    high = x.astype(BF16)
    return high, (x - high.astype(F32)).astype(BF16)


def kernel(
    mod_ref, turb_hbm, amp_hbm, pix_hbm, act_hbm, gx_hbm, gy_hbm, gt_hbm, rows_hbm, recon_hbm,
    cmd_out, frame_out,
    turb_ref, amp_ref, pix_ref, act_ref, gx_ref, gy_ref, gt_ref, gx_wide, gy_tall,
    recon_ref, recon_t, rows_ref, mod_a, mod_b, v_ref, l_ref, e_ref, e_other, x_ref, t_ref, y_ref,
    oh_sig, oh_act, fr_ref, sig_buf, part_bf, plane_buf, tot_ref, z_buf, gat_ref, grid_ref,
    local_sem, send_sem, recv_sem,
):
    c = lax.axis_index("case")
    m = lax.axis_index("mod")
    z = lax.rem(m, NZ)
    xy = lax.div(m, NZ)
    yl = lax.rem(xy, NYL)
    x = lax.div(xy, NYL)

    high = lax.div(c, 2)
    core = lax.rem(c, 2)

    def hops(d):
        return min(d[0], NX - d[0]) + (2 if d[2] and not d[1] else 1 if d[1] else 0)

    plane = [(dx, fl, fh, fc) for dx in range(NX) for fl in range(2) for fh in range(2) for fc in range(2)]
    plane = sorted(plane[1:], key=hops, reverse=True)
    column = sorted(range(1, NZ), key=lambda d: min(d, NZ - d), reverse=True)

    at_x = [x * (NYL * NZ)] + [lax.rem(x + d, NX) * (NYL * NZ) for d in range(1, NX)]
    at_yl = [yl * NZ, (1 - yl) * NZ]
    at_z = [z] + [lax.rem(z + d, NZ) for d in range(1, NZ)]
    at_high = [high * 2, (1 - high) * 2]
    at_core = [core, 1 - core]

    def plane_device(dx, fl, fh, fc):
        return at_high[fh] + at_core[fc], at_x[dx] + at_yl[fl] + z

    def z_device(dz):
        return c, m - z + at_z[dz]

    loads = [
        pltpu.make_async_copy(src, dst, local_sem.at[i])
        for i, (src, dst) in enumerate((
            (turb_hbm, turb_ref), (amp_hbm, amp_ref), (pix_hbm, pix_ref), (act_hbm, act_ref),
            (rows_hbm.at[:, pl.ds(pl.multiple_of(m * 8, 8), 8), :], rows_ref), (gt_hbm, gt_ref),
            (gx_hbm, gx_ref), (gy_hbm, gy_ref), (recon_hbm, recon_ref),
        ))
    ]
    for load in loads:
        load.start()
    barrier = pltpu.get_barrier_semaphore()
    for dz in column:
        pl.semaphore_signal(barrier, inc=1, device_id=z_device(dz), device_id_type=MESH)
    for d in plane:
        pl.semaphore_signal(barrier, inc=1, device_id=plane_device(*d), device_id_type=MESH)

    turb_load, amp_load, pix_load, act_load, rows_load, gt_load, gx_load, gy_load, recon_load = loads

    def send(src, dst, phase, device):
        pltpu.make_async_remote_copy(
            src_ref=src, dst_ref=dst, send_sem=send_sem.at[phase], recv_sem=recv_sem.at[phase],
            device_id=device, device_id_type=MESH,
        ).start()

    def await_all(ref, phase):
        pltpu.make_async_remote_copy(
            src_ref=ref, dst_ref=ref, send_sem=send_sem.at[phase], recv_sem=recv_sem.at[phase],
            device_id=z_device(1), device_id_type=MESH,
        ).wait_recv()

    def await_sent(ref, phase):
        pltpu.make_async_remote_copy(
            src_ref=ref, dst_ref=ref, send_sem=send_sem.at[phase], recv_sem=recv_sem.at[phase],
            device_id=z_device(1), device_id_type=MESH,
        ).wait_send()

    mod_a[xy] = jnp.full((1, 128), mod_ref[0], jnp.int32).astype(F32)

    def make_field(r, phase):
        cs, sn = sincos(phase)
        amp = amp_ref[r, :]
        er = (amp * cs).astype(BF16)
        ei = (amp * sn).astype(BF16)
        low = slice(r.start + PUPIL, r.stop + PUPIL)
        e_ref[r, 0:PUPIL] = er
        e_ref[r, PUPIL:] = ei
        e_ref[low, 0:PUPIL] = -ei
        e_ref[low, PUPIL:] = er

    turb_load.wait()
    amp_load.wait()
    for r0 in range(0, PUPIL, 32):
        r = slice(r0, r0 + 32)
        make_field(r, turb_ref[r, :])

    pl.semaphore_wait(barrier, len(plane) + NZ - 1)

    near = [d for d in plane if d[2] == 0 and d[3] == 0]
    for d in near:
        send(mod_a.at[xy], mod_a.at[xy], 0, plane_device(*d))
    send(e_ref.at[pl.ds(0, PUPIL)], e_other.at[pl.ds(0, PUPIL)], FIELD, plane_device(0, 1, 1, 0))

    lane = lax.broadcasted_iota(jnp.int32, (128, 128), 0)
    pix_load.wait()
    local = pix_ref[...] - m * (8 * NF)
    pix_r = lax.rem(local, 128)
    pix_q = lax.rem(lax.div(local, 128), 4) * 8 + lax.div(local, NF)
    for s in range(8):
        oh_sig[:, 128 * s:128 * s + 128] = jnp.where(lane == pix_r[s:s + 1, :], 1.0, 0.0).astype(BF16)
    act_load.wait()
    act = act_ref[...]
    act_r = lax.rem(act, 128)
    act_q = lax.div(act, 128)
    act_q = lax.rem(act_q, 5) * 8 + lax.div(act_q, 5)
    for s in range(40):
        oh_act[:, 128 * s:128 * s + 128] = jnp.where(lane == act_r[s:s + 1, :], 1.0, 0.0).astype(BF16)
    grid_ref[...] = jnp.zeros_like(grid_ref)

    gx_load.wait()
    gx_high, gx_low = halves(gx_ref[...].T)
    gx_wide[:, 0:AY] = gx_high
    gx_wide[:, AY:2 * AY] = gx_low
    gx_wide[:, 2 * AY:] = gx_high
    gy_load.wait()
    gy_high, gy_low = halves(gy_ref[...])
    gy_tall[...] = jnp.zeros_like(gy_tall)
    gy_tall[0:AX, :] = gy_high
    gy_tall[128:128 + AX, :] = gy_high
    gy_tall[256:256 + AX, :] = gy_low

    await_all(mod_a.at[pl.ds(0, len(near))], 0)
    for j in range(NX * NYL):
        mod_b[z, j:j + 1, :] = mod_a[j]
    for dz in column:
        send(mod_b.at[z], mod_b.at[z], 1, z_device(dz))
    recon_load.wait()
    for i in range(10):
        recon_t[:, 128 * i:128 * i + 128] = recon_ref[128 * i:128 * i + 128, :].T
    gt_load.wait()
    await_all(mod_b.at[pl.ds(0, NZ - 1)], 1)

    angle = (2.0 * math.pi / POINTS) * mod_b[...].reshape(64, 128)
    ca, sa = sincos(angle)
    centred = lax.broadcasted_iota(jnp.int32, (64, 128), 1).astype(F32)
    scale = 2.0 * math.pi * RADIUS / NF
    rows_load.wait()
    for h in range(2):
        pos = scale * (centred + (128.0 * h - PUPIL // 2))
        cols = slice(128 * h, 128 * h + 128)
        vr, vi = sincos(pos * sa)
        v_ref[0, :, cols] = vr
        v_ref[1, :, cols] = vi
        ur, ui = sincos(pos * ca)
        for i in range(8):
            mr = rows_ref[0, i:i + 1, cols]
            mi = rows_ref[1, i:i + 1, cols]
            l_ref[64 * i:64 * i + 64, cols] = (mr * ur - mi * ui).astype(BF16)
            l_ref[64 * i:64 * i + 64, 128 * h + PUPIL:128 * h + PUPIL + 128] = (mr * ui + mi * ur).astype(BF16)

    def compute_frame(field):
        x_ref[...] = jnp.dot(l_ref[...], field[...], preferred_element_type=F32)
        for i in range(8):
            r = slice(64 * i, 64 * i + 64)
            xr = x_ref[r, 0:PUPIL]
            xi = x_ref[r, PUPIL:]
            vr = v_ref[0]
            vi = v_ref[1]
            tr = xr * vr - xi * vi
            ti = xr * vi + xi * vr
            x_ref[r, 0:PUPIL] = tr
            x_ref[r, PUPIL:] = ti
            t_ref[r, :] = tr.astype(BF16)
            t_ref[64 * i + 512:64 * i + 576, :] = ti.astype(BF16)
        y_ref[...] = jnp.dot(t_ref[...], gt_ref[...], preferred_element_type=F32)
        for i in range(8):
            for q in range(4):
                cols = slice(128 * q, 128 * q + 128)
                src = 128 * (1 - q % 2)
                r = slice(64 * i, 64 * i + 64)
                dr = x_ref[r, src:src + 128] - y_ref[64 * i + 512:64 * i + 576, cols]
                di = x_ref[r, src + PUPIL:src + PUPIL + 128] + y_ref[r, cols]
                fr_ref[i:i + 1, cols] = jnp.sum(dr * dr + di * di, axis=0, keepdims=True) * (1.0 / 256)
        return fr_ref[...]

    def select_signals(frame, slot):
        tiles = jnp.concatenate([frame[:, 128 * q:128 * q + 128] for q in range(4)], axis=0).astype(BF16)
        found = jnp.dot(tiles, oh_sig[...], preferred_element_type=F32)
        s_iota = lax.broadcasted_iota(jnp.int32, (32, 128), 0)
        for s in range(8):
            cols = slice(128 * s, 128 * s + 128)
            slot[:, cols] = jnp.sum(
                jnp.where(s_iota == pix_q[s:s + 1, :], found[:, cols], 0.0), axis=0, keepdims=True
            )

    for step in range(STEPS):
        if step > 0:
            total = tot_ref[step - 1]
            if step == 1:
                await_sent(e_ref.at[pl.ds(0, PUPIL)], FIELD)
            stacked = jnp.concatenate([total[:, 128 * t:128 * t + 128] for t in range(5)], axis=0)
            picked = jnp.dot(stacked.astype(BF16), oh_act[...], preferred_element_type=F32)
            q_iota = lax.broadcasted_iota(jnp.int32, (40, 128), 0)
            for s in range(40):
                cols = slice(128 * s, 128 * s + 128)
                block = picked[:, cols]
                gat_ref[s:s + 1, :] = jnp.sum(jnp.where(q_iota == act_q[s:s + 1, :], block, 0.0), axis=0, keepdims=True)
            for y8 in range(8):
                s5, t = divmod(AX * y8, 128)
                first = gat_ref[pl.ds(s5, 8, stride=5), :]
                if t + AX <= 128:
                    row = first[:, t:t + AX]
                else:
                    second = gat_ref[pl.ds(s5 + 1, 8, stride=5), :]
                    row = jnp.concatenate([first[:, t:], second[:, :t + AX - 128]], axis=1)
                grid_ref[pl.ds(y8, 8, stride=8), :] = jnp.concatenate([row, jnp.zeros((8, 128 - AX), F32)], axis=1)
            grid_high, grid_low = halves(grid_ref[...])
            mapped = jnp.dot(
                jnp.concatenate([grid_high, grid_low, grid_high], axis=1), gy_tall[...], preferred_element_type=F32
            )
            mapped_high, mapped_low = halves(mapped)
            surface = jnp.dot(
                gx_wide[...], jnp.concatenate([mapped_high, mapped_high, mapped_low], axis=0),
                preferred_element_type=F32,
            )
            for r0 in range(0, PUPIL, 32):
                r = slice(r0, r0 + 32)
                make_field(r, turb_ref[r, :] - surface[r, :])

        frame = compute_frame(e_ref)
        if step == STEPS - 1:
            frame_out[...] = frame

        select_signals(frame, sig_buf.at[step, c])
        base = 2 + 3 * step
        if step == 0:
            other = at_high[1] + core
            send(sig_buf.at[step, c], sig_buf.at[step, c], base, plane_device(0, 0, 0, 1))
            await_all(e_other.at[pl.ds(0, PUPIL)], FIELD)
            e_other[PUPIL:, 0:PUPIL] = -e_other[0:PUPIL, PUPIL:]
            e_other[PUPIL:, PUPIL:] = e_other[0:PUPIL, 0:PUPIL]
            select_signals(compute_frame(e_other), sig_buf.at[step, other])
            send(sig_buf.at[step, other], sig_buf.at[step, other], base, plane_device(0, 0, 0, 1))
            await_all(sig_buf.at[step, pl.ds(0, 2)], base)
        else:
            for fh, fc in ((1, 1), (1, 0), (0, 1)):
                send(sig_buf.at[step, c], sig_buf.at[step, c], base, plane_device(0, 0, fh, fc))
            await_all(sig_buf.at[step, pl.ds(0, 3)], base)
        signals = jnp.concatenate([sig_buf[step, k] for k in range(NCASE)], axis=0).astype(BF16)
        part = jnp.dot(signals, recon_t[...], preferred_element_type=F32)
        for k in range(NCASE):
            rows = [part[k:k + 1, 640 * h:640 * h + 640] for h in range(2)]
            part_bf[step, k] = jnp.concatenate(rows, axis=0).astype(BF16)
        plane_buf[step, xy * NCASE + c] = part_bf[step, c]
        for d in plane:
            device = plane_device(*d)
            send(part_bf.at[step, device[0]], plane_buf.at[step, xy * NCASE + c], base + 1, device)
        await_all(plane_buf.at[step, pl.ds(0, len(plane))], base + 1)
        for k in range(NCASE):
            acc = plane_buf[step, k].astype(F32)
            for j in range(1, NX * NYL):
                acc = acc + plane_buf[step, j * NCASE + k].astype(F32)
            tot_ref[step, 2 * k:2 * k + 2, :] = acc
        z_buf[step, z] = tot_ref[step].astype(BF16)
        for dz in column:
            send(z_buf.at[step, z], z_buf.at[step, z], base + 2, z_device(dz))
        await_all(z_buf.at[step, pl.ds(0, NZ - 1)], base + 2)
        acc = z_buf[step, 0].astype(F32)
        for j in range(1, NZ):
            acc = acc + z_buf[step, j].astype(F32)
        acc = LOOP_GAIN * acc
        if step > 0:
            acc = acc + tot_ref[step - 1]
        tot_ref[step] = acc
        if step == STEPS - 1:
            for t in range(5):
                cmd_out[pl.ds(t, 8, stride=5), :] = acc[:, 128 * t:128 * t + 128]

    await_sent(mod_a.at[pl.ds(0, len(near))], 0)
    await_sent(mod_b.at[pl.ds(0, NZ - 1)], 1)
    for step in range(STEPS):
        base = 2 + 3 * step
        await_sent(sig_buf.at[step, pl.ds(0, 2 + step)], base)
        await_sent(plane_buf.at[step, pl.ds(0, len(plane))], base + 1)
        await_sent(z_buf.at[step, pl.ds(0, NZ - 1)], base + 2)


def body(turbulence, pupil_amp, mod_points, valid_pix, recon, gx, gy, act_map):
    rows, gt = sensor_tables()
    vmem = pl.BlockSpec(memory_space=pltpu.VMEM)
    hbm = pl.BlockSpec(memory_space=pltpu.HBM)
    command, frame = pl.pallas_call(
        kernel,
        out_shape=(pltpu.VMEM((40, 128), F32), pltpu.VMEM((8, NF), F32)),
        in_specs=[pl.BlockSpec(memory_space=pltpu.SMEM)] + [hbm] * 9,
        out_specs=(vmem, vmem),
        scratch_shapes=[
            pltpu.VMEM((PUPIL, PUPIL), F32),
            pltpu.VMEM((PUPIL, PUPIL), F32),
            pltpu.VMEM((8, 128), jnp.int32),
            pltpu.VMEM((40, 128), jnp.int32),
            pltpu.VMEM((AY, PUPIL), F32),
            pltpu.VMEM((AX, PUPIL), F32),
            pltpu.VMEM((PUPIL, NF), BF16),
            pltpu.VMEM((PUPIL, 3 * AY), BF16),
            pltpu.VMEM((384, PUPIL), BF16),
            pltpu.VMEM((1280, 1024), BF16),
            pltpu.VMEM((1024, 1280), BF16),
            pltpu.VMEM((2, 8, PUPIL), F32),
            pltpu.VMEM((8, 1, 128), F32),
            pltpu.VMEM((8, 8, 128), F32),
            pltpu.VMEM((2, 64, PUPIL), F32),
            pltpu.VMEM((512, 512), BF16),
            pltpu.VMEM((512, 512), BF16),
            pltpu.VMEM((512, 512), BF16),
            pltpu.VMEM((512, 512), F32),
            pltpu.VMEM((1024, PUPIL), BF16),
            pltpu.VMEM((1024, NF), F32),
            pltpu.VMEM((128, 1024), BF16),
            pltpu.VMEM((128, 5120), BF16),
            pltpu.VMEM((8, NF), F32),
            pltpu.VMEM((STEPS, NCASE, 1, 1024), F32),
            pltpu.VMEM((STEPS, NCASE, 2, 640), BF16),
            pltpu.VMEM((STEPS, 32, 2, 640), BF16),
            pltpu.VMEM((STEPS, 8, 640), F32),
            pltpu.VMEM((STEPS, NZ, 8, 640), BF16),
            pltpu.VMEM((40, 128), F32),
            pltpu.VMEM((64, 128), F32),
            pltpu.SemaphoreType.DMA((9,)),
            pltpu.SemaphoreType.DMA((3 + 3 * STEPS,)),
            pltpu.SemaphoreType.DMA((3 + 3 * STEPS,)),
        ],
        compiler_params=pltpu.CompilerParams(
            collective_id=0, has_side_effects=True, vmem_limit_bytes=60 * 1024 * 1024
        ),
    )(
        mod_points, turbulence[0], pupil_amp, valid_pix.reshape(8, 128), act_map.reshape(40, 128), gx.T, gy.T,
        jnp.asarray(gt).astype(BF16), jnp.asarray(rows), recon,
    )
    return command.reshape(1, 5120), frame[None]


def solution(mesh):
    return jax.shard_map(
        body,
        mesh=mesh,
        in_specs=(P("case", None, None), P(), P("mod"), P("mod"), P("case", "mod"), P(), P(), P()),
        out_specs=(P("case", None), P("case", "mod", None)),
        check_vma=False,
    )
```

```python
import functools
import math

import jax
import jax.numpy as jnp
import numpy as np
from jax import lax
from jax.experimental import pallas as pl
from jax.experimental.pallas import tpu as pltpu
from jax.sharding import PartitionSpec as P

STEPS = 2
PUPIL = 256
NF = 512
AY = 64
AX = 80
LOOP_GAIN = 0.5
RADIUS = 6.0
POINTS = 256
NX, NYL, NZ = 4, 2, 8
NCASE = 4
MESH = pl.DeviceIdType.MESH
FIELD, PIXELS, FRAME = 2 + 3 * STEPS, 3 + 3 * STEPS, 4 + 3 * STEPS
F32 = jnp.float32
BF16 = jnp.bfloat16


def sensor_tables():
    k = np.arange(NF) - NF // 2
    n = np.arange(PUPIL)
    p = np.arange(NF)
    w = np.exp(-2j * np.pi * np.outer(k, n) / NF) / np.sqrt(NF)
    v = np.exp(2j * np.pi * np.outer(p, k) / NF) / np.sqrt(NF)
    turn = np.array([1, 1j, -1, -1j])[np.abs(k) % 4]
    m = (v * turn) @ w
    rows = np.stack([m.real, m.imag]).astype(np.float32)
    return rows, 2.0 * m.imag.T.astype(np.float32)


def sincos(x):
    t = x * (0.5 / math.pi)
    f = t - jnp.floor(t + 0.5)
    g = f * f
    s = 0.10920575
    for a in (-0.8457636, 3.60628896, -7.30824115, 4.44288283):
        s = s * g + a
    s = s * f
    c = 0.31124104
    for a in (-1.88386521, 5.73951693, -6.97885475, 1.4142135623730951):
        c = c * g + a
    return 1.0 - s * s, s * c


def halves(x):
    high = x.astype(BF16)
    return high, (x - high.astype(F32)).astype(BF16)


def kernel(
    mod_ref, turb_hbm, amp_hbm, pix_hbm, act_hbm, gx_hbm, gy_hbm, gt_hbm, rows_hbm, recon_hbm,
    cmd_out, frame_out,
    turb_ref, amp_ref, pix_ref, act_ref, gx_ref, gy_ref, gt_ref, gx_wide, gy_tall,
    recon_ref, recon_t, rows_ref, near_rows_ref, near_pix, frame_in, sig_out, u_ref, mod_a, mod_b, v_ref, l_ref, e_ref, e_other, x_ref, t_ref, y_ref,
    oh_sig, oh_act, fr_ref, sig_buf, part_bf, plane_buf, tot_ref, z_buf, gat_ref, grid_ref,
    local_sem, send_sem, recv_sem,
):
    c = lax.axis_index("case")
    m = lax.axis_index("mod")
    z = lax.rem(m, NZ)
    xy = lax.div(m, NZ)
    yl = lax.rem(xy, NYL)
    x = lax.div(xy, NYL)

    near_m = m + (1 - 2 * yl) * NZ
    high = lax.div(c, 2)
    core = lax.rem(c, 2)

    def hops(d):
        return min(d[0], NX - d[0]) + (2 if d[2] and not d[1] else 1 if d[1] else 0)

    plane = [(dx, fl, fh, fc) for dx in range(NX) for fl in range(2) for fh in range(2) for fc in range(2)]
    plane = sorted(plane[1:], key=hops, reverse=True)
    column = sorted(range(1, NZ), key=lambda d: min(d, NZ - d), reverse=True)

    at_x = [x * (NYL * NZ)] + [lax.rem(x + d, NX) * (NYL * NZ) for d in range(1, NX)]
    at_yl = [yl * NZ, (1 - yl) * NZ]
    at_z = [z] + [lax.rem(z + d, NZ) for d in range(1, NZ)]
    at_high = [high * 2, (1 - high) * 2]
    at_core = [core, 1 - core]

    def plane_device(dx, fl, fh, fc):
        return at_high[fh] + at_core[fc], at_x[dx] + at_yl[fl] + z

    def z_device(dz):
        return c, m - z + at_z[dz]

    loads = [
        pltpu.make_async_copy(src, dst, local_sem.at[i])
        for i, (src, dst) in enumerate((
            (turb_hbm, turb_ref), (amp_hbm, amp_ref), (pix_hbm, pix_ref), (act_hbm, act_ref),
            (rows_hbm.at[:, pl.ds(pl.multiple_of(m * 8, 8), 8), :], rows_ref), (gt_hbm, gt_ref),
            (gx_hbm, gx_ref), (gy_hbm, gy_ref), (recon_hbm, recon_ref),
            (rows_hbm.at[:, pl.ds(pl.multiple_of(near_m * 8, 8), 8), :], near_rows_ref),
        ))
    ]
    for load in loads:
        load.start()
    barrier = pltpu.get_barrier_semaphore()
    for dz in column:
        pl.semaphore_signal(barrier, inc=1, device_id=z_device(dz), device_id_type=MESH)
    for d in plane:
        pl.semaphore_signal(barrier, inc=1, device_id=plane_device(*d), device_id_type=MESH)

    turb_load, amp_load, pix_load, act_load, rows_load, gt_load, gx_load, gy_load, recon_load, near_rows_load = loads

    def send(src, dst, phase, device):
        pltpu.make_async_remote_copy(
            src_ref=src, dst_ref=dst, send_sem=send_sem.at[phase], recv_sem=recv_sem.at[phase],
            device_id=device, device_id_type=MESH,
        ).start()

    def await_all(ref, phase):
        pltpu.make_async_remote_copy(
            src_ref=ref, dst_ref=ref, send_sem=send_sem.at[phase], recv_sem=recv_sem.at[phase],
            device_id=z_device(1), device_id_type=MESH,
        ).wait_recv()

    def await_sent(ref, phase):
        pltpu.make_async_remote_copy(
            src_ref=ref, dst_ref=ref, send_sem=send_sem.at[phase], recv_sem=recv_sem.at[phase],
            device_id=z_device(1), device_id_type=MESH,
        ).wait_send()

    mod_a[xy] = jnp.full((1, 128), mod_ref[0], jnp.int32).astype(F32)

    def make_field(r, phase):
        cs, sn = sincos(phase)
        amp = amp_ref[r, :]
        er = (amp * cs).astype(BF16)
        ei = (amp * sn).astype(BF16)
        low = slice(r.start + PUPIL, r.stop + PUPIL)
        e_ref[r, 0:PUPIL] = er
        e_ref[r, PUPIL:] = ei
        e_ref[low, 0:PUPIL] = -ei
        e_ref[low, PUPIL:] = er

    turb_load.wait()
    amp_load.wait()
    for r0 in range(0, PUPIL, 32):
        r = slice(r0, r0 + 32)
        make_field(r, turb_ref[r, :])

    pl.semaphore_wait(barrier, len(plane) + NZ - 1)

    near = [d for d in plane if d[2] == 0 and d[3] == 0]
    for d in near:
        send(mod_a.at[xy], mod_a.at[xy], 0, plane_device(*d))
    send(e_ref.at[pl.ds(0, PUPIL)], e_other.at[pl.ds(0, PUPIL)], FIELD, plane_device(0, 1, 1, 0))

    lane = lax.broadcasted_iota(jnp.int32, (128, 128), 0)
    pix_load.wait()
    send(pix_ref, near_pix, PIXELS, plane_device(0, 1, 0, 0))

    def pixel_table(pixels, block):
        local = pixels - block * (8 * NF)
        pix_r = lax.rem(local, 128)
        for s in range(8):
            oh_sig[:, 128 * s:128 * s + 128] = jnp.where(lane == pix_r[s:s + 1, :], 1.0, 0.0).astype(BF16)
        return lax.rem(lax.div(local, 128), 4) * 8 + lax.div(local, NF)

    pix_q = pixel_table(pix_ref[...], m)
    act_load.wait()
    act = act_ref[...]
    act_r = lax.rem(act, 128)
    act_q = lax.div(act, 128)
    act_q = lax.rem(act_q, 5) * 8 + lax.div(act_q, 5)
    for s in range(40):
        oh_act[:, 128 * s:128 * s + 128] = jnp.where(lane == act_r[s:s + 1, :], 1.0, 0.0).astype(BF16)
    grid_ref[...] = jnp.zeros_like(grid_ref)

    gx_load.wait()
    gx_high, gx_low = halves(gx_ref[...].T)
    gx_wide[:, 0:AY] = gx_high
    gx_wide[:, AY:2 * AY] = gx_low
    gx_wide[:, 2 * AY:] = gx_high
    gy_load.wait()
    gy_high, gy_low = halves(gy_ref[...])
    gy_tall[...] = jnp.zeros_like(gy_tall)
    gy_tall[0:AX, :] = gy_high
    gy_tall[128:128 + AX, :] = gy_high
    gy_tall[256:256 + AX, :] = gy_low

    await_all(mod_a.at[pl.ds(0, len(near))], 0)
    for j in range(NX * NYL):
        mod_b[z, j:j + 1, :] = mod_a[j]
    for dz in column:
        send(mod_b.at[z], mod_b.at[z], 1, z_device(dz))
    recon_load.wait()
    for i in range(10):
        recon_t[:, 128 * i:128 * i + 128] = recon_ref[128 * i:128 * i + 128, :].T
    gt_load.wait()
    await_all(mod_b.at[pl.ds(0, NZ - 1)], 1)

    angle = (2.0 * math.pi / POINTS) * mod_b[...].reshape(64, 128)
    ca, sa = sincos(angle)
    centred = lax.broadcasted_iota(jnp.int32, (64, 128), 1).astype(F32)
    scale = 2.0 * math.pi * RADIUS / NF
    for h in range(2):
        pos = scale * (centred + (128.0 * h - PUPIL // 2))
        cols = slice(128 * h, 128 * h + 128)
        vr, vi = sincos(pos * sa)
        v_ref[0, :, cols] = vr
        v_ref[1, :, cols] = vi
        ur, ui = sincos(pos * ca)
        u_ref[0, :, cols] = ur
        u_ref[1, :, cols] = ui

    def left_factor(table):
        for h in range(2):
            cols = slice(128 * h, 128 * h + 128)
            ur = u_ref[0, :, cols]
            ui = u_ref[1, :, cols]
            for i in range(8):
                mr = table[0, i:i + 1, cols]
                mi = table[1, i:i + 1, cols]
                r = slice(64 * i, 64 * i + 64)
                l_ref[r, cols] = (mr * ur - mi * ui).astype(BF16)
                l_ref[r, 128 * h + PUPIL:128 * h + PUPIL + 128] = (mr * ui + mi * ur).astype(BF16)

    rows_load.wait()
    left_factor(rows_ref)

    def compute_frame(field):
        x_ref[...] = jnp.dot(l_ref[...], field[...], preferred_element_type=F32)
        for i in range(8):
            r = slice(64 * i, 64 * i + 64)
            xr = x_ref[r, 0:PUPIL]
            xi = x_ref[r, PUPIL:]
            vr = v_ref[0]
            vi = v_ref[1]
            tr = xr * vr - xi * vi
            ti = xr * vi + xi * vr
            x_ref[r, 0:PUPIL] = tr
            x_ref[r, PUPIL:] = ti
            t_ref[r, :] = tr.astype(BF16)
            t_ref[64 * i + 512:64 * i + 576, :] = ti.astype(BF16)
        y_ref[...] = jnp.dot(t_ref[...], gt_ref[...], preferred_element_type=F32)
        for i in range(8):
            for q in range(4):
                cols = slice(128 * q, 128 * q + 128)
                src = 128 * (1 - q % 2)
                r = slice(64 * i, 64 * i + 64)
                dr = x_ref[r, src:src + 128] - y_ref[64 * i + 512:64 * i + 576, cols]
                di = x_ref[r, src + PUPIL:src + PUPIL + 128] + y_ref[r, cols]
                fr_ref[i:i + 1, cols] = jnp.sum(dr * dr + di * di, axis=0, keepdims=True) * (1.0 / 256)
        return fr_ref[...]

    def select_signals(frame, pix_q, slot):
        tiles = jnp.concatenate([frame[:, 128 * q:128 * q + 128] for q in range(4)], axis=0).astype(BF16)
        found = jnp.dot(tiles, oh_sig[...], preferred_element_type=F32)
        s_iota = lax.broadcasted_iota(jnp.int32, (32, 128), 0)
        for s in range(8):
            cols = slice(128 * s, 128 * s + 128)
            slot[:, cols] = jnp.sum(
                jnp.where(s_iota == pix_q[s:s + 1, :], found[:, cols], 0.0), axis=0, keepdims=True
            )

    for step in range(STEPS):
        if step > 0:
            total = tot_ref[step - 1]
            if step == 1:
                await_sent(e_ref.at[pl.ds(0, PUPIL)], FIELD)
            stacked = jnp.concatenate([total[:, 128 * t:128 * t + 128] for t in range(5)], axis=0)
            picked = jnp.dot(stacked.astype(BF16), oh_act[...], preferred_element_type=F32)
            q_iota = lax.broadcasted_iota(jnp.int32, (40, 128), 0)
            for s in range(40):
                cols = slice(128 * s, 128 * s + 128)
                block = picked[:, cols]
                gat_ref[s:s + 1, :] = jnp.sum(jnp.where(q_iota == act_q[s:s + 1, :], block, 0.0), axis=0, keepdims=True)
            for y8 in range(8):
                s5, t = divmod(AX * y8, 128)
                first = gat_ref[pl.ds(s5, 8, stride=5), :]
                if t + AX <= 128:
                    row = first[:, t:t + AX]
                else:
                    second = gat_ref[pl.ds(s5 + 1, 8, stride=5), :]
                    row = jnp.concatenate([first[:, t:], second[:, :t + AX - 128]], axis=1)
                grid_ref[pl.ds(y8, 8, stride=8), :] = jnp.concatenate([row, jnp.zeros((8, 128 - AX), F32)], axis=1)
            grid_high, grid_low = halves(grid_ref[...])
            mapped = jnp.dot(
                jnp.concatenate([grid_high, grid_low, grid_high], axis=1), gy_tall[...], preferred_element_type=F32
            )
            mapped_high, mapped_low = halves(mapped)
            surface = jnp.dot(
                gx_wide[...], jnp.concatenate([mapped_high, mapped_high, mapped_low], axis=0),
                preferred_element_type=F32,
            )
            for r0 in range(0, PUPIL, 32):
                r = slice(r0, r0 + 32)
                make_field(r, turb_ref[r, :] - surface[r, :])

        frame = compute_frame(e_ref)
        base = 2 + 3 * step
        if step == 0:
            select_signals(frame, pix_q, sig_buf.at[step, c])
            other = at_high[1] + core
            send(sig_buf.at[step, c], sig_buf.at[step, c], base, plane_device(0, 0, 0, 1))
            await_all(e_other.at[pl.ds(0, PUPIL)], FIELD)
            e_other[PUPIL:, 0:PUPIL] = -e_other[0:PUPIL, PUPIL:]
            e_other[PUPIL:, PUPIL:] = e_other[0:PUPIL, 0:PUPIL]
            select_signals(compute_frame(e_other), pix_q, sig_buf.at[step, other])
            send(sig_buf.at[step, other], sig_buf.at[step, other], base, plane_device(0, 0, 0, 1))
            await_all(sig_buf.at[step, pl.ds(0, 2)], base)
        else:
            select_signals(frame, pix_q, sig_out)
            for fh, fc in ((1, 1), (0, 1), (1, 0), (0, 0)):
                send(sig_out, sig_buf.at[step, c], base, plane_device(0, 1, fh, fc))
            send(fr_ref, frame_in, FRAME, plane_device(0, 1, 0, 0))
            await_all(sig_buf.at[step], base)
        signals = jnp.concatenate([sig_buf[step, k] for k in range(NCASE)], axis=0).astype(BF16)
        part = jnp.dot(signals, recon_t[...], preferred_element_type=F32)
        for k in range(NCASE):
            rows = [part[k:k + 1, 640 * h:640 * h + 640] for h in range(2)]
            part_bf[step, k] = jnp.concatenate(rows, axis=0).astype(BF16)
        plane_buf[step, xy * NCASE + c] = part_bf[step, c]
        for d in plane:
            device = plane_device(*d)
            send(part_bf.at[step, device[0]], plane_buf.at[step, xy * NCASE + c], base + 1, device)
        if step == 0:
            await_all(near_pix, PIXELS)
            pix_q = pixel_table(near_pix[...], near_m)
            near_rows_load.wait()
            left_factor(near_rows_ref)
        await_all(plane_buf.at[step, pl.ds(0, len(plane))], base + 1)
        for k in range(NCASE):
            acc = plane_buf[step, k].astype(F32)
            for j in range(1, NX * NYL):
                acc = acc + plane_buf[step, j * NCASE + k].astype(F32)
            tot_ref[step, 2 * k:2 * k + 2, :] = acc
        z_buf[step, z] = tot_ref[step].astype(BF16)
        for dz in column:
            send(z_buf.at[step, z], z_buf.at[step, z], base + 2, z_device(dz))
        await_all(z_buf.at[step, pl.ds(0, NZ - 1)], base + 2)
        acc = z_buf[step, 0].astype(F32)
        for j in range(1, NZ):
            acc = acc + z_buf[step, j].astype(F32)
        acc = LOOP_GAIN * acc
        if step > 0:
            acc = acc + tot_ref[step - 1]
        tot_ref[step] = acc
        if step == STEPS - 1:
            await_all(frame_in, FRAME)
            frame_out[...] = frame_in[...]
            for t in range(5):
                cmd_out[pl.ds(t, 8, stride=5), :] = acc[:, 128 * t:128 * t + 128]

    await_sent(pix_ref, PIXELS)
    await_sent(fr_ref, FRAME)
    await_sent(mod_a.at[pl.ds(0, len(near))], 0)
    await_sent(mod_b.at[pl.ds(0, NZ - 1)], 1)
    for step in range(STEPS):
        base = 2 + 3 * step
        await_sent(sig_buf.at[step, pl.ds(0, 2 + 2 * step)], base)
        await_sent(plane_buf.at[step, pl.ds(0, len(plane))], base + 1)
        await_sent(z_buf.at[step, pl.ds(0, NZ - 1)], base + 2)


def body(turbulence, pupil_amp, mod_points, valid_pix, recon, gx, gy, act_map):
    rows, gt = sensor_tables()
    vmem = pl.BlockSpec(memory_space=pltpu.VMEM)
    hbm = pl.BlockSpec(memory_space=pltpu.HBM)
    command, frame = pl.pallas_call(
        kernel,
        out_shape=(pltpu.VMEM((40, 128), F32), pltpu.VMEM((8, NF), F32)),
        in_specs=[pl.BlockSpec(memory_space=pltpu.SMEM)] + [hbm] * 9,
        out_specs=(vmem, vmem),
        scratch_shapes=[
            pltpu.VMEM((PUPIL, PUPIL), F32),
            pltpu.VMEM((PUPIL, PUPIL), F32),
            pltpu.VMEM((8, 128), jnp.int32),
            pltpu.VMEM((40, 128), jnp.int32),
            pltpu.VMEM((AY, PUPIL), F32),
            pltpu.VMEM((AX, PUPIL), F32),
            pltpu.VMEM((PUPIL, NF), BF16),
            pltpu.VMEM((PUPIL, 3 * AY), BF16),
            pltpu.VMEM((384, PUPIL), BF16),
            pltpu.VMEM((1280, 1024), BF16),
            pltpu.VMEM((1024, 1280), BF16),
            pltpu.VMEM((2, 8, PUPIL), F32),
            pltpu.VMEM((2, 8, PUPIL), F32),
            pltpu.VMEM((8, 128), jnp.int32),
            pltpu.VMEM((8, NF), F32),
            pltpu.VMEM((1, 1024), F32),
            pltpu.VMEM((2, 64, PUPIL), F32),
            pltpu.VMEM((8, 1, 128), F32),
            pltpu.VMEM((8, 8, 128), F32),
            pltpu.VMEM((2, 64, PUPIL), F32),
            pltpu.VMEM((512, 512), BF16),
            pltpu.VMEM((512, 512), BF16),
            pltpu.VMEM((512, 512), BF16),
            pltpu.VMEM((512, 512), F32),
            pltpu.VMEM((1024, PUPIL), BF16),
            pltpu.VMEM((1024, NF), F32),
            pltpu.VMEM((128, 1024), BF16),
            pltpu.VMEM((128, 5120), BF16),
            pltpu.VMEM((8, NF), F32),
            pltpu.VMEM((STEPS, NCASE, 1, 1024), F32),
            pltpu.VMEM((STEPS, NCASE, 2, 640), BF16),
            pltpu.VMEM((STEPS, 32, 2, 640), BF16),
            pltpu.VMEM((STEPS, 8, 640), F32),
            pltpu.VMEM((STEPS, NZ, 8, 640), BF16),
            pltpu.VMEM((40, 128), F32),
            pltpu.VMEM((64, 128), F32),
            pltpu.SemaphoreType.DMA((10,)),
            pltpu.SemaphoreType.DMA((5 + 3 * STEPS,)),
            pltpu.SemaphoreType.DMA((5 + 3 * STEPS,)),
        ],
        compiler_params=pltpu.CompilerParams(
            collective_id=0, has_side_effects=True, vmem_limit_bytes=60 * 1024 * 1024
        ),
    )(
        mod_points, turbulence[0], pupil_amp, valid_pix.reshape(8, 128), act_map.reshape(40, 128), gx.T, gy.T,
        jnp.asarray(gt).astype(BF16), jnp.asarray(rows), recon,
    )
    return command.reshape(1, 5120), frame[None]


def solution(mesh):
    return jax.shard_map(
        body,
        mesh=mesh,
        in_specs=(P("case", None, None), P(), P("mod"), P("mod"), P("case", "mod"), P(), P(), P()),
        out_specs=(P("case", None), P("case", "mod", None)),
        check_vma=False,
    )
```

```python
import functools
import math

import jax
import jax.numpy as jnp
import numpy as np
from jax import lax
from jax.experimental import pallas as pl
from jax.experimental.pallas import tpu as pltpu
from jax.sharding import PartitionSpec as P

STEPS = 2
PUPIL = 256
NF = 512
AY = 64
AX = 80
LOOP_GAIN = 0.5
RADIUS = 6.0
POINTS = 256
NX, NYL, NZ = 4, 2, 8
NCASE = 4
MESH = pl.DeviceIdType.MESH
FIELD, RECON = 2 + 3 * STEPS, 3 + 3 * STEPS
F32 = jnp.float32
BF16 = jnp.bfloat16


def sensor_tables():
    k = np.arange(NF) - NF // 2
    n = np.arange(PUPIL)
    p = np.arange(NF)
    w = np.exp(-2j * np.pi * np.outer(k, n) / NF) / np.sqrt(NF)
    v = np.exp(2j * np.pi * np.outer(p, k) / NF) / np.sqrt(NF)
    turn = np.array([1, 1j, -1, -1j])[np.abs(k) % 4]
    m = (v * turn) @ w
    rows = np.stack([m.real, m.imag]).astype(np.float32)
    return rows, 2.0 * m.imag.T.astype(np.float32)


def sincos(x):
    t = x * (0.5 / math.pi)
    f = t - jnp.floor(t + 0.5)
    g = f * f
    s = 0.10920575
    for a in (-0.8457636, 3.60628896, -7.30824115, 4.44288283):
        s = s * g + a
    s = s * f
    c = 0.31124104
    for a in (-1.88386521, 5.73951693, -6.97885475, 1.4142135623730951):
        c = c * g + a
    return 1.0 - s * s, s * c


def halves(x):
    high = x.astype(BF16)
    return high, (x - high.astype(F32)).astype(BF16)


def kernel(
    mod_ref, turb_hbm, amp_hbm, pix_hbm, act_hbm, gx_hbm, gy_hbm, gt_hbm, rows_hbm, recon_hbm,
    cmd_out, frame_out,
    turb_ref, amp_ref, pix_ref, act_ref, gx_ref, gy_ref, gt_ref, gx_wide, gy_tall,
    recon_ref, recon_t, rows_ref, mod_a, mod_b, v_ref, l_ref, e_ref, e_other, x_ref, t_ref, y_ref,
    oh_sig, oh_act, fr_ref, sig_buf, part_bf, plane_buf, tot_ref, z_buf, gat_ref, grid_ref,
    local_sem, send_sem, recv_sem,
):
    c = lax.axis_index("case")
    m = lax.axis_index("mod")
    z = lax.rem(m, NZ)
    xy = lax.div(m, NZ)
    yl = lax.rem(xy, NYL)
    x = lax.div(xy, NYL)

    high = lax.div(c, 2)
    core = lax.rem(c, 2)

    def hops(d):
        return min(d[0], NX - d[0]) + (2 if d[2] and not d[1] else 1 if d[1] else 0)

    plane = [(dx, fl, fh) for dx in range(NX) for fl in range(2) for fh in range(2)]
    plane = sorted(plane[1:], key=hops, reverse=True)
    column = sorted(range(1, NZ), key=lambda d: min(d, NZ - d), reverse=True)

    at_x = [x * (NYL * NZ)] + [lax.rem(x + d, NX) * (NYL * NZ) for d in range(1, NX)]
    at_yl = [yl * NZ, (1 - yl) * NZ]
    at_z = [z] + [lax.rem(z + d, NZ) for d in range(1, NZ)]
    at_high = [high, 1 - high]
    at_core = [core, 1 - core]

    def plane_device(dx, fl, fh):
        return at_high[fh] * 2 + core, at_x[dx] + at_yl[fl] + z

    sibling = (high * 2 + 1 - core, m)

    def z_device(dz):
        return c, m - z + at_z[dz]

    loads = [
        pltpu.make_async_copy(src, dst, local_sem.at[i])
        for i, (src, dst) in enumerate((
            (turb_hbm, turb_ref), (amp_hbm, amp_ref), (pix_hbm, pix_ref), (act_hbm, act_ref),
            (rows_hbm.at[:, pl.ds(pl.multiple_of(m * 8, 8), 8), :], rows_ref), (gt_hbm, gt_ref),
            (gx_hbm, gx_ref), (gy_hbm, gy_ref), (recon_hbm, recon_ref),
        ))
    ]
    for load in loads:
        load.start()
    barrier = pltpu.get_barrier_semaphore()
    for dz in column:
        pl.semaphore_signal(barrier, inc=1, device_id=z_device(dz), device_id_type=MESH)
    pl.semaphore_signal(barrier, inc=1, device_id=sibling, device_id_type=MESH)
    for d in plane:
        pl.semaphore_signal(barrier, inc=1, device_id=plane_device(*d), device_id_type=MESH)

    turb_load, amp_load, pix_load, act_load, rows_load, gt_load, gx_load, gy_load, recon_load = loads

    def send(src, dst, phase, device):
        pltpu.make_async_remote_copy(
            src_ref=src, dst_ref=dst, send_sem=send_sem.at[phase], recv_sem=recv_sem.at[phase],
            device_id=device, device_id_type=MESH,
        ).start()

    def await_all(ref, phase):
        pltpu.make_async_remote_copy(
            src_ref=ref, dst_ref=ref, send_sem=send_sem.at[phase], recv_sem=recv_sem.at[phase],
            device_id=z_device(1), device_id_type=MESH,
        ).wait_recv()

    def await_sent(ref, phase):
        pltpu.make_async_remote_copy(
            src_ref=ref, dst_ref=ref, send_sem=send_sem.at[phase], recv_sem=recv_sem.at[phase],
            device_id=z_device(1), device_id_type=MESH,
        ).wait_send()

    mod_a[xy] = jnp.full((1, 128), mod_ref[0], jnp.int32).astype(F32)

    def make_field(r, phase):
        cs, sn = sincos(phase)
        amp = amp_ref[r, :]
        er = (amp * cs).astype(BF16)
        ei = (amp * sn).astype(BF16)
        low = slice(r.start + PUPIL, r.stop + PUPIL)
        e_ref[r, 0:PUPIL] = er
        e_ref[r, PUPIL:] = ei
        e_ref[low, 0:PUPIL] = -ei
        e_ref[low, PUPIL:] = er

    turb_load.wait()
    amp_load.wait()
    for r0 in range(0, PUPIL, 32):
        r = slice(r0, r0 + 32)
        make_field(r, turb_ref[r, :])

    pl.semaphore_wait(barrier, len(plane) + NZ)

    near = [d for d in plane if d[2] == 0]
    for d in near:
        send(mod_a.at[xy], mod_a.at[xy], 0, plane_device(*d))
    send(e_ref.at[pl.ds(0, PUPIL)], e_other.at[pl.ds(0, PUPIL)], FIELD, plane_device(0, 1, 1))

    recon_load.wait()
    for j in range(5):
        recon_t[0, j] = recon_ref[256 * j:256 * j + 256, :].T
        send(recon_t.at[0, j], recon_t.at[1, j], RECON, sibling)

    lane = lax.broadcasted_iota(jnp.int32, (128, 128), 0)
    pix_load.wait()
    local = pix_ref[...] - m * (8 * NF)
    pix_r = lax.rem(local, 128)
    pix_q = lax.rem(lax.div(local, 128), 4) * 8 + lax.div(local, NF)
    for s in range(8):
        oh_sig[:, 128 * s:128 * s + 128] = jnp.where(lane == pix_r[s:s + 1, :], 1.0, 0.0).astype(BF16)
    act_load.wait()
    act = act_ref[...]
    act_r = lax.rem(act, 128)
    act_q = lax.div(act, 128)
    act_q = lax.rem(act_q, 5) * 8 + lax.div(act_q, 5)
    for s in range(40):
        oh_act[:, 128 * s:128 * s + 128] = jnp.where(lane == act_r[s:s + 1, :], 1.0, 0.0).astype(BF16)
    grid_ref[...] = jnp.zeros_like(grid_ref)

    gx_load.wait()
    gx_high, gx_low = halves(gx_ref[...].T)
    gx_wide[:, 0:AY] = gx_high
    gx_wide[:, AY:2 * AY] = gx_low
    gx_wide[:, 2 * AY:] = gx_high
    gy_load.wait()
    gy_high, gy_low = halves(gy_ref[...])
    gy_tall[...] = jnp.zeros_like(gy_tall)
    gy_tall[0:AX, :] = gy_high
    gy_tall[128:128 + AX, :] = gy_high
    gy_tall[256:256 + AX, :] = gy_low

    await_all(mod_a.at[pl.ds(0, len(near))], 0)
    for j in range(NX * NYL):
        mod_b[z, j:j + 1, :] = mod_a[j]
    for dz in column:
        send(mod_b.at[z], mod_b.at[z], 1, z_device(dz))
    gt_load.wait()
    await_all(mod_b.at[pl.ds(0, NZ - 1)], 1)

    angle = (2.0 * math.pi / POINTS) * mod_b[...].reshape(64, 128)
    ca, sa = sincos(angle)
    centred = lax.broadcasted_iota(jnp.int32, (64, 128), 1).astype(F32)
    scale = 2.0 * math.pi * RADIUS / NF
    rows_load.wait()
    for h in range(2):
        pos = scale * (centred + (128.0 * h - PUPIL // 2))
        cols = slice(128 * h, 128 * h + 128)
        vr, vi = sincos(pos * sa)
        v_ref[0, :, cols] = vr
        v_ref[1, :, cols] = vi
        ur, ui = sincos(pos * ca)
        for i in range(8):
            mr = rows_ref[0, i:i + 1, cols]
            mi = rows_ref[1, i:i + 1, cols]
            l_ref[64 * i:64 * i + 64, cols] = (mr * ur - mi * ui).astype(BF16)
            l_ref[64 * i:64 * i + 64, 128 * h + PUPIL:128 * h + PUPIL + 128] = (mr * ui + mi * ur).astype(BF16)

    def compute_frame(field):
        x_ref[...] = jnp.dot(l_ref[...], field[...], preferred_element_type=F32)
        for i in range(8):
            r = slice(64 * i, 64 * i + 64)
            xr = x_ref[r, 0:PUPIL]
            xi = x_ref[r, PUPIL:]
            vr = v_ref[0]
            vi = v_ref[1]
            tr = xr * vr - xi * vi
            ti = xr * vi + xi * vr
            x_ref[r, 0:PUPIL] = tr
            x_ref[r, PUPIL:] = ti
            t_ref[r, :] = tr.astype(BF16)
            t_ref[64 * i + 512:64 * i + 576, :] = ti.astype(BF16)
        y_ref[...] = jnp.dot(t_ref[...], gt_ref[...], preferred_element_type=F32)
        for i in range(8):
            for q in range(4):
                cols = slice(128 * q, 128 * q + 128)
                src = 128 * (1 - q % 2)
                r = slice(64 * i, 64 * i + 64)
                dr = x_ref[r, src:src + 128] - y_ref[64 * i + 512:64 * i + 576, cols]
                di = x_ref[r, src + PUPIL:src + PUPIL + 128] + y_ref[r, cols]
                fr_ref[i:i + 1, cols] = jnp.sum(dr * dr + di * di, axis=0, keepdims=True) * (1.0 / 256)
        return fr_ref[...]

    def select_signals(frame, slot):
        tiles = jnp.concatenate([frame[:, 128 * q:128 * q + 128] for q in range(4)], axis=0).astype(BF16)
        found = jnp.dot(tiles, oh_sig[...], preferred_element_type=F32)
        s_iota = lax.broadcasted_iota(jnp.int32, (32, 128), 0)
        for s in range(8):
            cols = slice(128 * s, 128 * s + 128)
            slot[:, cols] = jnp.sum(
                jnp.where(s_iota == pix_q[s:s + 1, :], found[:, cols], 0.0), axis=0, keepdims=True
            )

    for step in range(STEPS):
        if step > 0:
            total = tot_ref[step - 1]
            if step == 1:
                await_sent(e_ref.at[pl.ds(0, PUPIL)], FIELD)
            stacked = jnp.concatenate([total[:, 128 * t:128 * t + 128] for t in range(5)], axis=0)
            picked = jnp.dot(stacked.astype(BF16), oh_act[...], preferred_element_type=F32)
            q_iota = lax.broadcasted_iota(jnp.int32, (40, 128), 0)
            for s in range(40):
                cols = slice(128 * s, 128 * s + 128)
                block = picked[:, cols]
                gat_ref[s:s + 1, :] = jnp.sum(jnp.where(q_iota == act_q[s:s + 1, :], block, 0.0), axis=0, keepdims=True)
            for y8 in range(8):
                s5, t = divmod(AX * y8, 128)
                first = gat_ref[pl.ds(s5, 8, stride=5), :]
                if t + AX <= 128:
                    row = first[:, t:t + AX]
                else:
                    second = gat_ref[pl.ds(s5 + 1, 8, stride=5), :]
                    row = jnp.concatenate([first[:, t:], second[:, :t + AX - 128]], axis=1)
                grid_ref[pl.ds(y8, 8, stride=8), :] = jnp.concatenate([row, jnp.zeros((8, 128 - AX), F32)], axis=1)
            grid_high, grid_low = halves(grid_ref[...])
            mapped = jnp.dot(
                jnp.concatenate([grid_high, grid_low, grid_high], axis=1), gy_tall[...], preferred_element_type=F32
            )
            mapped_high, mapped_low = halves(mapped)
            surface = jnp.dot(
                gx_wide[...], jnp.concatenate([mapped_high, mapped_high, mapped_low], axis=0),
                preferred_element_type=F32,
            )
            for r0 in range(0, PUPIL, 32):
                r = slice(r0, r0 + 32)
                make_field(r, turb_ref[r, :] - surface[r, :])

        frame = compute_frame(e_ref)
        if step == STEPS - 1:
            frame_out[...] = frame

        select_signals(frame, sig_buf.at[step, high])
        base = 2 + 3 * step
        if step == 0:
            await_all(e_other.at[pl.ds(0, PUPIL)], FIELD)
            e_other[PUPIL:, 0:PUPIL] = -e_other[0:PUPIL, PUPIL:]
            e_other[PUPIL:, PUPIL:] = e_other[0:PUPIL, 0:PUPIL]
            select_signals(compute_frame(e_other), sig_buf.at[step, at_high[1]])
            await_all(recon_t.at[1], RECON)
        else:
            send(sig_buf.at[step, high], sig_buf.at[step, high], base, plane_device(0, 0, 1))
            await_all(sig_buf.at[step, pl.ds(0, 1)], base)

        signals = jnp.concatenate([sig_buf[step, k] for k in range(2)], axis=0).astype(BF16)
        for b in range(2):
            part = jnp.concatenate(
                [jnp.dot(signals, recon_t[b, j], preferred_element_type=F32) for j in range(5)], axis=1
            )
            for k in range(2):
                rows = [part[k:k + 1, 640 * h:640 * h + 640] for h in range(2)]
                part_bf[step, k, at_core[b]] = jnp.concatenate(rows, axis=0).astype(BF16)
        plane_buf[step, xy * 2 + high] = part_bf[step, high]
        for d in plane:
            send(part_bf.at[step, at_high[d[2]]], plane_buf.at[step, xy * 2 + high], base + 1, plane_device(*d))
        await_all(plane_buf.at[step, pl.ds(0, len(plane))], base + 1)
        for k in range(NCASE):
            acc = plane_buf[step, k // 2, k % 2].astype(F32)
            for j in range(1, NX * NYL):
                acc = acc + plane_buf[step, j * 2 + k // 2, k % 2].astype(F32)
            tot_ref[step, 2 * k:2 * k + 2, :] = acc
        z_buf[step, z] = tot_ref[step].astype(BF16)
        for dz in column:
            send(z_buf.at[step, z], z_buf.at[step, z], base + 2, z_device(dz))
        await_all(z_buf.at[step, pl.ds(0, NZ - 1)], base + 2)
        acc = z_buf[step, 0].astype(F32)
        for j in range(1, NZ):
            acc = acc + z_buf[step, j].astype(F32)
        acc = LOOP_GAIN * acc
        if step > 0:
            acc = acc + tot_ref[step - 1]
        tot_ref[step] = acc
        if step == STEPS - 1:
            for t in range(5):
                cmd_out[pl.ds(t, 8, stride=5), :] = acc[:, 128 * t:128 * t + 128]

    await_sent(recon_t.at[0], RECON)
    await_sent(mod_a.at[pl.ds(0, len(near))], 0)
    await_sent(mod_b.at[pl.ds(0, NZ - 1)], 1)
    for step in range(STEPS):
        base = 2 + 3 * step
        if step > 0:
            await_sent(sig_buf.at[step, pl.ds(0, 1)], base)
        await_sent(plane_buf.at[step, pl.ds(0, len(plane))], base + 1)
        await_sent(z_buf.at[step, pl.ds(0, NZ - 1)], base + 2)


def body(turbulence, pupil_amp, mod_points, valid_pix, recon, gx, gy, act_map):
    rows, gt = sensor_tables()
    vmem = pl.BlockSpec(memory_space=pltpu.VMEM)
    hbm = pl.BlockSpec(memory_space=pltpu.HBM)
    command, frame = pl.pallas_call(
        kernel,
        out_shape=(pltpu.VMEM((40, 128), F32), pltpu.VMEM((8, NF), F32)),
        in_specs=[pl.BlockSpec(memory_space=pltpu.SMEM)] + [hbm] * 9,
        out_specs=(vmem, vmem),
        scratch_shapes=[
            pltpu.VMEM((PUPIL, PUPIL), F32),
            pltpu.VMEM((PUPIL, PUPIL), F32),
            pltpu.VMEM((8, 128), jnp.int32),
            pltpu.VMEM((40, 128), jnp.int32),
            pltpu.VMEM((AY, PUPIL), F32),
            pltpu.VMEM((AX, PUPIL), F32),
            pltpu.VMEM((PUPIL, NF), BF16),
            pltpu.VMEM((PUPIL, 3 * AY), BF16),
            pltpu.VMEM((384, PUPIL), BF16),
            pltpu.VMEM((1280, 1024), BF16),
            pltpu.VMEM((2, 5, 1024, 256), BF16),
            pltpu.VMEM((2, 8, PUPIL), F32),
            pltpu.VMEM((8, 1, 128), F32),
            pltpu.VMEM((8, 8, 128), F32),
            pltpu.VMEM((2, 64, PUPIL), F32),
            pltpu.VMEM((512, 512), BF16),
            pltpu.VMEM((512, 512), BF16),
            pltpu.VMEM((512, 512), BF16),
            pltpu.VMEM((512, 512), F32),
            pltpu.VMEM((1024, PUPIL), BF16),
            pltpu.VMEM((1024, NF), F32),
            pltpu.VMEM((128, 1024), BF16),
            pltpu.VMEM((128, 5120), BF16),
            pltpu.VMEM((8, NF), F32),
            pltpu.VMEM((STEPS, 2, 1, 1024), F32),
            pltpu.VMEM((STEPS, 2, 2, 2, 640), BF16),
            pltpu.VMEM((STEPS, 16, 2, 2, 640), BF16),
            pltpu.VMEM((STEPS, 8, 640), F32),
            pltpu.VMEM((STEPS, NZ, 8, 640), BF16),
            pltpu.VMEM((40, 128), F32),
            pltpu.VMEM((64, 128), F32),
            pltpu.SemaphoreType.DMA((9,)),
            pltpu.SemaphoreType.DMA((4 + 3 * STEPS,)),
            pltpu.SemaphoreType.DMA((4 + 3 * STEPS,)),
        ],
        compiler_params=pltpu.CompilerParams(
            collective_id=0, has_side_effects=True, vmem_limit_bytes=60 * 1024 * 1024
        ),
    )(
        mod_points, turbulence[0], pupil_amp, valid_pix.reshape(8, 128), act_map.reshape(40, 128), gx.T, gy.T,
        jnp.asarray(gt).astype(BF16), jnp.asarray(rows), recon,
    )
    return command.reshape(1, 5120), frame[None]


def solution(mesh):
    return jax.shard_map(
        body,
        mesh=mesh,
        in_specs=(P("case", None, None), P(), P("mod"), P("mod"), P("case", "mod"), P(), P(), P()),
        out_specs=(P("case", None), P("case", "mod", None)),
        check_vma=False,
    )
```

```python
import functools
import math

import jax
import jax.numpy as jnp
import numpy as np
from jax import lax
from jax.experimental import pallas as pl
from jax.experimental.pallas import tpu as pltpu
from jax.sharding import PartitionSpec as P

STEPS = 2
PUPIL = 256
NF = 512
AY = 64
AX = 80
LOOP_GAIN = 0.5
RADIUS = 6.0
POINTS = 256
NX, NYL, NZ = 4, 2, 8
NCASE = 4
MESH = pl.DeviceIdType.MESH
FIELD, RECON, LATE = 2 + 3 * STEPS, 3 + 3 * STEPS, 4 + 3 * STEPS
F32 = jnp.float32
BF16 = jnp.bfloat16


def sensor_tables():
    k = np.arange(NF) - NF // 2
    n = np.arange(PUPIL)
    p = np.arange(NF)
    w = np.exp(-2j * np.pi * np.outer(k, n) / NF) / np.sqrt(NF)
    v = np.exp(2j * np.pi * np.outer(p, k) / NF) / np.sqrt(NF)
    turn = np.array([1, 1j, -1, -1j])[np.abs(k) % 4]
    m = (v * turn) @ w
    rows = np.stack([m.real, m.imag]).astype(np.float32)
    return rows, 2.0 * m.imag.T.astype(np.float32)


def sincos(x):
    t = x * (0.5 / math.pi)
    f = t - jnp.floor(t + 0.5)
    g = f * f
    s = 0.10920575
    for a in (-0.8457636, 3.60628896, -7.30824115, 4.44288283):
        s = s * g + a
    s = s * f
    c = 0.31124104
    for a in (-1.88386521, 5.73951693, -6.97885475, 1.4142135623730951):
        c = c * g + a
    return 1.0 - s * s, s * c


def halves(x):
    high = x.astype(BF16)
    return high, (x - high.astype(F32)).astype(BF16)


def kernel(
    mod_ref, turb_hbm, amp_hbm, pix_hbm, act_hbm, gx_hbm, gy_hbm, gt_hbm, rows_hbm, recon_hbm,
    cmd_out, frame_out,
    turb_ref, amp_ref, pix_ref, act_ref, gx_ref, gy_ref, gt_ref, gx_wide, gy_tall,
    recon_ref, recon_t, rows_ref, mod_a, mod_b, v_ref, l_ref, e_ref, e_other, x_ref, t_ref, y_ref,
    oh_sig, oh_act, fr_ref, fr_other, sig_buf, part_bf, plane_buf, tot_ref, z_buf, gat_ref, grid_ref,
    local_sem, send_sem, recv_sem,
):
    c = lax.axis_index("case")
    m = lax.axis_index("mod")
    z = lax.rem(m, NZ)
    xy = lax.div(m, NZ)
    yl = lax.rem(xy, NYL)
    x = lax.div(xy, NYL)

    high = lax.div(c, 2)
    core = lax.rem(c, 2)

    def hops(d):
        return min(d[0], NX - d[0]) + (2 if d[2] and not d[1] else 1 if d[1] else 0)

    plane = [(dx, fl, fh) for dx in range(NX) for fl in range(2) for fh in range(2)]
    plane = sorted(plane[1:], key=hops, reverse=True)
    column = sorted(range(1, NZ), key=lambda d: min(d, NZ - d), reverse=True)

    at_x = [x * (NYL * NZ)] + [lax.rem(x + d, NX) * (NYL * NZ) for d in range(1, NX)]
    at_yl = [yl * NZ, (1 - yl) * NZ]
    at_z = [z] + [lax.rem(z + d, NZ) for d in range(1, NZ)]
    at_high = [high, 1 - high]
    at_core = [core, 1 - core]

    def plane_device(dx, fl, fh):
        return at_high[fh] * 2 + core, at_x[dx] + at_yl[fl] + z

    sibling = (high * 2 + 1 - core, m)

    def z_device(dz):
        return c, m - z + at_z[dz]

    loads = [
        pltpu.make_async_copy(src, dst, local_sem.at[i])
        for i, (src, dst) in enumerate((
            (turb_hbm, turb_ref), (amp_hbm, amp_ref), (pix_hbm, pix_ref), (act_hbm, act_ref),
            (rows_hbm.at[:, pl.ds(pl.multiple_of(m * 8, 8), 8), :], rows_ref), (gt_hbm, gt_ref),
            (gx_hbm, gx_ref), (gy_hbm, gy_ref), (recon_hbm, recon_ref),
        ))
    ]
    for load in loads:
        load.start()
    barrier = pltpu.get_barrier_semaphore()
    for dz in column:
        pl.semaphore_signal(barrier, inc=1, device_id=z_device(dz), device_id_type=MESH)
    pl.semaphore_signal(barrier, inc=1, device_id=sibling, device_id_type=MESH)
    for d in plane:
        pl.semaphore_signal(barrier, inc=1, device_id=plane_device(*d), device_id_type=MESH)

    turb_load, amp_load, pix_load, act_load, rows_load, gt_load, gx_load, gy_load, recon_load = loads

    def send(src, dst, phase, device):
        pltpu.make_async_remote_copy(
            src_ref=src, dst_ref=dst, send_sem=send_sem.at[phase], recv_sem=recv_sem.at[phase],
            device_id=device, device_id_type=MESH,
        ).start()

    def await_all(ref, phase):
        pltpu.make_async_remote_copy(
            src_ref=ref, dst_ref=ref, send_sem=send_sem.at[phase], recv_sem=recv_sem.at[phase],
            device_id=z_device(1), device_id_type=MESH,
        ).wait_recv()

    def await_sent(ref, phase):
        pltpu.make_async_remote_copy(
            src_ref=ref, dst_ref=ref, send_sem=send_sem.at[phase], recv_sem=recv_sem.at[phase],
            device_id=z_device(1), device_id_type=MESH,
        ).wait_send()

    mod_a[xy] = jnp.full((1, 128), mod_ref[0], jnp.int32).astype(F32)

    def make_field(r, phase):
        cs, sn = sincos(phase)
        amp = amp_ref[r, :]
        er = (amp * cs).astype(BF16)
        ei = (amp * sn).astype(BF16)
        low = slice(r.start + PUPIL, r.stop + PUPIL)
        e_ref[r, 0:PUPIL] = er
        e_ref[r, PUPIL:] = ei
        e_ref[low, 0:PUPIL] = -ei
        e_ref[low, PUPIL:] = er

    turb_load.wait()
    amp_load.wait()
    for r0 in range(0, PUPIL, 32):
        r = slice(r0, r0 + 32)
        make_field(r, turb_ref[r, :])

    pl.semaphore_wait(barrier, len(plane) + NZ)

    near = [d for d in plane if d[2] == 0]
    for d in near:
        send(mod_a.at[xy], mod_a.at[xy], 0, plane_device(*d))
    send(e_ref.at[pl.ds(0, PUPIL)], e_other.at[pl.ds(0, PUPIL)], FIELD, plane_device(0, 1, 1))

    recon_load.wait()
    for j in range(5):
        recon_t[0, j] = recon_ref[256 * j:256 * j + 256, :].T
        send(recon_t.at[0, j], recon_t.at[1, j], RECON, sibling)

    lane = lax.broadcasted_iota(jnp.int32, (128, 128), 0)
    pix_load.wait()
    local = pix_ref[...] - m * (8 * NF)
    pix_r = lax.rem(local, 128)
    pix_q = lax.rem(lax.div(local, 128), 4) * 8 + lax.div(local, NF)
    for s in range(8):
        oh_sig[:, 128 * s:128 * s + 128] = jnp.where(lane == pix_r[s:s + 1, :], 1.0, 0.0).astype(BF16)
    act_load.wait()
    act = act_ref[...]
    act_r = lax.rem(act, 128)
    act_q = lax.div(act, 128)
    act_q = lax.rem(act_q, 5) * 8 + lax.div(act_q, 5)
    for s in range(40):
        oh_act[:, 128 * s:128 * s + 128] = jnp.where(lane == act_r[s:s + 1, :], 1.0, 0.0).astype(BF16)
    grid_ref[...] = jnp.zeros_like(grid_ref)

    gx_load.wait()
    gx_high, gx_low = halves(gx_ref[...].T)
    gx_wide[:, 0:AY] = gx_high
    gx_wide[:, AY:2 * AY] = gx_low
    gx_wide[:, 2 * AY:] = gx_high
    gy_load.wait()
    gy_high, gy_low = halves(gy_ref[...])
    gy_tall[...] = jnp.zeros_like(gy_tall)
    gy_tall[0:AX, :] = gy_high
    gy_tall[128:128 + AX, :] = gy_high
    gy_tall[256:256 + AX, :] = gy_low

    await_all(mod_a.at[pl.ds(0, len(near))], 0)
    slots = {0: 0, 1: 1, 7: 2, 2: 3, 6: 4, 3: 5, 5: 6, 4: 7}
    for j in range(NX * NYL):
        mod_b[0, j:j + 1, :] = mod_a[j]
    for dz in column:
        send(mod_b.at[0], mod_b.at[slots[dz]], 1 if slots[dz] < 4 else LATE, z_device(dz))
    gt_load.wait()
    centred = lax.broadcasted_iota(jnp.int32, (32, 128), 1).astype(F32)
    scale = 2.0 * math.pi * RADIUS / NF

    def modulate(part):
        angle = (2.0 * math.pi / POINTS) * mod_b[4 * part:4 * part + 4].reshape(32, 128)
        ca, sa = sincos(angle)
        for h in range(2):
            pos = scale * (centred + (128.0 * h - PUPIL // 2))
            cols = slice(128 * h, 128 * h + 128)
            vr, vi = sincos(pos * sa)
            v_ref[0, 32 * part:32 * part + 32, cols] = vr
            v_ref[1, 32 * part:32 * part + 32, cols] = vi
            ur, ui = sincos(pos * ca)
            for i in range(8):
                mr = rows_ref[0, i:i + 1, cols]
                mi = rows_ref[1, i:i + 1, cols]
                r = slice(256 * part + 32 * i, 256 * part + 32 * i + 32)
                l_ref[r, cols] = (mr * ur - mi * ui).astype(BF16)
                l_ref[r, 128 * h + PUPIL:128 * h + PUPIL + 128] = (mr * ui + mi * ur).astype(BF16)

    def compute_frame(field, out, parts, add):
        points = slice(256 * parts[0], 256 * parts[-1] + 256)
        x_ref[points, :] = jnp.dot(l_ref[points, :], field[...], preferred_element_type=F32)
        for part in parts:
            vr = v_ref[0, 32 * part:32 * part + 32, :]
            vi = v_ref[1, 32 * part:32 * part + 32, :]
            for i in range(8):
                r = slice(256 * part + 32 * i, 256 * part + 32 * i + 32)
                xr = x_ref[r, 0:PUPIL]
                xi = x_ref[r, PUPIL:]
                tr = xr * vr - xi * vi
                ti = xr * vi + xi * vr
                x_ref[r, 0:PUPIL] = tr
                x_ref[r, PUPIL:] = ti
                t_ref[512 * part + 32 * i:512 * part + 32 * i + 32, :] = tr.astype(BF16)
                t_ref[512 * part + 32 * i + 256:512 * part + 32 * i + 288, :] = ti.astype(BF16)
        both = slice(512 * parts[0], 512 * parts[-1] + 512)
        y_ref[both, :] = jnp.dot(t_ref[both, :], gt_ref[...], preferred_element_type=F32)
        for i in range(8):
            for q in range(4):
                cols = slice(128 * q, 128 * q + 128)
                src = 128 * (1 - q % 2)
                total = 0.0
                for part in parts:
                    r = slice(256 * part + 32 * i, 256 * part + 32 * i + 32)
                    at = 512 * part + 32 * i
                    dr = x_ref[r, src:src + 128] - y_ref[at + 256:at + 288, cols]
                    di = x_ref[r, src + PUPIL:src + PUPIL + 128] + y_ref[at:at + 32, cols]
                    total = total + (dr * dr + di * di)
                row = jnp.sum(total, axis=0, keepdims=True) * (1.0 / 256)
                out[i:i + 1, cols] = out[i:i + 1, cols] + row if add else row

    def select_signals(frame, slot):
        tiles = jnp.concatenate([frame[:, 128 * q:128 * q + 128] for q in range(4)], axis=0).astype(BF16)
        found = jnp.dot(tiles, oh_sig[...], preferred_element_type=F32)
        s_iota = lax.broadcasted_iota(jnp.int32, (32, 128), 0)
        for s in range(8):
            cols = slice(128 * s, 128 * s + 128)
            slot[:, cols] = jnp.sum(
                jnp.where(s_iota == pix_q[s:s + 1, :], found[:, cols], 0.0), axis=0, keepdims=True
            )

    for step in range(STEPS):
        if step > 0:
            total = tot_ref[step - 1]
            if step == 1:
                await_sent(e_ref.at[pl.ds(0, PUPIL)], FIELD)
            stacked = jnp.concatenate([total[:, 128 * t:128 * t + 128] for t in range(5)], axis=0)
            picked = jnp.dot(stacked.astype(BF16), oh_act[...], preferred_element_type=F32)
            q_iota = lax.broadcasted_iota(jnp.int32, (40, 128), 0)
            for s in range(40):
                cols = slice(128 * s, 128 * s + 128)
                block = picked[:, cols]
                gat_ref[s:s + 1, :] = jnp.sum(jnp.where(q_iota == act_q[s:s + 1, :], block, 0.0), axis=0, keepdims=True)
            for y8 in range(8):
                s5, t = divmod(AX * y8, 128)
                first = gat_ref[pl.ds(s5, 8, stride=5), :]
                if t + AX <= 128:
                    row = first[:, t:t + AX]
                else:
                    second = gat_ref[pl.ds(s5 + 1, 8, stride=5), :]
                    row = jnp.concatenate([first[:, t:], second[:, :t + AX - 128]], axis=1)
                grid_ref[pl.ds(y8, 8, stride=8), :] = jnp.concatenate([row, jnp.zeros((8, 128 - AX), F32)], axis=1)
            grid_high, grid_low = halves(grid_ref[...])
            mapped = jnp.dot(
                jnp.concatenate([grid_high, grid_low, grid_high], axis=1), gy_tall[...], preferred_element_type=F32
            )
            mapped_high, mapped_low = halves(mapped)
            surface = jnp.dot(
                gx_wide[...], jnp.concatenate([mapped_high, mapped_high, mapped_low], axis=0),
                preferred_element_type=F32,
            )
            for r0 in range(0, PUPIL, 32):
                r = slice(r0, r0 + 32)
                make_field(r, turb_ref[r, :] - surface[r, :])

        base = 2 + 3 * step
        if step == 0:
            rows_load.wait()
            await_all(mod_b.at[pl.ds(0, 3)], 1)
            modulate(0)
            compute_frame(e_ref, fr_ref, (0,), False)
            await_all(e_other.at[pl.ds(0, PUPIL)], FIELD)
            e_other[PUPIL:, 0:PUPIL] = -e_other[0:PUPIL, PUPIL:]
            e_other[PUPIL:, PUPIL:] = e_other[0:PUPIL, 0:PUPIL]
            compute_frame(e_other, fr_other, (0,), False)
            await_all(mod_b.at[pl.ds(0, 4)], LATE)
            modulate(1)
            compute_frame(e_ref, fr_ref, (1,), True)
            compute_frame(e_other, fr_other, (1,), True)
            select_signals(fr_ref[...], sig_buf.at[step, high])
            select_signals(fr_other[...], sig_buf.at[step, at_high[1]])
            await_all(recon_t.at[1], RECON)
        else:
            compute_frame(e_ref, fr_ref, (0, 1), False)
            select_signals(fr_ref[...], sig_buf.at[step, high])
            send(sig_buf.at[step, high], sig_buf.at[step, high], base, plane_device(0, 0, 1))
            await_all(sig_buf.at[step, pl.ds(0, 1)], base)

        signals = jnp.concatenate([sig_buf[step, k] for k in range(2)], axis=0).astype(BF16)
        for b in range(2):
            part = jnp.concatenate(
                [jnp.dot(signals, recon_t[b, j], preferred_element_type=F32) for j in range(5)], axis=1
            )
            for k in range(2):
                rows = [part[k:k + 1, 640 * h:640 * h + 640] for h in range(2)]
                part_bf[step, k, at_core[b]] = jnp.concatenate(rows, axis=0).astype(BF16)
        plane_buf[step, xy * 2 + high] = part_bf[step, high]
        for d in plane:
            send(part_bf.at[step, at_high[d[2]]], plane_buf.at[step, xy * 2 + high], base + 1, plane_device(*d))
        await_all(plane_buf.at[step, pl.ds(0, len(plane))], base + 1)
        for k in range(NCASE):
            acc = plane_buf[step, k // 2, k % 2].astype(F32)
            for j in range(1, NX * NYL):
                acc = acc + plane_buf[step, j * 2 + k // 2, k % 2].astype(F32)
            tot_ref[step, 2 * k:2 * k + 2, :] = acc
        z_buf[step, z] = tot_ref[step].astype(BF16)
        for dz in column:
            send(z_buf.at[step, z], z_buf.at[step, z], base + 2, z_device(dz))
        await_all(z_buf.at[step, pl.ds(0, NZ - 1)], base + 2)
        acc = z_buf[step, 0].astype(F32)
        for j in range(1, NZ):
            acc = acc + z_buf[step, j].astype(F32)
        acc = LOOP_GAIN * acc
        if step > 0:
            acc = acc + tot_ref[step - 1]
        tot_ref[step] = acc
        if step == STEPS - 1:
            frame_out[...] = fr_ref[...]
            for t in range(5):
                cmd_out[pl.ds(t, 8, stride=5), :] = acc[:, 128 * t:128 * t + 128]

    await_sent(recon_t.at[0], RECON)
    await_sent(mod_a.at[pl.ds(0, len(near))], 0)
    await_sent(mod_b.at[pl.ds(0, 3)], 1)
    await_sent(mod_b.at[pl.ds(0, 4)], LATE)
    for step in range(STEPS):
        base = 2 + 3 * step
        if step > 0:
            await_sent(sig_buf.at[step, pl.ds(0, 1)], base)
        await_sent(plane_buf.at[step, pl.ds(0, len(plane))], base + 1)
        await_sent(z_buf.at[step, pl.ds(0, NZ - 1)], base + 2)


def body(turbulence, pupil_amp, mod_points, valid_pix, recon, gx, gy, act_map):
    rows, gt = sensor_tables()
    vmem = pl.BlockSpec(memory_space=pltpu.VMEM)
    hbm = pl.BlockSpec(memory_space=pltpu.HBM)
    command, frame = pl.pallas_call(
        kernel,
        out_shape=(pltpu.VMEM((40, 128), F32), pltpu.VMEM((8, NF), F32)),
        in_specs=[pl.BlockSpec(memory_space=pltpu.SMEM)] + [hbm] * 9,
        out_specs=(vmem, vmem),
        scratch_shapes=[
            pltpu.VMEM((PUPIL, PUPIL), F32),
            pltpu.VMEM((PUPIL, PUPIL), F32),
            pltpu.VMEM((8, 128), jnp.int32),
            pltpu.VMEM((40, 128), jnp.int32),
            pltpu.VMEM((AY, PUPIL), F32),
            pltpu.VMEM((AX, PUPIL), F32),
            pltpu.VMEM((PUPIL, NF), BF16),
            pltpu.VMEM((PUPIL, 3 * AY), BF16),
            pltpu.VMEM((384, PUPIL), BF16),
            pltpu.VMEM((1280, 1024), BF16),
            pltpu.VMEM((2, 5, 1024, 256), BF16),
            pltpu.VMEM((2, 8, PUPIL), F32),
            pltpu.VMEM((8, 1, 128), F32),
            pltpu.VMEM((8, 8, 128), F32),
            pltpu.VMEM((2, 64, PUPIL), F32),
            pltpu.VMEM((512, 512), BF16),
            pltpu.VMEM((512, 512), BF16),
            pltpu.VMEM((512, 512), BF16),
            pltpu.VMEM((512, 512), F32),
            pltpu.VMEM((1024, PUPIL), BF16),
            pltpu.VMEM((1024, NF), F32),
            pltpu.VMEM((128, 1024), BF16),
            pltpu.VMEM((128, 5120), BF16),
            pltpu.VMEM((8, NF), F32),
            pltpu.VMEM((8, NF), F32),
            pltpu.VMEM((STEPS, 2, 1, 1024), F32),
            pltpu.VMEM((STEPS, 2, 2, 2, 640), BF16),
            pltpu.VMEM((STEPS, 16, 2, 2, 640), BF16),
            pltpu.VMEM((STEPS, 8, 640), F32),
            pltpu.VMEM((STEPS, NZ, 8, 640), BF16),
            pltpu.VMEM((40, 128), F32),
            pltpu.VMEM((64, 128), F32),
            pltpu.SemaphoreType.DMA((9,)),
            pltpu.SemaphoreType.DMA((5 + 3 * STEPS,)),
            pltpu.SemaphoreType.DMA((5 + 3 * STEPS,)),
        ],
        compiler_params=pltpu.CompilerParams(
            collective_id=0, has_side_effects=True, vmem_limit_bytes=60 * 1024 * 1024
        ),
    )(
        mod_points, turbulence[0], pupil_amp, valid_pix.reshape(8, 128), act_map.reshape(40, 128), gx.T, gy.T,
        jnp.asarray(gt).astype(BF16), jnp.asarray(rows), recon,
    )
    return command.reshape(1, 5120), frame[None]


def solution(mesh):
    return jax.shard_map(
        body,
        mesh=mesh,
        in_specs=(P("case", None, None), P(), P("mod"), P("mod"), P("case", "mod"), P(), P(), P()),
        out_specs=(P("case", None), P("case", "mod", None)),
        check_vma=False,
    )
```

```python
import functools
import math

import jax
import jax.numpy as jnp
import numpy as np
from jax import lax
from jax.experimental import pallas as pl
from jax.experimental.pallas import tpu as pltpu
from jax.sharding import PartitionSpec as P

STEPS = 2
PUPIL = 256
NF = 512
AY = 64
AX = 80
LOOP_GAIN = 0.5
RADIUS = 6.0
POINTS = 256
NX, NYL, NZ = 4, 2, 8
NCASE = 4
MESH = pl.DeviceIdType.MESH
FIELD, RECON, LATE, SCREEN, TOTAL = range(2 + 3 * STEPS, 7 + 3 * STEPS)
F32 = jnp.float32
BF16 = jnp.bfloat16


def sensor_tables():
    k = np.arange(NF) - NF // 2
    n = np.arange(PUPIL)
    p = np.arange(NF)
    w = np.exp(-2j * np.pi * np.outer(k, n) / NF) / np.sqrt(NF)
    v = np.exp(2j * np.pi * np.outer(p, k) / NF) / np.sqrt(NF)
    turn = np.array([1, 1j, -1, -1j])[np.abs(k) % 4]
    m = (v * turn) @ w
    rows = np.stack([m.real, m.imag]).astype(np.float32)
    return rows, 2.0 * m.imag.T.astype(np.float32)


def sincos(x):
    t = x * (0.5 / math.pi)
    f = t - jnp.floor(t + 0.5)
    g = f * f
    s = 0.10920575
    for a in (-0.8457636, 3.60628896, -7.30824115, 4.44288283):
        s = s * g + a
    s = s * f
    c = 0.31124104
    for a in (-1.88386521, 5.73951693, -6.97885475, 1.4142135623730951):
        c = c * g + a
    return 1.0 - s * s, s * c


def halves(x):
    high = x.astype(BF16)
    return high, (x - high.astype(F32)).astype(BF16)


def kernel(
    mod_ref, turb_hbm, amp_hbm, pix_hbm, act_hbm, gx_hbm, gy_hbm, gt_hbm, rows_hbm, recon_hbm,
    cmd_out, frame_out,
    turb_ref, amp_ref, pix_ref, act_ref, gx_ref, gy_ref, gt_ref, gx_wide, gy_tall,
    recon_ref, recon_t, rows_ref, mod_a, mod_b, v_ref, l_ref, e_ref, e_other, x_ref, t_ref, y_ref,
    oh_sig, oh_act, fr_ref, fr_other, sig_buf, part_bf, plane_buf, tot_ref, tot_other, turb_other, z_buf, gat_ref, grid_ref,
    local_sem, send_sem, recv_sem,
):
    c = lax.axis_index("case")
    m = lax.axis_index("mod")
    z = lax.rem(m, NZ)
    xy = lax.div(m, NZ)
    yl = lax.rem(xy, NYL)
    x = lax.div(xy, NYL)

    high = lax.div(c, 2)
    core = lax.rem(c, 2)

    def hops(d):
        return min(d[0], NX - d[0]) + (2 if d[2] and not d[1] else 1 if d[1] else 0)

    plane = [(dx, fl, fh) for dx in range(NX) for fl in range(2) for fh in range(2)]
    plane = sorted(plane[1:], key=hops, reverse=True)
    column = sorted(range(1, NZ), key=lambda d: min(d, NZ - d), reverse=True)

    at_x = [x * (NYL * NZ)] + [lax.rem(x + d, NX) * (NYL * NZ) for d in range(1, NX)]
    at_yl = [yl * NZ, (1 - yl) * NZ]
    at_z = [z] + [lax.rem(z + d, NZ) for d in range(1, NZ)]
    at_high = [high, 1 - high]
    at_core = [core, 1 - core]

    def plane_device(dx, fl, fh):
        return at_high[fh] * 2 + core, at_x[dx] + at_yl[fl] + z

    sibling = (high * 2 + 1 - core, m)

    def z_device(dz):
        return c, m - z + at_z[dz]

    loads = [
        pltpu.make_async_copy(src, dst, local_sem.at[i])
        for i, (src, dst) in enumerate((
            (turb_hbm, turb_ref), (amp_hbm, amp_ref), (pix_hbm, pix_ref), (act_hbm, act_ref),
            (rows_hbm.at[:, pl.ds(pl.multiple_of(m * 8, 8), 8), :], rows_ref), (gt_hbm, gt_ref),
            (gx_hbm, gx_ref), (gy_hbm, gy_ref), (recon_hbm, recon_ref),
        ))
    ]
    for load in loads:
        load.start()
    barrier = pltpu.get_barrier_semaphore()
    for dz in column:
        pl.semaphore_signal(barrier, inc=1, device_id=z_device(dz), device_id_type=MESH)
    pl.semaphore_signal(barrier, inc=1, device_id=sibling, device_id_type=MESH)
    for d in plane:
        pl.semaphore_signal(barrier, inc=1, device_id=plane_device(*d), device_id_type=MESH)

    turb_load, amp_load, pix_load, act_load, rows_load, gt_load, gx_load, gy_load, recon_load = loads

    def send(src, dst, phase, device):
        pltpu.make_async_remote_copy(
            src_ref=src, dst_ref=dst, send_sem=send_sem.at[phase], recv_sem=recv_sem.at[phase],
            device_id=device, device_id_type=MESH,
        ).start()

    def await_all(ref, phase):
        pltpu.make_async_remote_copy(
            src_ref=ref, dst_ref=ref, send_sem=send_sem.at[phase], recv_sem=recv_sem.at[phase],
            device_id=z_device(1), device_id_type=MESH,
        ).wait_recv()

    def await_sent(ref, phase):
        pltpu.make_async_remote_copy(
            src_ref=ref, dst_ref=ref, send_sem=send_sem.at[phase], recv_sem=recv_sem.at[phase],
            device_id=z_device(1), device_id_type=MESH,
        ).wait_send()

    mod_a[xy] = jnp.full((1, 128), mod_ref[0], jnp.int32).astype(F32)

    def make_field(r, phase, field):
        cs, sn = sincos(phase)
        amp = amp_ref[r, :]
        er = (amp * cs).astype(BF16)
        ei = (amp * sn).astype(BF16)
        low = slice(r.start + PUPIL, r.stop + PUPIL)
        field[r, 0:PUPIL] = er
        field[r, PUPIL:] = ei
        field[low, 0:PUPIL] = -ei
        field[low, PUPIL:] = er

    turb_load.wait()
    amp_load.wait()
    for r0 in range(0, PUPIL, 32):
        r = slice(r0, r0 + 32)
        make_field(r, turb_ref[r, :], e_ref)

    pl.semaphore_wait(barrier, len(plane) + NZ)

    near = [d for d in plane if d[2] == 0]
    for d in near:
        send(mod_a.at[xy], mod_a.at[xy], 0, plane_device(*d))
    send(e_ref.at[pl.ds(0, PUPIL)], e_other.at[pl.ds(0, PUPIL)], FIELD, plane_device(0, 1, 1))

    recon_load.wait()
    for j in range(5):
        recon_t[0, j] = recon_ref[256 * j:256 * j + 256, :].T
        send(recon_t.at[0, j], recon_t.at[1, j], RECON, sibling)

    lane = lax.broadcasted_iota(jnp.int32, (128, 128), 0)
    pix_load.wait()
    local = pix_ref[...] - m * (8 * NF)
    pix_r = lax.rem(local, 128)
    pix_q = lax.rem(lax.div(local, 128), 4) * 8 + lax.div(local, NF)
    for s in range(8):
        oh_sig[:, 128 * s:128 * s + 128] = jnp.where(lane == pix_r[s:s + 1, :], 1.0, 0.0).astype(BF16)
    act_load.wait()
    act = act_ref[...]
    act_r = lax.rem(act, 128)
    act_q = lax.div(act, 128)
    act_q = lax.rem(act_q, 5) * 8 + lax.div(act_q, 5)
    for s in range(40):
        oh_act[:, 128 * s:128 * s + 128] = jnp.where(lane == act_r[s:s + 1, :], 1.0, 0.0).astype(BF16)
    grid_ref[...] = jnp.zeros_like(grid_ref)

    gx_load.wait()
    gx_high, gx_low = halves(gx_ref[...].T)
    gx_wide[:, 0:AY] = gx_high
    gx_wide[:, AY:2 * AY] = gx_low
    gx_wide[:, 2 * AY:] = gx_high
    gy_load.wait()
    gy_high, gy_low = halves(gy_ref[...])
    gy_tall[...] = jnp.zeros_like(gy_tall)
    gy_tall[0:AX, :] = gy_high
    gy_tall[128:128 + AX, :] = gy_high
    gy_tall[256:256 + AX, :] = gy_low

    await_all(mod_a.at[pl.ds(0, len(near))], 0)
    slots = {0: 0, 1: 1, 7: 2, 2: 3, 6: 4, 3: 5, 5: 6, 4: 7}
    for j in range(NX * NYL):
        mod_b[0, j:j + 1, :] = mod_a[j]
    for dz in column:
        send(mod_b.at[0], mod_b.at[slots[dz]], 1 if slots[dz] < 4 else LATE, z_device(dz))
    gt_load.wait()
    centred = lax.broadcasted_iota(jnp.int32, (32, 128), 1).astype(F32)
    scale = 2.0 * math.pi * RADIUS / NF

    def modulate(part):
        angle = (2.0 * math.pi / POINTS) * mod_b[4 * part:4 * part + 4].reshape(32, 128)
        ca, sa = sincos(angle)
        for h in range(2):
            pos = scale * (centred + (128.0 * h - PUPIL // 2))
            cols = slice(128 * h, 128 * h + 128)
            vr, vi = sincos(pos * sa)
            v_ref[0, 32 * part:32 * part + 32, cols] = vr
            v_ref[1, 32 * part:32 * part + 32, cols] = vi
            ur, ui = sincos(pos * ca)
            for i in range(8):
                mr = rows_ref[0, i:i + 1, cols]
                mi = rows_ref[1, i:i + 1, cols]
                r = slice(256 * part + 32 * i, 256 * part + 32 * i + 32)
                l_ref[r, cols] = (mr * ur - mi * ui).astype(BF16)
                l_ref[r, 128 * h + PUPIL:128 * h + PUPIL + 128] = (mr * ui + mi * ur).astype(BF16)

    def flatten_phase(total, screen, field):
        stacked = jnp.concatenate([total[:, 128 * t:128 * t + 128] for t in range(5)], axis=0)
        picked = jnp.dot(stacked.astype(BF16), oh_act[...], preferred_element_type=F32)
        q_iota = lax.broadcasted_iota(jnp.int32, (40, 128), 0)
        for s in range(40):
            cols = slice(128 * s, 128 * s + 128)
            block = picked[:, cols]
            gat_ref[s:s + 1, :] = jnp.sum(jnp.where(q_iota == act_q[s:s + 1, :], block, 0.0), axis=0, keepdims=True)
        for y8 in range(8):
            s5, t = divmod(AX * y8, 128)
            first = gat_ref[pl.ds(s5, 8, stride=5), :]
            if t + AX <= 128:
                row = first[:, t:t + AX]
            else:
                second = gat_ref[pl.ds(s5 + 1, 8, stride=5), :]
                row = jnp.concatenate([first[:, t:], second[:, :t + AX - 128]], axis=1)
            grid_ref[pl.ds(y8, 8, stride=8), :] = jnp.concatenate([row, jnp.zeros((8, 128 - AX), F32)], axis=1)
        grid_high, grid_low = halves(grid_ref[...])
        mapped = jnp.dot(
            jnp.concatenate([grid_high, grid_low, grid_high], axis=1), gy_tall[...], preferred_element_type=F32
        )
        mapped_high, mapped_low = halves(mapped)
        surface = jnp.dot(
            gx_wide[...], jnp.concatenate([mapped_high, mapped_high, mapped_low], axis=0),
            preferred_element_type=F32,
        )
        for r0 in range(0, PUPIL, 32):
            r = slice(r0, r0 + 32)
            make_field(r, screen[r, :] - surface[r, :], field)

    def compute_frame(field, out, parts, add):
        points = slice(256 * parts[0], 256 * parts[-1] + 256)
        x_ref[points, :] = jnp.dot(l_ref[points, :], field[...], preferred_element_type=F32)
        for part in parts:
            vr = v_ref[0, 32 * part:32 * part + 32, :]
            vi = v_ref[1, 32 * part:32 * part + 32, :]
            for i in range(8):
                r = slice(256 * part + 32 * i, 256 * part + 32 * i + 32)
                xr = x_ref[r, 0:PUPIL]
                xi = x_ref[r, PUPIL:]
                tr = xr * vr - xi * vi
                ti = xr * vi + xi * vr
                x_ref[r, 0:PUPIL] = tr
                x_ref[r, PUPIL:] = ti
                t_ref[512 * part + 32 * i:512 * part + 32 * i + 32, :] = tr.astype(BF16)
                t_ref[512 * part + 32 * i + 256:512 * part + 32 * i + 288, :] = ti.astype(BF16)
        both = slice(512 * parts[0], 512 * parts[-1] + 512)
        y_ref[both, :] = jnp.dot(t_ref[both, :], gt_ref[...], preferred_element_type=F32)
        for i in range(8):
            for q in range(4):
                cols = slice(128 * q, 128 * q + 128)
                src = 128 * (1 - q % 2)
                total = 0.0
                for part in parts:
                    r = slice(256 * part + 32 * i, 256 * part + 32 * i + 32)
                    at = 512 * part + 32 * i
                    dr = x_ref[r, src:src + 128] - y_ref[at + 256:at + 288, cols]
                    di = x_ref[r, src + PUPIL:src + PUPIL + 128] + y_ref[at:at + 32, cols]
                    total = total + (dr * dr + di * di)
                row = jnp.sum(total, axis=0, keepdims=True) * (1.0 / 256)
                out[i:i + 1, cols] = out[i:i + 1, cols] + row if add else row

    def select_signals(frame, slot):
        tiles = jnp.concatenate([frame[:, 128 * q:128 * q + 128] for q in range(4)], axis=0).astype(BF16)
        found = jnp.dot(tiles, oh_sig[...], preferred_element_type=F32)
        s_iota = lax.broadcasted_iota(jnp.int32, (32, 128), 0)
        for s in range(8):
            cols = slice(128 * s, 128 * s + 128)
            slot[:, cols] = jnp.sum(
                jnp.where(s_iota == pix_q[s:s + 1, :], found[:, cols], 0.0), axis=0, keepdims=True
            )

    for step in range(STEPS):
        base = 2 + 3 * step
        if step == 0:
            rows_load.wait()
            await_all(mod_b.at[pl.ds(0, 3)], 1)
            modulate(0)
            compute_frame(e_ref, fr_ref, (0,), False)
            await_all(e_other.at[pl.ds(0, PUPIL)], FIELD)
            e_other[PUPIL:, 0:PUPIL] = -e_other[0:PUPIL, PUPIL:]
            e_other[PUPIL:, PUPIL:] = e_other[0:PUPIL, 0:PUPIL]
            compute_frame(e_other, fr_other, (0,), False)
            await_all(mod_b.at[pl.ds(0, 4)], LATE)
            modulate(1)
            compute_frame(e_ref, fr_ref, (1,), True)
            compute_frame(e_other, fr_other, (1,), True)
            select_signals(fr_ref[...], sig_buf.at[step, high])
            select_signals(fr_other[...], sig_buf.at[step, at_high[1]])
            await_all(recon_t.at[1], RECON)
        else:
            await_sent(e_ref.at[pl.ds(0, PUPIL)], FIELD)
            flatten_phase(tot_ref[0], turb_ref, e_ref)
            compute_frame(e_ref, fr_ref, (0, 1), False)
            select_signals(fr_ref[...], sig_buf.at[step, high])
            await_all(turb_other, SCREEN)
            await_all(tot_other, TOTAL)
            flatten_phase(tot_other[...], turb_other, e_other)
            compute_frame(e_other, fr_other, (0, 1), False)
            select_signals(fr_other[...], sig_buf.at[step, at_high[1]])

        signals = jnp.concatenate([sig_buf[step, k] for k in range(2)], axis=0).astype(BF16)
        for b in range(2):
            part = jnp.concatenate(
                [jnp.dot(signals, recon_t[b, j], preferred_element_type=F32) for j in range(5)], axis=1
            )
            for k in range(2):
                rows = [part[k:k + 1, 640 * h:640 * h + 640] for h in range(2)]
                part_bf[step, k, at_core[b]] = jnp.concatenate(rows, axis=0).astype(BF16)
        plane_buf[step, xy * 2 + high] = part_bf[step, high]
        for d in plane:
            send(part_bf.at[step, at_high[d[2]]], plane_buf.at[step, xy * 2 + high], base + 1, plane_device(*d))
        await_all(plane_buf.at[step, pl.ds(0, len(plane))], base + 1)
        for k in range(NCASE):
            acc = plane_buf[step, k // 2, k % 2].astype(F32)
            for j in range(1, NX * NYL):
                acc = acc + plane_buf[step, j * 2 + k // 2, k % 2].astype(F32)
            tot_ref[step, 2 * k:2 * k + 2, :] = acc
        z_buf[step, z] = tot_ref[step].astype(BF16)
        for dz in column:
            send(z_buf.at[step, z], z_buf.at[step, z], base + 2, z_device(dz))
        if step == 0:
            send(turb_ref, turb_other, SCREEN, plane_device(0, 1, 1))
        await_all(z_buf.at[step, pl.ds(0, NZ - 1)], base + 2)
        acc = z_buf[step, 0].astype(F32)
        for j in range(1, NZ):
            acc = acc + z_buf[step, j].astype(F32)
        acc = LOOP_GAIN * acc
        if step > 0:
            acc = acc + tot_ref[step - 1]
        tot_ref[step] = acc
        if step == 0:
            send(tot_ref.at[0], tot_other, TOTAL, plane_device(0, 1, 1))
        if step == STEPS - 1:
            frame_out[...] = fr_ref[...]
            for t in range(5):
                cmd_out[pl.ds(t, 8, stride=5), :] = acc[:, 128 * t:128 * t + 128]

    await_sent(recon_t.at[0], RECON)
    await_sent(turb_ref, SCREEN)
    await_sent(tot_ref.at[0], TOTAL)
    await_sent(mod_a.at[pl.ds(0, len(near))], 0)
    await_sent(mod_b.at[pl.ds(0, 3)], 1)
    await_sent(mod_b.at[pl.ds(0, 4)], LATE)
    for step in range(STEPS):
        base = 2 + 3 * step
        await_sent(plane_buf.at[step, pl.ds(0, len(plane))], base + 1)
        await_sent(z_buf.at[step, pl.ds(0, NZ - 1)], base + 2)


def body(turbulence, pupil_amp, mod_points, valid_pix, recon, gx, gy, act_map):
    rows, gt = sensor_tables()
    vmem = pl.BlockSpec(memory_space=pltpu.VMEM)
    hbm = pl.BlockSpec(memory_space=pltpu.HBM)
    command, frame = pl.pallas_call(
        kernel,
        out_shape=(pltpu.VMEM((40, 128), F32), pltpu.VMEM((8, NF), F32)),
        in_specs=[pl.BlockSpec(memory_space=pltpu.SMEM)] + [hbm] * 9,
        out_specs=(vmem, vmem),
        scratch_shapes=[
            pltpu.VMEM((PUPIL, PUPIL), F32),
            pltpu.VMEM((PUPIL, PUPIL), F32),
            pltpu.VMEM((8, 128), jnp.int32),
            pltpu.VMEM((40, 128), jnp.int32),
            pltpu.VMEM((AY, PUPIL), F32),
            pltpu.VMEM((AX, PUPIL), F32),
            pltpu.VMEM((PUPIL, NF), BF16),
            pltpu.VMEM((PUPIL, 3 * AY), BF16),
            pltpu.VMEM((384, PUPIL), BF16),
            pltpu.VMEM((1280, 1024), BF16),
            pltpu.VMEM((2, 5, 1024, 256), BF16),
            pltpu.VMEM((2, 8, PUPIL), F32),
            pltpu.VMEM((8, 1, 128), F32),
            pltpu.VMEM((8, 8, 128), F32),
            pltpu.VMEM((2, 64, PUPIL), F32),
            pltpu.VMEM((512, 512), BF16),
            pltpu.VMEM((512, 512), BF16),
            pltpu.VMEM((512, 512), BF16),
            pltpu.VMEM((512, 512), F32),
            pltpu.VMEM((1024, PUPIL), BF16),
            pltpu.VMEM((1024, NF), F32),
            pltpu.VMEM((128, 1024), BF16),
            pltpu.VMEM((128, 5120), BF16),
            pltpu.VMEM((8, NF), F32),
            pltpu.VMEM((8, NF), F32),
            pltpu.VMEM((STEPS, 2, 1, 1024), F32),
            pltpu.VMEM((STEPS, 2, 2, 2, 640), BF16),
            pltpu.VMEM((STEPS, 16, 2, 2, 640), BF16),
            pltpu.VMEM((STEPS, 8, 640), F32),
            pltpu.VMEM((8, 640), F32),
            pltpu.VMEM((PUPIL, PUPIL), F32),
            pltpu.VMEM((STEPS, NZ, 8, 640), BF16),
            pltpu.VMEM((40, 128), F32),
            pltpu.VMEM((64, 128), F32),
            pltpu.SemaphoreType.DMA((9,)),
            pltpu.SemaphoreType.DMA((7 + 3 * STEPS,)),
            pltpu.SemaphoreType.DMA((7 + 3 * STEPS,)),
        ],
        compiler_params=pltpu.CompilerParams(
            collective_id=0, has_side_effects=True, vmem_limit_bytes=60 * 1024 * 1024
        ),
    )(
        mod_points, turbulence[0], pupil_amp, valid_pix.reshape(8, 128), act_map.reshape(40, 128), gx.T, gy.T,
        jnp.asarray(gt).astype(BF16), jnp.asarray(rows), recon,
    )
    return command.reshape(1, 5120), frame[None]


def solution(mesh):
    return jax.shard_map(
        body,
        mesh=mesh,
        in_specs=(P("case", None, None), P(), P("mod"), P("mod"), P("case", "mod"), P(), P(), P()),
        out_specs=(P("case", None), P("case", "mod", None)),
        check_vma=False,
    )
```

```python
import functools
import math

import jax
import jax.numpy as jnp
import numpy as np
from jax import lax
from jax.experimental import pallas as pl
from jax.experimental.pallas import tpu as pltpu
from jax.sharding import PartitionSpec as P

STEPS = 2
PUPIL = 256
NF = 512
AY = 64
AX = 80
LOOP_GAIN = 0.5
RADIUS = 6.0
POINTS = 256
NX, NYL, NZ = 4, 2, 8
NCASE = 4
MESH = pl.DeviceIdType.MESH
FIELD, RECON, LATE = 2 + 3 * STEPS, 3 + 3 * STEPS, 4 + 3 * STEPS
F32 = jnp.float32
BF16 = jnp.bfloat16


def sensor_tables():
    k = np.arange(NF) - NF // 2
    n = np.arange(PUPIL)
    p = np.arange(NF)
    w = np.exp(-2j * np.pi * np.outer(k, n) / NF) / np.sqrt(NF)
    v = np.exp(2j * np.pi * np.outer(p, k) / NF) / np.sqrt(NF)
    turn = np.array([1, 1j, -1, -1j])[np.abs(k) % 4]
    m = (v * turn) @ w
    rows = np.stack([m.real, m.imag]).astype(np.float32)
    return rows, 2.0 * m.imag.T.astype(np.float32)


def sincos(x):
    t = x * (0.5 / math.pi)
    f = t - jnp.floor(t + 0.5)
    g = f * f
    s = 0.10920575
    for a in (-0.8457636, 3.60628896, -7.30824115, 4.44288283):
        s = s * g + a
    s = s * f
    c = 0.31124104
    for a in (-1.88386521, 5.73951693, -6.97885475, 1.4142135623730951):
        c = c * g + a
    return 1.0 - s * s, s * c


def halves(x):
    high = x.astype(BF16)
    return high, (x - high.astype(F32)).astype(BF16)


def kernel(
    mod_ref, turb_hbm, amp_hbm, pix_hbm, act_hbm, gx_hbm, gy_hbm, gt_hbm, rows_hbm, recon_hbm,
    cmd_out, frame_out,
    turb_ref, amp_ref, pix_ref, act_ref, gx_ref, gy_ref, gt_ref, gx_wide, gy_tall,
    recon_ref, recon_t, rows_ref, mod_a, mod_b, v_ref, l_ref, e_ref, e_other, x_ref, t_ref, y_ref,
    oh_sig, oh_act, fr_ref, fr_other, sig_buf, part_bf, plane_buf, tot_ref, z_buf, gat_ref, grid_ref,
    local_sem, send_sem, recv_sem,
):
    c = lax.axis_index("case")
    m = lax.axis_index("mod")
    z = lax.rem(m, NZ)
    xy = lax.div(m, NZ)
    yl = lax.rem(xy, NYL)
    x = lax.div(xy, NYL)

    high = lax.div(c, 2)
    core = lax.rem(c, 2)

    def hops(d):
        return min(d[0], NX - d[0]) + (2 if d[2] and not d[1] else 1 if d[1] else 0)

    plane = [(dx, fl, fh) for dx in range(NX) for fl in range(2) for fh in range(2)]
    plane = sorted(plane[1:], key=hops, reverse=True)
    column = sorted(range(1, NZ), key=lambda d: min(d, NZ - d), reverse=True)

    at_x = [x * (NYL * NZ)] + [lax.rem(x + d, NX) * (NYL * NZ) for d in range(1, NX)]
    at_yl = [yl * NZ, (1 - yl) * NZ]
    at_z = [z] + [lax.rem(z + d, NZ) for d in range(1, NZ)]
    at_high = [high, 1 - high]
    at_core = [core, 1 - core]

    def plane_device(dx, fl, fh):
        return at_high[fh] * 2 + core, at_x[dx] + at_yl[fl] + z

    sibling = (high * 2 + 1 - core, m)

    def z_device(dz):
        return c, m - z + at_z[dz]

    loads = [
        pltpu.make_async_copy(src, dst, local_sem.at[i])
        for i, (src, dst) in enumerate((
            (turb_hbm, turb_ref), (amp_hbm, amp_ref), (pix_hbm, pix_ref), (act_hbm, act_ref),
            (rows_hbm.at[:, pl.ds(pl.multiple_of(m * 8, 8), 8), :], rows_ref), (gt_hbm, gt_ref),
            (gx_hbm, gx_ref), (gy_hbm, gy_ref), (recon_hbm, recon_ref),
        ))
    ]
    for load in loads:
        load.start()
    barrier = pltpu.get_barrier_semaphore()
    for dz in column:
        pl.semaphore_signal(barrier, inc=1, device_id=z_device(dz), device_id_type=MESH)
    pl.semaphore_signal(barrier, inc=1, device_id=sibling, device_id_type=MESH)
    for d in plane:
        pl.semaphore_signal(barrier, inc=1, device_id=plane_device(*d), device_id_type=MESH)

    turb_load, amp_load, pix_load, act_load, rows_load, gt_load, gx_load, gy_load, recon_load = loads

    def send(src, dst, phase, device):
        pltpu.make_async_remote_copy(
            src_ref=src, dst_ref=dst, send_sem=send_sem.at[phase], recv_sem=recv_sem.at[phase],
            device_id=device, device_id_type=MESH,
        ).start()

    def await_all(ref, phase):
        pltpu.make_async_remote_copy(
            src_ref=ref, dst_ref=ref, send_sem=send_sem.at[phase], recv_sem=recv_sem.at[phase],
            device_id=z_device(1), device_id_type=MESH,
        ).wait_recv()

    def await_sent(ref, phase):
        pltpu.make_async_remote_copy(
            src_ref=ref, dst_ref=ref, send_sem=send_sem.at[phase], recv_sem=recv_sem.at[phase],
            device_id=z_device(1), device_id_type=MESH,
        ).wait_send()

    mod_a[xy] = jnp.full((1, 128), mod_ref[0], jnp.int32).astype(F32)

    def make_field(r, phase):
        cs, sn = sincos(phase)
        amp = amp_ref[r, :]
        er = (amp * cs).astype(BF16)
        ei = (amp * sn).astype(BF16)
        low = slice(r.start + PUPIL, r.stop + PUPIL)
        e_ref[r, 0:PUPIL] = er
        e_ref[r, PUPIL:] = ei
        e_ref[low, 0:PUPIL] = -ei
        e_ref[low, PUPIL:] = er

    turb_load.wait()
    amp_load.wait()
    for r0 in range(0, PUPIL, 32):
        r = slice(r0, r0 + 32)
        make_field(r, turb_ref[r, :])

    pl.semaphore_wait(barrier, len(plane) + NZ)

    near = [d for d in plane if d[2] == 0]
    for d in near:
        send(mod_a.at[xy], mod_a.at[xy], 0, plane_device(*d))
    send(e_ref.at[pl.ds(0, PUPIL)], e_other.at[pl.ds(0, PUPIL)], FIELD, plane_device(0, 1, 1))

    recon_load.wait()
    for j in range(5):
        recon_t[0, j] = recon_ref[256 * j:256 * j + 256, :].T
        send(recon_t.at[0, j], recon_t.at[1, j], RECON, sibling)

    lane = lax.broadcasted_iota(jnp.int32, (128, 128), 0)
    pix_load.wait()
    local = pix_ref[...] - m * (8 * NF)
    pix_r = lax.rem(local, 128)
    pix_q = lax.rem(lax.div(local, 128), 4) * 8 + lax.div(local, NF)
    for s in range(8):
        oh_sig[:, 128 * s:128 * s + 128] = jnp.where(lane == pix_r[s:s + 1, :], 1.0, 0.0).astype(BF16)
    act_load.wait()
    act = act_ref[...]
    act_r = lax.rem(act, 128)
    act_q = lax.div(act, 128)
    act_q = lax.rem(act_q, 5) * 8 + lax.div(act_q, 5)
    for s in range(40):
        oh_act[:, 128 * s:128 * s + 128] = jnp.where(lane == act_r[s:s + 1, :], 1.0, 0.0).astype(BF16)
    grid_ref[...] = jnp.zeros_like(grid_ref)

    gx_load.wait()
    gx_high, gx_low = halves(gx_ref[...].T)
    gx_wide[:, 0:AY] = gx_high
    gx_wide[:, AY:2 * AY] = gx_low
    gx_wide[:, 2 * AY:] = gx_high
    gy_load.wait()
    gy_high, gy_low = halves(gy_ref[...])
    gy_tall[...] = jnp.zeros_like(gy_tall)
    gy_tall[0:AX, :] = gy_high
    gy_tall[128:128 + AX, :] = gy_high
    gy_tall[256:256 + AX, :] = gy_low

    await_all(mod_a.at[pl.ds(0, len(near))], 0)
    slots = {0: 0, 1: 1, 7: 2, 2: 3, 6: 4, 3: 5, 5: 6, 4: 7}
    for j in range(NX * NYL):
        mod_b[0, j:j + 1, :] = mod_a[j]
    for dz in column:
        send(mod_b.at[0], mod_b.at[slots[dz]], 1 if slots[dz] < 4 else LATE, z_device(dz))
    gt_load.wait()
    centred = lax.broadcasted_iota(jnp.int32, (32, 128), 1).astype(F32)
    scale = 2.0 * math.pi * RADIUS / NF

    def modulate(part):
        angle = (2.0 * math.pi / POINTS) * mod_b[4 * part:4 * part + 4].reshape(32, 128)
        ca, sa = sincos(angle)
        for h in range(2):
            pos = scale * (centred + (128.0 * h - PUPIL // 2))
            cols = slice(128 * h, 128 * h + 128)
            vr, vi = sincos(pos * sa)
            v_ref[0, 32 * part:32 * part + 32, cols] = vr
            v_ref[1, 32 * part:32 * part + 32, cols] = vi
            ur, ui = sincos(pos * ca)
            for i in range(8):
                mr = rows_ref[0, i:i + 1, cols]
                mi = rows_ref[1, i:i + 1, cols]
                r = slice(256 * part + 32 * i, 256 * part + 32 * i + 32)
                l_ref[r, cols] = (mr * ur - mi * ui).astype(BF16)
                l_ref[r, 128 * h + PUPIL:128 * h + PUPIL + 128] = (mr * ui + mi * ur).astype(BF16)

    def compute_frame(field, out, parts, add):
        points = slice(256 * parts[0], 256 * parts[-1] + 256)
        x_ref[points, :] = jnp.dot(l_ref[points, :], field[...], preferred_element_type=F32)
        for part in parts:
            vr = v_ref[0, 32 * part:32 * part + 32, :]
            vi = v_ref[1, 32 * part:32 * part + 32, :]
            for i in range(8):
                r = slice(256 * part + 32 * i, 256 * part + 32 * i + 32)
                xr = x_ref[r, 0:PUPIL]
                xi = x_ref[r, PUPIL:]
                tr = xr * vr - xi * vi
                ti = xr * vi + xi * vr
                x_ref[r, 0:PUPIL] = tr
                x_ref[r, PUPIL:] = ti
                t_ref[512 * part + 32 * i:512 * part + 32 * i + 32, :] = tr.astype(BF16)
                t_ref[512 * part + 32 * i + 256:512 * part + 32 * i + 288, :] = ti.astype(BF16)
        both = slice(512 * parts[0], 512 * parts[-1] + 512)
        y_ref[both, :] = jnp.dot(t_ref[both, :], gt_ref[...], preferred_element_type=F32)
        for i in range(8):
            for q in range(4):
                cols = slice(128 * q, 128 * q + 128)
                src = 128 * (1 - q % 2)
                total = 0.0
                for part in parts:
                    r = slice(256 * part + 32 * i, 256 * part + 32 * i + 32)
                    at = 512 * part + 32 * i
                    dr = x_ref[r, src:src + 128] - y_ref[at + 256:at + 288, cols]
                    di = x_ref[r, src + PUPIL:src + PUPIL + 128] + y_ref[at:at + 32, cols]
                    total = total + (dr * dr + di * di)
                row = jnp.sum(total, axis=0, keepdims=True) * (1.0 / 256)
                out[i:i + 1, cols] = out[i:i + 1, cols] + row if add else row

    def select_signals(frame, slot):
        tiles = jnp.concatenate([frame[:, 128 * q:128 * q + 128] for q in range(4)], axis=0).astype(BF16)
        found = jnp.dot(tiles, oh_sig[...], preferred_element_type=F32)
        s_iota = lax.broadcasted_iota(jnp.int32, (32, 128), 0)
        for s in range(8):
            cols = slice(128 * s, 128 * s + 128)
            slot[:, cols] = jnp.sum(
                jnp.where(s_iota == pix_q[s:s + 1, :], found[:, cols], 0.0), axis=0, keepdims=True
            )

    for step in range(STEPS):
        if step > 0:
            total = tot_ref[step - 1]
            if step == 1:
                await_sent(e_ref.at[pl.ds(0, PUPIL)], FIELD)
            stacked = jnp.concatenate([total[:, 128 * t:128 * t + 128] for t in range(5)], axis=0)
            picked = jnp.dot(stacked.astype(BF16), oh_act[...], preferred_element_type=F32)
            q_iota = lax.broadcasted_iota(jnp.int32, (40, 128), 0)
            for s in range(40):
                cols = slice(128 * s, 128 * s + 128)
                block = picked[:, cols]
                gat_ref[s:s + 1, :] = jnp.sum(jnp.where(q_iota == act_q[s:s + 1, :], block, 0.0), axis=0, keepdims=True)
            for y8 in range(8):
                s5, t = divmod(AX * y8, 128)
                first = gat_ref[pl.ds(s5, 8, stride=5), :]
                if t + AX <= 128:
                    row = first[:, t:t + AX]
                else:
                    second = gat_ref[pl.ds(s5 + 1, 8, stride=5), :]
                    row = jnp.concatenate([first[:, t:], second[:, :t + AX - 128]], axis=1)
                grid_ref[pl.ds(y8, 8, stride=8), :] = jnp.concatenate([row, jnp.zeros((8, 128 - AX), F32)], axis=1)
            grid_high, grid_low = halves(grid_ref[...])
            mapped = jnp.dot(
                jnp.concatenate([grid_high, grid_low, grid_high], axis=1), gy_tall[...], preferred_element_type=F32
            )
            mapped_high, mapped_low = halves(mapped)
            surface = jnp.dot(
                gx_wide[...], jnp.concatenate([mapped_high, mapped_high, mapped_low], axis=0),
                preferred_element_type=F32,
            )
            for r0 in range(0, PUPIL, 32):
                r = slice(r0, r0 + 32)
                make_field(r, turb_ref[r, :] - surface[r, :])

        base = 2 + 3 * step
        if step == 0:
            rows_load.wait()
            await_all(mod_b.at[pl.ds(0, 3)], 1)
            modulate(0)
            compute_frame(e_ref, fr_ref, (0,), False)
            await_all(e_other.at[pl.ds(0, PUPIL)], FIELD)
            e_other[PUPIL:, 0:PUPIL] = -e_other[0:PUPIL, PUPIL:]
            e_other[PUPIL:, PUPIL:] = e_other[0:PUPIL, 0:PUPIL]
            compute_frame(e_other, fr_other, (0,), False)
            await_all(mod_b.at[pl.ds(0, 4)], LATE)
            modulate(1)
            compute_frame(e_ref, fr_ref, (1,), True)
            compute_frame(e_other, fr_other, (1,), True)
            select_signals(fr_ref[...], sig_buf.at[step, high])
            select_signals(fr_other[...], sig_buf.at[step, at_high[1]])
            await_all(recon_t.at[1], RECON)
        else:
            compute_frame(e_ref, fr_ref, (0, 1), False)
            select_signals(fr_ref[...], sig_buf.at[step, high])
            send(sig_buf.at[step, high], sig_buf.at[step, high], base, plane_device(0, 0, 1))

        for turn in (((0, 1),), ((0,), (1,)))[min(step, 1)]:
            if turn == (1,):
                await_all(sig_buf.at[step, pl.ds(0, 1)], base)
            signals = jnp.concatenate([sig_buf[step, at_high[k]] for k in turn], axis=0).astype(BF16)
            for b in range(2):
                part = jnp.concatenate(
                    [jnp.dot(signals, recon_t[b, j], preferred_element_type=F32) for j in range(5)], axis=1
                )
                for n, k in enumerate(turn):
                    rows = [part[n:n + 1, 640 * h:640 * h + 640] for h in range(2)]
                    part_bf[step, at_high[k], at_core[b]] = jnp.concatenate(rows, axis=0).astype(BF16)
            if 0 in turn:
                plane_buf[step, xy * 2 + high] = part_bf[step, high]
            for d in plane:
                if d[2] in turn:
                    send(part_bf.at[step, at_high[d[2]]], plane_buf.at[step, xy * 2 + high], base + 1, plane_device(*d))
        await_all(plane_buf.at[step, pl.ds(0, len(plane))], base + 1)
        for k in range(NCASE):
            acc = plane_buf[step, k // 2, k % 2].astype(F32)
            for j in range(1, NX * NYL):
                acc = acc + plane_buf[step, j * 2 + k // 2, k % 2].astype(F32)
            tot_ref[step, 2 * k:2 * k + 2, :] = acc
        z_buf[step, z] = tot_ref[step].astype(BF16)
        for dz in column:
            send(z_buf.at[step, z], z_buf.at[step, z], base + 2, z_device(dz))
        await_all(z_buf.at[step, pl.ds(0, NZ - 1)], base + 2)
        acc = z_buf[step, 0].astype(F32)
        for j in range(1, NZ):
            acc = acc + z_buf[step, j].astype(F32)
        acc = LOOP_GAIN * acc
        if step > 0:
            acc = acc + tot_ref[step - 1]
        tot_ref[step] = acc
        if step == STEPS - 1:
            frame_out[...] = fr_ref[...]
            for t in range(5):
                cmd_out[pl.ds(t, 8, stride=5), :] = acc[:, 128 * t:128 * t + 128]

    await_sent(recon_t.at[0], RECON)
    await_sent(mod_a.at[pl.ds(0, len(near))], 0)
    await_sent(mod_b.at[pl.ds(0, 3)], 1)
    await_sent(mod_b.at[pl.ds(0, 4)], LATE)
    for step in range(STEPS):
        base = 2 + 3 * step
        if step > 0:
            await_sent(sig_buf.at[step, pl.ds(0, 1)], base)
        await_sent(plane_buf.at[step, pl.ds(0, len(plane))], base + 1)
        await_sent(z_buf.at[step, pl.ds(0, NZ - 1)], base + 2)


def body(turbulence, pupil_amp, mod_points, valid_pix, recon, gx, gy, act_map):
    rows, gt = sensor_tables()
    vmem = pl.BlockSpec(memory_space=pltpu.VMEM)
    hbm = pl.BlockSpec(memory_space=pltpu.HBM)
    command, frame = pl.pallas_call(
        kernel,
        out_shape=(pltpu.VMEM((40, 128), F32), pltpu.VMEM((8, NF), F32)),
        in_specs=[pl.BlockSpec(memory_space=pltpu.SMEM)] + [hbm] * 9,
        out_specs=(vmem, vmem),
        scratch_shapes=[
            pltpu.VMEM((PUPIL, PUPIL), F32),
            pltpu.VMEM((PUPIL, PUPIL), F32),
            pltpu.VMEM((8, 128), jnp.int32),
            pltpu.VMEM((40, 128), jnp.int32),
            pltpu.VMEM((AY, PUPIL), F32),
            pltpu.VMEM((AX, PUPIL), F32),
            pltpu.VMEM((PUPIL, NF), BF16),
            pltpu.VMEM((PUPIL, 3 * AY), BF16),
            pltpu.VMEM((384, PUPIL), BF16),
            pltpu.VMEM((1280, 1024), BF16),
            pltpu.VMEM((2, 5, 1024, 256), BF16),
            pltpu.VMEM((2, 8, PUPIL), F32),
            pltpu.VMEM((8, 1, 128), F32),
            pltpu.VMEM((8, 8, 128), F32),
            pltpu.VMEM((2, 64, PUPIL), F32),
            pltpu.VMEM((512, 512), BF16),
            pltpu.VMEM((512, 512), BF16),
            pltpu.VMEM((512, 512), BF16),
            pltpu.VMEM((512, 512), F32),
            pltpu.VMEM((1024, PUPIL), BF16),
            pltpu.VMEM((1024, NF), F32),
            pltpu.VMEM((128, 1024), BF16),
            pltpu.VMEM((128, 5120), BF16),
            pltpu.VMEM((8, NF), F32),
            pltpu.VMEM((8, NF), F32),
            pltpu.VMEM((STEPS, 2, 1, 1024), F32),
            pltpu.VMEM((STEPS, 2, 2, 2, 640), BF16),
            pltpu.VMEM((STEPS, 16, 2, 2, 640), BF16),
            pltpu.VMEM((STEPS, 8, 640), F32),
            pltpu.VMEM((STEPS, NZ, 8, 640), BF16),
            pltpu.VMEM((40, 128), F32),
            pltpu.VMEM((64, 128), F32),
            pltpu.SemaphoreType.DMA((9,)),
            pltpu.SemaphoreType.DMA((5 + 3 * STEPS,)),
            pltpu.SemaphoreType.DMA((5 + 3 * STEPS,)),
        ],
        compiler_params=pltpu.CompilerParams(
            collective_id=0, has_side_effects=True, vmem_limit_bytes=60 * 1024 * 1024
        ),
    )(
        mod_points, turbulence[0], pupil_amp, valid_pix.reshape(8, 128), act_map.reshape(40, 128), gx.T, gy.T,
        jnp.asarray(gt).astype(BF16), jnp.asarray(rows), recon,
    )
    return command.reshape(1, 5120), frame[None]


def solution(mesh):
    return jax.shard_map(
        body,
        mesh=mesh,
        in_specs=(P("case", None, None), P(), P("mod"), P("mod"), P("case", "mod"), P(), P(), P()),
        out_specs=(P("case", None), P("case", "mod", None)),
        check_vma=False,
    )
```
